512 devices in a mesh: req: 128 (over x, z, core), tp: 4 (over y).
Axes of the slice: x: 4, y: 4, z: 16, core: 2. Of those that a mesh axis runs over, the one named last changes fastest.
Arguments:
- x_pre: bfloat16 [65536, 1280], P('req', 'tp'), may hold values from -6 to 6
- x_dec: bfloat16 [512, 1280], P('req', 'tp'), may hold values from -6 to 6
- norm_gain: float32 [1280], replicated, may hold values from 0.1 to 1.9
- w_qkv: bfloat16 [3, 1280, 1280], P(None, None, 'tp'), may hold values from -0.15625 to 0.15625
- w_out: bfloat16 [1280, 1280], P('tp'), may hold values from -0.625 to 0.625
- pre_keys: bfloat16 [49152, 1280], P('req', 'tp'), may hold values from -70 to 70
- pre_values: bfloat16 [49152, 1280], P('req', 'tp'), may hold values from -6 to 6
- pre_lens: int32 [128], P('req'), may hold values from 0 to 384, as said below
- dec_keys: bfloat16 [81920, 1280], P('req', 'tp'), may hold values from -70 to 70
- dec_values: bfloat16 [81920, 1280], P('req', 'tp'), may hold values from -6 to 6
- dec_lens: int32 [512], replicated, may hold values from 1 to 41600, as said below
Outputs:
- pre_out: bfloat16 [65536, 1280], P('req', 'tp')
- dec_out: bfloat16 [512, 1280], P('req', 'tp')
The draws below stay inside these ranges and needn't reach their ends.
Inputs may be any that keep to these rules, and one draw needn't show every extreme that they name: `pre_lens`: at least one prefill block has all 384 cached rows valid. `dec_lens`: the lengths sum to 61440; request 0 has exactly 41600 rows, every other request fewer.
All inputs are finite; a program needn't handle non-finite values.
Results may differ from the reference program's by a relative error of at most 0.012.
The reference program's roundings to bfloat16 on the way count: a program that leaves them out, or rounds other values in their place, can miss the bound.
Values may be sent and summed in bfloat16 or wider, within the bound.
No kernel may reach another device: no remote copies, remote signals or barrier semaphores. Data moves between devices by JAX's collectives and lax.ppermute only.
A program may use at most 64 MiB of HBM per device.

```python
import math
import jax
import jax.numpy as jnp
from jax import lax

D = 1280
H = 16
HD = 80
PRE_DEV = 512
PREF = 384
PRE = 65536
PREFIX = 49152
DEC = 512
POOL = 81920
MAXLEN = 41600
FILLED = 61440
N_REQ = 128


def spiky_keys(key, rows):
    base = jnp.clip(jax.random.normal(key, (rows, D), jnp.float32), -6.0, 6.0)
    return base.astype(jnp.bfloat16)


def draw_pre_keys(key, part):
    return spiky_keys(jax.random.fold_in(key, 3), PREFIX)


def draw_dec_keys(key, part):
    return spiky_keys(jax.random.fold_in(key, 5), POOL)


def draw_pre_lens(key, part):
    count = PREFIX // PREF
    first_key = jax.random.fold_in(key, 7)
    second_key = jax.random.fold_in(key, 9)
    lengths = jax.random.randint(first_key, (count,), 0, PREF + 1)
    full_place = jax.random.randint(second_key, (), 0, count)
    return jnp.where(jnp.arange(count) == full_place, PREF, lengths).astype(jnp.int32)


def draw_dec_lens(key, part):
    others = DEC - 1
    extra = FILLED - MAXLEN - others
    cut_key = jax.random.fold_in(key, 13)
    cuts = jnp.sort(jax.random.randint(cut_key, (others - 1,), 0, extra + 1))
    edges = jnp.concatenate([jnp.zeros((1,), jnp.int32), cuts.astype(jnp.int32), jnp.full((1,), extra, jnp.int32)])
    rest = (edges[1:] - edges[:-1] + 1).astype(jnp.int32)
    return jnp.concatenate([jnp.full((1,), MAXLEN, jnp.int32), rest]).astype(jnp.int32)


def shard_levels(own_key, dims, pieces, smallest, largest):
    loudness, own = 1.0, jax.random.fold_in(own_key, 6)
    for axis_at, parts in pieces:
        steps = jnp.exp(jax.random.uniform(jax.random.fold_in(own, axis_at), (parts,), jnp.float32, smallest / len(pieces), largest / len(pieces)))
        loudness = loudness * jnp.repeat(steps, dims[axis_at] // parts).reshape([-1 if axis == axis_at else 1 for axis in range(len(dims))])
    return loudness


def gaussian(key, extent, deviation, most, split=(), held_as=jnp.bfloat16):
    drawn = jax.random.normal(key, extent, jnp.float32) * deviation
    if len(split) > 0:
        drawn = shard_levels(key, extent, split, -0.22, 0.18) * drawn
    return jnp.clip(drawn, min=-most, max=most).astype(held_as)


def setup_inputs(seed: int = 0) -> dict:
    keys = jax.random.split(jax.random.key(seed), 12)
    return {
        "x_pre": gaussian(keys[0], (PRE, D), 1.0, 6.0, ((0, 128), (1, 4))),
        "x_dec": gaussian(keys[1], (DEC, D), 1.0, 6.0, ((0, 128), (1, 4))),
        "norm_gain": jnp.clip(1.0 + 0.18 * jax.random.normal(keys[2], (D,), jnp.float32), 0.1, 1.9),
        "w_qkv": gaussian(keys[3], (3, D, D), D ** -0.5, 0.15625, ((2, 4),)),
        "w_out": gaussian(keys[4], (D, D), HD ** -0.5, 0.625, ((0, 4),)),
        "pre_keys": draw_pre_keys(jax.random.fold_in(keys[11], 71), 0),
        "pre_values": gaussian(keys[6], (PREFIX, D), 1.0, 6.0, ((0, 128), (1, 4))),
        "pre_lens": draw_pre_lens(jax.random.fold_in(keys[11], 71), 0),
        "dec_keys": draw_dec_keys(jax.random.fold_in(keys[11], 71), 0),
        "dec_values": gaussian(keys[9], (POOL, D), 1.0, 6.0, ((0, 128), (1, 4))),
        "dec_lens": draw_dec_lens(jax.random.fold_in(keys[11], 71), 0),
    }


EPSILON = 1e-06
MASKED_SCORE = -1e+30

def normalize(tokens, norm_gain):
    tokens_f = tokens.astype(jnp.float32)
    mean_square = lax.optimization_barrier(jnp.mean(tokens_f * tokens_f, axis=-1, keepdims=True))
    return (tokens_f * lax.rsqrt(mean_square + EPSILON) * norm_gain.astype(jnp.float32)).astype(jnp.bfloat16)

def project(hidden, w_qkv):
    return tuple((jnp.dot(hidden, w_qkv[matrix_index], preferred_element_type=jnp.float32).astype(jnp.bfloat16) for matrix_index in range(3)))

def rounded(weights):
    held = lax.optimization_barrier(weights.astype(jnp.bfloat16))
    return held.astype(jnp.float32)

def prefill_block(block_items):
    queries, keys_new, values_new, cache_keys, cache_values, prefix = block_items
    score_scale = 1.0 / math.sqrt(HD)
    keys_all = jnp.concatenate([cache_keys, keys_new], axis=0).astype(jnp.float32).reshape(-1, H, HD)
    values_all = jnp.concatenate([cache_values, values_new], axis=0).astype(jnp.float32).reshape(-1, H, HD)
    query_f = queries.astype(jnp.float32).reshape(-1, H, HD)
    scores = jnp.einsum('phd,rhd->hpr', query_f, keys_all) * score_scale
    column = jnp.arange(keys_all.shape[0], dtype=jnp.int32)[None, :]
    position = jnp.arange(query_f.shape[0], dtype=jnp.int32)[:, None]
    cached = cache_keys.shape[0]
    allowed = jnp.where(column < cached, column < prefix, column - cached <= position)
    scores = jnp.where(allowed[None], scores, MASKED_SCORE)
    row_top = lax.optimization_barrier(jnp.max(scores, axis=-1, keepdims=True))
    weights = jnp.where(allowed[None], jnp.exp(scores - row_top), 0.0)
    totals = lax.optimization_barrier(jnp.sum(weights, axis=-1))
    mixed = jnp.einsum('hpr,rhd->hpd', rounded(weights), values_all) / totals[..., None]
    return jnp.transpose(mixed, (1, 0, 2)).reshape(query_f.shape[0], D).astype(jnp.bfloat16)

def reference(x_pre, x_dec, norm_gain, w_qkv, w_out, pre_keys, pre_values, pre_lens, dec_keys, dec_values, dec_lens):
    score_scale = 1.0 / math.sqrt(HD)
    query_pre, key_pre, value_pre = project(normalize(x_pre, norm_gain), w_qkv)
    attn_pre = lax.map(prefill_block, (query_pre.reshape(N_REQ, PRE_DEV, D), key_pre.reshape(N_REQ, PRE_DEV, D), value_pre.reshape(N_REQ, PRE_DEV, D), pre_keys.reshape(N_REQ, PREF, D), pre_values.reshape(N_REQ, PREF, D), pre_lens))
    attn_pre = attn_pre.reshape(PRE, D)
    query_dec, key_dec, value_dec = project(normalize(x_dec, norm_gain), w_qkv)
    starts = (jnp.cumsum(dec_lens) - dec_lens).astype(jnp.int32)
    padding = jnp.zeros((MAXLEN, D), jnp.bfloat16)
    keys_pad = jnp.concatenate([dec_keys, padding], axis=0)
    values_pad = jnp.concatenate([dec_values, padding], axis=0)

    def decode_one(request_items):
        query, key_self, value_self, row_start, length = request_items
        cache_k = lax.dynamic_slice_in_dim(keys_pad, row_start.astype(jnp.int32), MAXLEN, 0).astype(jnp.float32).reshape(MAXLEN, H, HD)
        cache_v = lax.dynamic_slice_in_dim(values_pad, row_start.astype(jnp.int32), MAXLEN, 0).astype(jnp.float32).reshape(MAXLEN, H, HD)
        query_f = query.astype(jnp.float32).reshape(H, HD)
        scores = jnp.einsum('hd,rhd->hr', query_f, cache_k) * score_scale
        self_score = lax.optimization_barrier(jnp.sum(query_f * key_self.astype(jnp.float32).reshape(H, HD), axis=-1)) * score_scale
        allowed = jnp.arange(MAXLEN, dtype=jnp.int32) < length
        scores = jnp.where(allowed[None], scores, MASKED_SCORE)
        row_top = jnp.maximum(lax.optimization_barrier(jnp.max(scores, axis=-1)), self_score)
        weights = jnp.where(allowed[None], jnp.exp(scores - row_top[:, None]), 0.0)
        self_weight = jnp.exp(self_score - row_top)
        numerator = jnp.einsum('hr,rhd->hd', rounded(weights), cache_v) + rounded(self_weight)[:, None] * value_self.astype(jnp.float32).reshape(H, HD)
        denominator = lax.optimization_barrier(jnp.sum(weights, axis=-1)) + self_weight
        return (numerator / denominator[:, None]).reshape(D).astype(jnp.bfloat16)
    attn_dec = lax.map(decode_one, (query_dec, key_dec, value_dec, starts, dec_lens))
    pre_out = jnp.dot(attn_pre, w_out, preferred_element_type=jnp.float32).astype(jnp.bfloat16)
    dec_out = jnp.dot(attn_dec, w_out, preferred_element_type=jnp.float32).astype(jnp.bfloat16)
    return (pre_out, dec_out)
```

```python
import math

import jax
import jax.numpy as jnp
from jax import lax
from jax.experimental import pallas as pl
from jax.experimental.pallas import tpu as pltpu
from jax.sharding import Mesh
from jax.sharding import PartitionSpec as P

HD = 80
HEADS = 4
WIDTH = HEADS * HD
LANES = 384
EPSILON = 1e-06
MASKED = -1e30
NX, NZ, NC, NT = 4, 16, 2, 4
LOG2E_SCALE = math.log2(math.e) / math.sqrt(HD)
F32, BF16 = jnp.float32, jnp.bfloat16
VMEM_LIMIT = 40 * 1024 * 1024


def dot(a, b, dims):
    return lax.dot_general(a, b, (dims, ((), ())), preferred_element_type=F32)


def by_head(columns, rows):
    lane = lax.broadcasted_iota(jnp.int32, (rows, WIDTH), 1)
    out = jnp.broadcast_to(columns[HEADS - 1], (rows, WIDTH))
    for h in range(HEADS - 2, -1, -1):
        out = jnp.where(lane < (h + 1) * HD, columns[h], out)
    return out


def normed_rows(x, gain):
    mean_square = jnp.sum(x * x, axis=-1, keepdims=True) * (1.0 / x.shape[-1])
    return (x * lax.rsqrt(mean_square + EPSILON) * gain).astype(BF16)


def dec_project_kernel(x_ref, gain_ref, w_ref, qb_ref, qkv_ref, rows):
    rows[...] = jnp.zeros_like(rows)
    for t in range(NT):
        rows[0:4, t * WIDTH : (t + 1) * WIDTH] = x_ref[t].astype(F32)
    hidden = normed_rows(rows[...], gain_ref[...])
    for part in range(3):
        value = dot(hidden, w_ref[part], ((1,), (1,)))[0:4].astype(BF16)
        qkv_ref[part] = value
        if part == 0:
            for z in range(NZ):
                qb_ref[z] = value


def dec_attention_kernel(base_ref, q_ref, k_ref, v_ref, lens_ref, out_ref):
    requests, pool = q_ref.shape[0], k_ref.shape[1]
    place = lax.broadcasted_iota(jnp.int32, (requests, requests), 0)
    x, c, z, i = place >> 7, (place >> 6) & 1, (place >> 2) & 15, place & 3
    request = (x << 7) | (z << 3) | (c << 2) | i
    other = lax.broadcasted_iota(jnp.int32, (requests, requests), 1)
    lens = lens_ref[...].astype(F32)
    begin = jnp.sum(jnp.where(other < request, lens, 0.0), axis=1, keepdims=True)
    end = jnp.sum(jnp.where(other <= request, lens, 0.0), axis=1, keepdims=True)
    base = base_ref[0].astype(F32)
    row = lax.broadcasted_iota(jnp.int32, (requests, pool), 1).astype(F32) + base
    allowed = (row >= begin) & (row < end)
    lane = lax.broadcasted_iota(jnp.int32, (requests, LANES - WIDTH), 1)
    extra = jnp.zeros((requests, LANES - WIDTH), F32)
    for h in range(HEADS):
        s = dot(q_ref[:, h * HD : (h + 1) * HD], k_ref[h * HD : (h + 1) * HD, :], ((1,), (0,)))
        s = jnp.where(allowed, s, MASKED)
        top = jnp.max(s, axis=1, keepdims=True)
        w = jnp.where(allowed, jnp.exp2((s - top) * LOG2E_SCALE), 0.0)
        total = jnp.sum(w, axis=1, keepdims=True)
        mixed = dot(w.astype(BF16), v_ref[h * HD : (h + 1) * HD, :], ((1,), (1,)))
        out_ref[:, h * HD : (h + 1) * HD] = mixed
        extra = jnp.where(lane == h, top, extra)
        extra = jnp.where(lane == HEADS + h, total, extra)
    out_ref[:, WIDTH:LANES] = extra


def merged(parts, rows):
    tops, totals, values = [], [], jnp.zeros((rows, WIDTH), F32)
    scales = []
    for h in range(HEADS):
        best = parts[0][:, WIDTH + h : WIDTH + h + 1]
        for part in parts[1:]:
            best = jnp.maximum(best, part[:, WIDTH + h : WIDTH + h + 1])
        tops.append(best)
        scale = [jnp.exp2((part[:, WIDTH + h : WIDTH + h + 1] - best) * LOG2E_SCALE) for part in parts]
        scales.append(scale)
        total = jnp.zeros_like(best)
        for part, factor in zip(parts, scale):
            total = total + factor * part[:, WIDTH + HEADS + h : WIDTH + HEADS + h + 1]
        totals.append(total)
    for n, part in enumerate(parts):
        values = values + by_head([scales[h][n] for h in range(HEADS)], rows) * part[:, :WIDTH]
    return values, tops, totals


def dec_merge_kernel(in_ref, out_ref):
    count, rows = in_ref.shape[0], in_ref.shape[1]
    values, tops, totals = merged([in_ref[n] for n in range(count)], rows)
    lane = lax.broadcasted_iota(jnp.int32, (rows, LANES - WIDTH), 1)
    extra = jnp.zeros((rows, LANES - WIDTH), F32)
    for h in range(HEADS):
        extra = jnp.where(lane == h, tops[h], extra)
        extra = jnp.where(lane == HEADS + h, totals[h], extra)
    for z in range(NZ):
        out_ref[z, :, 0:WIDTH] = values[4 * z : 4 * z + 4]
        out_ref[z, :, WIDTH:LANES] = extra[4 * z : 4 * z + 4]


def dec_finish_kernel(in_ref, qkv_ref, w_ref, out_ref):
    rows = 4
    values, tops, totals = merged([in_ref[n] for n in range(NZ)], rows)
    query, key = qkv_ref[0].astype(F32), qkv_ref[1].astype(F32)
    value = qkv_ref[2].astype(F32)
    product = query * key
    lane = lax.broadcasted_iota(jnp.int32, (rows, WIDTH), 1)
    old, own, below = [], [], []
    for h in range(HEADS):
        inside = (lane >= h * HD) & (lane < (h + 1) * HD)
        score = jnp.sum(jnp.where(inside, product, 0.0), axis=1, keepdims=True)
        best = jnp.maximum(tops[h], score)
        factor = jnp.exp2((tops[h] - best) * LOG2E_SCALE)
        self_weight = jnp.exp2((score - best) * LOG2E_SCALE)
        old.append(factor)
        own.append(self_weight.astype(BF16).astype(F32))
        below.append(factor * totals[h] + self_weight)
    numerator = by_head(old, rows) * values + by_head(own, rows) * value
    attn = (numerator / by_head(below, rows)).astype(BF16)
    terms = dot(attn, w_ref[...], ((1,), (0,)))
    for t in range(NT):
        out_ref[t] = terms[:, t * WIDTH : (t + 1) * WIDTH]


def prefill_kernel(len_ref, x_ref, gain_ref, w_ref, kc_ref, vc_ref, wo_ref, out_ref, q_s, k_s, v_s, a_s):
    tokens, cached = x_ref.shape[1], kc_ref.shape[1]
    block = 256
    for b in range(tokens // block):
        cols = slice(b * block, (b + 1) * block)
        x = x_ref[:, cols].astype(F32)
        mean_square = jnp.sum(x * x, axis=0, keepdims=True) * (1.0 / x.shape[0])
        hidden = (x * lax.rsqrt(mean_square + EPSILON) * gain_ref[...]).astype(BF16)
        for part, held in enumerate((q_s, k_s, v_s)):
            held[:, cols] = dot(w_ref[part], hidden, ((1,), (0,))).astype(BF16)
    length = len_ref[0]
    for b in range(tokens // block):
        cols = slice(b * block, (b + 1) * block)
        seen = (b + 1) * block
        in_cache = lax.broadcasted_iota(jnp.int32, (cached, block), 0) < length
        causal = lax.broadcasted_iota(jnp.int32, (seen, block), 0) <= (
            lax.broadcasted_iota(jnp.int32, (seen, block), 1) + b * block
        )
        for h in range(HEADS):
            feats = slice(h * HD, (h + 1) * HD)
            query = q_s[feats, cols]
            s_old = jnp.where(in_cache, dot(kc_ref[feats, :], query, ((0,), (0,))), MASKED)
            s_new = jnp.where(causal, dot(k_s[feats, 0:seen], query, ((0,), (0,))), MASKED)
            top = jnp.maximum(
                jnp.max(s_old, axis=0, keepdims=True), jnp.max(s_new, axis=0, keepdims=True)
            )
            w_old = jnp.exp2((s_old - top) * LOG2E_SCALE)
            w_new = jnp.exp2((s_new - top) * LOG2E_SCALE)
            total = jnp.sum(w_old, axis=0, keepdims=True) + jnp.sum(w_new, axis=0, keepdims=True)
            mixed = dot(vc_ref[feats, :], w_old.astype(BF16), ((1,), (0,))) + dot(
                v_s[feats, 0:seen], w_new.astype(BF16), ((1,), (0,))
            )
            a_s[feats, cols] = (mixed / total).astype(BF16)
    for n in range(wo_ref.shape[1] // block):
        cols = slice(n * block, (n + 1) * block)
        out_ref[cols, :] = dot(wo_ref[:, cols], a_s[...], ((0,), (0,)))


def call(kernel, out_shape, scalars, arrays, scratch=(), flops=0, moved=0):
    return pl.pallas_call(
        kernel,
        out_shape=out_shape,
        in_specs=[pl.BlockSpec(memory_space=pltpu.SMEM)] * len(scalars)
        + [pl.BlockSpec(memory_space=pltpu.VMEM)] * len(arrays),
        out_specs=jax.tree.map(lambda _: pl.BlockSpec(memory_space=pltpu.VMEM), out_shape),
        scratch_shapes=scratch,
        compiler_params=pltpu.CompilerParams(vmem_limit_bytes=VMEM_LIMIT),
        cost_estimate=pl.CostEstimate(flops=flops, bytes_accessed=moved, transcendentals=0),
    )(*scalars, *arrays)


def shape(dims, dtype):
    return jax.ShapeDtypeStruct(dims, dtype)


def spread(block, axes, count):
    copies = jnp.broadcast_to(block[None], (count,) + block.shape)
    return lax.all_to_all(copies, axes, 0, 0, tiled=True)


def body(x_pre, x_dec, norm_gain, w_qkv, w_out, pre_keys, pre_values, pre_lens, dec_keys, dec_values, dec_lens):
    tokens, pool = x_pre.shape[0], dec_keys.shape[0]
    full = NT * WIDTH
    w_t = jnp.transpose(w_qkv, (0, 2, 1))
    index = (lax.axis_index("x") * NZ + lax.axis_index("z")) * NC + lax.axis_index("c")
    base = (index * pool).astype(jnp.int32).reshape(1)

    x_all = lax.all_gather(x_pre.T, "tp", axis=0, tiled=True)

    x_rows = spread(x_dec, "tp", NT)
    queries, qkv = call(
        dec_project_kernel,
        (shape((NZ, 4, WIDTH), BF16), shape((3, 4, WIDTH), BF16)),
        (),
        (x_rows, norm_gain.reshape(1, full), w_t),
        scratch=[pltpu.VMEM((8, full), F32)],
        flops=2 * 8 * full * full,
        moved=2 * 3 * full * WIDTH,
    )
    queries = lax.all_to_all(queries, "z", 0, 0, tiled=True)
    queries = spread(queries.reshape(NZ * 4, WIDTH), ("x", "c"), NX * NC)
    queries = queries.reshape(NX * NC * NZ * 4, WIDTH)
    requests = queries.shape[0]
    partial = call(
        dec_attention_kernel,
        shape((requests, LANES), F32),
        (base,),
        (queries, dec_keys.T, dec_values.T, dec_lens.reshape(1, requests)),
        flops=4 * requests * pool * WIDTH,
        moved=4 * pool * WIDTH,
    )
    partial = lax.all_to_all(partial.reshape(NX * NC, NZ * 4, LANES), ("x", "c"), 0, 0, tiled=True)
    partial = call(
        dec_merge_kernel,
        shape((NZ, 4, LANES), F32),
        (),
        (partial,),
        flops=NX * NC * NZ * 4 * LANES,
        moved=NX * NC * NZ * 16 * LANES,
    )
    partial = lax.all_to_all(partial, "z", 0, 0, tiled=True)
    terms = call(
        dec_finish_kernel,
        shape((NT, 4, WIDTH), F32),
        (),
        (partial, qkv, w_out),
        flops=2 * 8 * full * WIDTH,
        moved=2 * full * WIDTH,
    )
    terms = lax.all_to_all(terms, "tp", 0, 0, tiled=True)
    dec_out = jnp.sum(terms, axis=0).astype(BF16)

    terms_pre = call(
        prefill_kernel,
        shape((full, tokens), F32),
        (pre_lens,),
        (x_all, norm_gain.reshape(full, 1), w_t, pre_keys.T, pre_values.T, w_out),
        scratch=[pltpu.VMEM((WIDTH, tokens), BF16)] * 4,
        flops=8 * tokens * full * WIDTH + 4 * tokens * 896 * WIDTH,
        moved=8 * full * WIDTH,
    )
    pre_out = lax.psum_scatter(terms_pre, "tp", scatter_dimension=0, tiled=True)
    return pre_out.astype(BF16).T, dec_out


def solution(mesh):
    req = ("x", "z", "c")
    grid = Mesh(mesh.devices.reshape(NX, NZ, NC, NT), req + ("tp",))
    return jax.shard_map(
        body,
        mesh=grid,
        in_specs=(
            P(req, "tp"),
            P(req, "tp"),
            P(),
            P(None, None, "tp"),
            P("tp", None),
            P(req, "tp"),
            P(req, "tp"),
            P(req),
            P(req, "tp"),
            P(req, "tp"),
            P(),
        ),
        out_specs=(P(req, "tp"), P(req, "tp")),
        check_vma=False,
    )
```

```python
import math

import jax
import jax.numpy as jnp
from jax import lax
from jax.experimental import pallas as pl
from jax.experimental.pallas import tpu as pltpu
from jax.sharding import Mesh
from jax.sharding import PartitionSpec as P

HD = 80
HEADS = 4
WIDTH = HEADS * HD
LANES = 384
EPSILON = 1e-06
MASKED = -1e30
NX, NZ, NC, NT = 4, 16, 2, 4
LOG2E_SCALE = math.log2(math.e) / math.sqrt(HD)
F32, BF16 = jnp.float32, jnp.bfloat16
VMEM_LIMIT = 24 * 1024 * 1024
VMEM_ALL = 58 * 1024 * 1024


def dot(a, b, dims):
    return lax.dot_general(a, b, (dims, ((), ())), preferred_element_type=F32)


def by_head(columns, rows):
    lane = lax.broadcasted_iota(jnp.int32, (rows, WIDTH), 1)
    out = jnp.broadcast_to(columns[HEADS - 1], (rows, WIDTH))
    for h in range(HEADS - 2, -1, -1):
        out = jnp.where(lane < (h + 1) * HD, columns[h], out)
    return out


def normed_rows(x, gain):
    mean_square = jnp.sum(x * x, axis=-1, keepdims=True) * (1.0 / x.shape[-1])
    return (x * lax.rsqrt(mean_square + EPSILON) * gain).astype(BF16)


def dec_project_kernel(x_ref, gain_ref, w_hbm, qb_ref, hidden_ref, rows, w_ref, sem):
    fetch = pltpu.make_async_copy(w_hbm.at[0], w_ref, sem)
    fetch.start()
    rows[...] = jnp.zeros_like(rows)
    for t in range(NT):
        rows[0:4, t * WIDTH : (t + 1) * WIDTH] = x_ref[t].astype(F32)
    hidden = normed_rows(rows[...], gain_ref[...])
    hidden_ref[...] = hidden
    fetch.wait()
    value = dot(hidden, w_ref[...], ((1,), (1,)))[0:4].astype(BF16)
    for z in range(NZ):
        qb_ref[z] = value


def dec_attention_kernel(base_ref, q_ref, lens_ref, k_hbm, v_hbm, out_ref, k_ref, v_ref, sems):
    fetch_k = pltpu.make_async_copy(k_hbm, k_ref, sems.at[0])
    fetch_v = pltpu.make_async_copy(v_hbm, v_ref, sems.at[1])
    fetch_k.start()
    fetch_v.start()
    requests, pool = q_ref.shape[0], k_ref.shape[1]
    place = lax.broadcasted_iota(jnp.int32, (requests, requests), 0)
    x, c, z, i = place >> 7, (place >> 6) & 1, (place >> 2) & 15, place & 3
    request = (x << 7) | (z << 3) | (c << 2) | i
    other = lax.broadcasted_iota(jnp.int32, (requests, requests), 1)
    lens = lens_ref[...].astype(F32)
    begin = jnp.sum(jnp.where(other < request, lens, 0.0), axis=1, keepdims=True)
    end = jnp.sum(jnp.where(other <= request, lens, 0.0), axis=1, keepdims=True)
    base = base_ref[0].astype(F32)
    row = lax.broadcasted_iota(jnp.int32, (requests, pool), 1).astype(F32) + base
    allowed = (row >= begin) & (row < end)
    tops, totals = [], []
    fetch_k.wait()
    fetch_v.wait()
    for h in range(HEADS):
        s = dot(q_ref[:, h * HD : (h + 1) * HD], k_ref[h * HD : (h + 1) * HD, :], ((1,), (0,)))
        s = jnp.where(allowed, s, MASKED)
        top = jnp.max(s, axis=1, keepdims=True)
        w = jnp.where(allowed, jnp.exp2((s - top) * LOG2E_SCALE), 0.0)
        total = jnp.sum(w, axis=1, keepdims=True)
        mixed = dot(w.astype(BF16), v_ref[h * HD : (h + 1) * HD, :], ((1,), (1,)))
        out_ref[:, h * HD : (h + 1) * HD] = mixed.astype(BF16)
        tops.append(top)
        totals.append(total)
    out_ref[:, WIDTH:LANES] = stats(tops, totals, requests)


def thirds(value):
    high = value.astype(BF16)
    rest = value - high.astype(F32)
    middle = rest.astype(BF16)
    return high, middle, (rest - middle.astype(F32)).astype(BF16)


def stats(tops, totals, rows):
    lane = lax.broadcasted_iota(jnp.int32, (rows, LANES - WIDTH), 1)
    out = jnp.zeros((rows, LANES - WIDTH), F32)
    for n, value in enumerate(tops + totals):
        for k, part in enumerate(thirds(value)):
            out = jnp.where(lane == 3 * n + k, part.astype(F32), out)
    return out.astype(BF16)


def stat(block, n):
    at = WIDTH + 3 * n
    return block[:, at : at + 1] + block[:, at + 1 : at + 2] + block[:, at + 2 : at + 3]


def merged(parts, rows):
    parts = [part.astype(F32) for part in parts]
    tops, totals, values = [], [], jnp.zeros((rows, WIDTH), F32)
    scales = []
    for h in range(HEADS):
        part_tops = [stat(part, h) for part in parts]
        best = part_tops[0]
        for top in part_tops[1:]:
            best = jnp.maximum(best, top)
        tops.append(best)
        scale = [jnp.exp2((top - best) * LOG2E_SCALE) for top in part_tops]
        scales.append(scale)
        total = jnp.zeros_like(best)
        for part, factor in zip(parts, scale):
            total = total + factor * stat(part, HEADS + h)
        totals.append(total)
    for n, part in enumerate(parts):
        values = values + by_head([scales[h][n] for h in range(HEADS)], rows) * part[:, :WIDTH]
    return values, tops, totals


def dec_merge_kernel(in_ref, out_ref):
    count, rows = in_ref.shape[0], in_ref.shape[1]
    values, tops, totals = merged([in_ref[n] for n in range(count)], rows)
    extra = stats(tops, totals, rows)
    values = values.astype(BF16)
    for z in range(NZ):
        out_ref[z, :, 0:WIDTH] = values[4 * z : 4 * z + 4]
        out_ref[z, :, WIDTH:LANES] = extra[4 * z : 4 * z + 4]


def dec_finish_kernel(in_ref, q_ref, kv_ref, w_ref, out_ref):
    rows = 4
    values, tops, totals = merged([in_ref[n] for n in range(NZ)], rows)
    query, key = q_ref[0].astype(F32), kv_ref[0].astype(F32)
    value = kv_ref[1].astype(F32)
    product = query * key
    lane = lax.broadcasted_iota(jnp.int32, (rows, WIDTH), 1)
    old, own, below = [], [], []
    for h in range(HEADS):
        inside = (lane >= h * HD) & (lane < (h + 1) * HD)
        score = jnp.sum(jnp.where(inside, product, 0.0), axis=1, keepdims=True)
        best = jnp.maximum(tops[h], score)
        factor = jnp.exp2((tops[h] - best) * LOG2E_SCALE)
        self_weight = jnp.exp2((score - best) * LOG2E_SCALE)
        old.append(factor)
        own.append(self_weight.astype(BF16).astype(F32))
        below.append(factor * totals[h] + self_weight)
    numerator = by_head(old, rows) * values + by_head(own, rows) * value
    attn = (numerator / by_head(below, rows)).astype(BF16)
    terms = dot(attn, w_ref[...], ((1,), (0,)))
    for t in range(NT):
        out_ref[t] = terms[:, t * WIDTH : (t + 1) * WIDTH]


def prefill_kernel(
    len_ref, gain_ref, hd_ref, x_hbm, w_hbm, kc_hbm, vc_hbm, wo_hbm,
    first_ref, second_ref, kv_ref,
    x_ref, w_ref, kc_ref, vc_ref, wo_ref, q_s, k_s, v_s, a_s, sems,
):
    tokens, cached = x_ref.shape[1], kc_ref.shape[1]
    block = 256
    fetches = [
        pltpu.make_async_copy(source, target, sems.at[n])
        for n, (source, target) in enumerate(
            [(x_hbm.at[:, 0:block], x_ref.at[:, 0:block]), (w_hbm, w_ref)]
            + [(x_hbm.at[:, block:tokens], x_ref.at[:, block:tokens])]
            + [(kc_hbm, kc_ref), (vc_hbm, vc_ref), (wo_hbm, wo_ref)]
        )
    ]
    for fetch in fetches:
        fetch.start()
    for b in range(tokens // block):
        cols = slice(b * block, (b + 1) * block)
        fetches[0 if b == 0 else 2].wait()
        x = x_ref[:, cols].astype(F32)
        mean_square = jnp.sum(x * x, axis=0, keepdims=True) * (1.0 / x.shape[0])
        hidden = (x * lax.rsqrt(mean_square + EPSILON) * gain_ref[...]).astype(BF16)
        if b == 0:
            fetches[1].wait()
            for part in (1, 2):
                kv_ref[part - 1] = dot(hd_ref[...], w_ref[part], ((1,), (1,)))[0:4].astype(BF16)
        for part, held in enumerate((q_s, k_s, v_s)):
            held[:, cols] = dot(w_ref[part], hidden, ((1,), (0,))).astype(BF16)
    fetches[3].wait()
    fetches[4].wait()
    length = len_ref[0]
    for b in range(tokens // block):
        cols = slice(b * block, (b + 1) * block)
        seen = (b + 1) * block
        in_cache = lax.broadcasted_iota(jnp.int32, (cached, block), 0) < length
        causal = lax.broadcasted_iota(jnp.int32, (seen, block), 0) <= (
            lax.broadcasted_iota(jnp.int32, (seen, block), 1) + b * block
        )
        for h in range(HEADS):
            feats = slice(h * HD, (h + 1) * HD)
            query = q_s[feats, cols]
            s_old = jnp.where(in_cache, dot(kc_ref[feats, :], query, ((0,), (0,))), MASKED)
            s_new = jnp.where(causal, dot(k_s[feats, 0:seen], query, ((0,), (0,))), MASKED)
            top = jnp.maximum(
                jnp.max(s_old, axis=0, keepdims=True), jnp.max(s_new, axis=0, keepdims=True)
            )
            w_old = jnp.exp2((s_old - top) * LOG2E_SCALE)
            w_new = jnp.exp2((s_new - top) * LOG2E_SCALE)
            total = jnp.sum(w_old, axis=0, keepdims=True) + jnp.sum(w_new, axis=0, keepdims=True)
            mixed = dot(vc_ref[feats, :], w_old.astype(BF16), ((1,), (0,))) + dot(
                v_s[feats, 0:seen], w_new.astype(BF16), ((1,), (0,))
            )
            a_s[feats, cols] = (mixed / total).astype(BF16)
        if b == 0:
            fetches[5].wait()
        out_ref = first_ref if b == 0 else second_ref
        for n in range(wo_ref.shape[1] // block):
            outs = slice(n * block, (n + 1) * block)
            out_ref[outs, :] = dot(wo_ref[:, outs], a_s[:, cols], ((0,), (0,)))


def call(
    kernel, out_shape, scalars, arrays, stored=(), scratch=(), flops=0, moved=0, limit=VMEM_LIMIT
):
    return pl.pallas_call(
        kernel,
        out_shape=out_shape,
        in_specs=[pl.BlockSpec(memory_space=pltpu.SMEM)] * len(scalars)
        + [pl.BlockSpec(memory_space=pltpu.VMEM)] * len(arrays)
        + [pl.BlockSpec(memory_space=pltpu.HBM)] * len(stored),
        out_specs=jax.tree.map(lambda _: pl.BlockSpec(memory_space=pltpu.VMEM), out_shape),
        scratch_shapes=scratch,
        compiler_params=pltpu.CompilerParams(vmem_limit_bytes=limit),
        cost_estimate=pl.CostEstimate(flops=flops, bytes_accessed=moved, transcendentals=0),
    )(*scalars, *arrays, *stored)


def shape(dims, dtype):
    return jax.ShapeDtypeStruct(dims, dtype)


def spread(block, axes, count):
    copies = jnp.broadcast_to(block[None], (count,) + block.shape)
    return lax.all_to_all(copies, axes, 0, 0, tiled=True)


def body(x_pre, x_dec, norm_gain, w_qkv, w_out, pre_keys, pre_values, pre_lens, dec_keys, dec_values, dec_lens):
    tokens, pool = x_pre.shape[0], dec_keys.shape[0]
    full = NT * WIDTH
    w_t = jnp.transpose(w_qkv, (0, 2, 1))
    index = (lax.axis_index("x") * NZ + lax.axis_index("z")) * NC + lax.axis_index("c")
    base = (index * pool).astype(jnp.int32).reshape(1)

    x_rows = spread(x_dec, "tp", NT)
    x_all = lax.all_gather(x_pre.T, "tp", axis=0, tiled=True)
    queries, hidden = call(
        dec_project_kernel,
        (shape((NZ, 4, WIDTH), BF16), shape((8, full), BF16)),
        (),
        (x_rows, norm_gain.reshape(1, full)),
        (w_t,),
        scratch=[
            pltpu.VMEM((8, full), F32),
            pltpu.VMEM((WIDTH, full), BF16),
            pltpu.SemaphoreType.DMA,
        ],
        flops=2 * 8 * full * WIDTH,
        moved=2 * full * WIDTH,
        limit=VMEM_ALL,
    )
    own_queries = queries
    queries = lax.all_to_all(queries, "z", 0, 0, tiled=True)
    x_all, queries = lax.optimization_barrier((x_all, queries))
    half = tokens // 2
    first, second, own_kv = call(
        prefill_kernel,
        (shape((full, half), F32), shape((full, half), F32), shape((2, 4, WIDTH), BF16)),
        (pre_lens,),
        (norm_gain.reshape(full, 1), hidden),
        (x_all, w_t, pre_keys.T, pre_values.T, w_out),
        scratch=[
            pltpu.VMEM((full, tokens), BF16),
            pltpu.VMEM((3, WIDTH, full), BF16),
            pltpu.VMEM((WIDTH, pre_keys.shape[0]), BF16),
            pltpu.VMEM((WIDTH, pre_keys.shape[0]), BF16),
            pltpu.VMEM((WIDTH, full), BF16),
        ]
        + [pltpu.VMEM((WIDTH, tokens), BF16)] * 4
        + [pltpu.SemaphoreType.DMA((6,))],
        flops=8 * tokens * full * WIDTH + 4 * tokens * 896 * WIDTH,
        moved=8 * full * WIDTH,
        limit=VMEM_ALL,
    )
    queries = spread(queries.reshape(NZ * 4, WIDTH), ("x", "c"), NX * NC)
    first, second, queries = lax.optimization_barrier((first, second, queries))
    pre_out = jnp.concatenate(
        [lax.psum_scatter(part, "tp", scatter_dimension=0, tiled=True) for part in (first, second)],
        axis=1,
    )
    queries = queries.reshape(NX * NC * NZ * 4, WIDTH)
    requests = queries.shape[0]
    partial = call(
        dec_attention_kernel,
        shape((requests, LANES), BF16),
        (base,),
        (queries, dec_lens.reshape(1, requests)),
        (dec_keys.T, dec_values.T),
        scratch=[
            pltpu.VMEM((WIDTH, pool), BF16),
            pltpu.VMEM((WIDTH, pool), BF16),
            pltpu.SemaphoreType.DMA((2,)),
        ],
        flops=4 * requests * pool * WIDTH,
        moved=4 * pool * WIDTH,
    )
    partial = lax.all_to_all(partial.reshape(NX * NC, NZ * 4, LANES), ("x", "c"), 0, 0, tiled=True)
    partial = call(
        dec_merge_kernel,
        shape((NZ, 4, LANES), BF16),
        (),
        (partial,),
        flops=NX * NC * NZ * 4 * LANES,
        moved=NX * NC * NZ * 16 * LANES,
    )
    partial = lax.all_to_all(partial, "z", 0, 0, tiled=True)
    terms = call(
        dec_finish_kernel,
        shape((NT, 4, WIDTH), F32),
        (),
        (partial, own_queries, own_kv, w_out),
        flops=2 * 8 * full * WIDTH,
        moved=2 * full * WIDTH,
    )
    terms = lax.all_to_all(terms, "tp", 0, 0, tiled=True)
    dec_out = jnp.sum(terms, axis=0).astype(BF16)
    return pre_out.astype(BF16).T, dec_out


def solution(mesh):
    req = ("x", "z", "c")
    grid = Mesh(mesh.devices.reshape(NX, NZ, NC, NT), req + ("tp",))
    return jax.shard_map(
        body,
        mesh=grid,
        in_specs=(
            P(req, "tp"),
            P(req, "tp"),
            P(),
            P(None, None, "tp"),
            P("tp", None),
            P(req, "tp"),
            P(req, "tp"),
            P(req),
            P(req, "tp"),
            P(req, "tp"),
            P(),
        ),
        out_specs=(P(req, "tp"), P(req, "tp")),
        check_vma=False,
    )
```

```python
import math

import jax
import jax.numpy as jnp
from jax import lax
from jax.experimental import pallas as pl
from jax.experimental.pallas import tpu as pltpu
from jax.sharding import Mesh
from jax.sharding import PartitionSpec as P

HD = 80
HEADS = 4
WIDTH = HEADS * HD
LANES = 384
EPSILON = 1e-06
MASKED = -1e30
NX, NZ, NC, NT = 4, 16, 2, 4
LOG2E_SCALE = math.log2(math.e) / math.sqrt(HD)
F32, BF16 = jnp.float32, jnp.bfloat16
VMEM_LIMIT = 24 * 1024 * 1024
VMEM_ALL = 58 * 1024 * 1024


def dot(a, b, dims):
    return lax.dot_general(a, b, (dims, ((), ())), preferred_element_type=F32)


def by_head(columns, rows):
    lane = lax.broadcasted_iota(jnp.int32, (rows, WIDTH), 1)
    out = jnp.broadcast_to(columns[HEADS - 1], (rows, WIDTH))
    for h in range(HEADS - 2, -1, -1):
        out = jnp.where(lane < (h + 1) * HD, columns[h], out)
    return out


def normed_rows(x, gain):
    mean_square = jnp.sum(x * x, axis=-1, keepdims=True) * (1.0 / x.shape[-1])
    return (x * lax.rsqrt(mean_square + EPSILON) * gain).astype(BF16)


def dec_project_kernel(x_ref, gain_ref, w_hbm, qb_ref, q_ref, hidden_ref, rows, w_ref, sem):
    fetch = pltpu.make_async_copy(w_hbm.at[0], w_ref, sem)
    fetch.start()
    for n in range(NX * NC):
        for t in range(NT):
            rows[4 * n : 4 * n + 4, t * WIDTH : (t + 1) * WIDTH] = x_ref[NT * n + t].astype(F32)
    hidden = normed_rows(rows[...], gain_ref[...])
    hidden_ref[...] = hidden
    fetch.wait()
    value = dot(hidden, w_ref[...], ((1,), (1,)))
    q_ref[...] = value.astype(BF16)
    tail = jnp.concatenate([value[0:16, 256:WIDTH], value[16:32, 256:WIDTH]], axis=1)
    packed = jnp.concatenate([value[:, 0:128], value[:, 128:256], tail], axis=0).astype(BF16)
    for z in range(NZ):
        qb_ref[z] = packed


def dec_attention_kernel(base_ref, qp_ref, lens_ref, k_hbm, v_hbm, out_ref, q_s, k_ref, v_ref, sems):
    fetch_k = pltpu.make_async_copy(k_hbm, k_ref, sems.at[0])
    fetch_v = pltpu.make_async_copy(v_hbm, v_ref, sems.at[1])
    fetch_k.start()
    fetch_v.start()
    for z in range(NZ):
        rows = slice(32 * z, 32 * z + 32)
        q_s[rows, 0:128] = qp_ref[z, 0:32]
        q_s[rows, 128:256] = qp_ref[z, 32:64]
        q_s[32 * z : 32 * z + 16, 256:WIDTH] = qp_ref[z, 64:80, 0:64]
        q_s[32 * z + 16 : 32 * z + 32, 256:WIDTH] = qp_ref[z, 64:80, 64:128]
    requests, pool = q_s.shape[0], k_ref.shape[1]
    place = lax.broadcasted_iota(jnp.int32, (requests, requests), 0)
    x, c, z, i = place >> 7, (place >> 6) & 1, (place >> 2) & 15, place & 3
    request = (x << 7) | (z << 3) | (c << 2) | i
    arrived = (z << 5) | (x << 3) | (c << 2) | i
    other = lax.broadcasted_iota(jnp.int32, (requests, requests), 1)
    lens = lens_ref[...].astype(F32)
    begin = jnp.sum(jnp.where(other < request, lens, 0.0), axis=1, keepdims=True)
    end = jnp.sum(jnp.where(other <= request, lens, 0.0), axis=1, keepdims=True)
    order = jnp.where(other == arrived, 1.0, 0.0).astype(BF16)
    queries = dot(order, q_s[...], ((1,), (0,))).astype(BF16)
    base = base_ref[0].astype(F32)
    row = lax.broadcasted_iota(jnp.int32, (requests, pool), 1).astype(F32) + base
    allowed = (row >= begin) & (row < end)
    tops, totals = [], []
    fetch_k.wait()
    fetch_v.wait()
    for h in range(HEADS):
        s = dot(queries[:, h * HD : (h + 1) * HD], k_ref[h * HD : (h + 1) * HD, :], ((1,), (0,)))
        s = jnp.where(allowed, s, MASKED)
        top = jnp.max(s, axis=1, keepdims=True)
        w = jnp.where(allowed, jnp.exp2((s - top) * LOG2E_SCALE), 0.0)
        total = jnp.sum(w, axis=1, keepdims=True)
        mixed = dot(w.astype(BF16), v_ref[h * HD : (h + 1) * HD, :], ((1,), (1,)))
        out_ref[:, h * HD : (h + 1) * HD] = mixed.astype(BF16)
        tops.append(top)
        totals.append(total)
    out_ref[:, WIDTH:LANES] = stats(tops, totals, requests)


def thirds(value):
    high = value.astype(BF16)
    rest = value - high.astype(F32)
    middle = rest.astype(BF16)
    return high, middle, (rest - middle.astype(F32)).astype(BF16)


def stats(tops, totals, rows):
    lane = lax.broadcasted_iota(jnp.int32, (rows, LANES - WIDTH), 1)
    out = jnp.zeros((rows, LANES - WIDTH), F32)
    for n, value in enumerate(tops + totals):
        for k, part in enumerate(thirds(value)):
            out = jnp.where(lane == 3 * n + k, part.astype(F32), out)
    return out.astype(BF16)


def stat(block, n):
    at = WIDTH + 3 * n
    return block[:, at : at + 1] + block[:, at + 1 : at + 2] + block[:, at + 2 : at + 3]


def merged(parts, rows):
    parts = [part.astype(F32) for part in parts]
    tops, totals, values = [], [], jnp.zeros((rows, WIDTH), F32)
    scales = []
    for h in range(HEADS):
        part_tops = [stat(part, h) for part in parts]
        best = part_tops[0]
        for top in part_tops[1:]:
            best = jnp.maximum(best, top)
        tops.append(best)
        scale = [jnp.exp2((top - best) * LOG2E_SCALE) for top in part_tops]
        scales.append(scale)
        total = jnp.zeros_like(best)
        for part, factor in zip(parts, scale):
            total = total + factor * stat(part, HEADS + h)
        totals.append(total)
    for n, part in enumerate(parts):
        values = values + by_head([scales[h][n] for h in range(HEADS)], rows) * part[:, :WIDTH]
    return values, tops, totals


def dec_merge_kernel(in_ref, out_ref):
    count, rows = in_ref.shape[0], in_ref.shape[1]
    values, tops, totals = merged([in_ref[n] for n in range(count)], rows)
    extra = stats(tops, totals, rows)
    values = values.astype(BF16)
    for z in range(NZ):
        out_ref[z, :, 0:WIDTH] = values[4 * z : 4 * z + 4]
        out_ref[z, :, WIDTH:LANES] = extra[4 * z : 4 * z + 4]


def dec_finish_kernel(own_ref, in_ref, q_ref, kv_ref, w_ref, out_ref):
    rows = 4
    values, tops, totals = merged([in_ref[n] for n in range(NZ)], rows)
    row = lax.broadcasted_iota(jnp.int32, (8, 32), 0) + 4 * own_ref[0]
    mine = jnp.where(row == lax.broadcasted_iota(jnp.int32, (8, 32), 1), 1.0, 0.0).astype(BF16)
    query = dot(mine, q_ref[...], ((1,), (0,)))[0:rows]
    key = dot(mine, kv_ref[0], ((1,), (0,)))[0:rows]
    value = dot(mine, kv_ref[1], ((1,), (0,)))[0:rows]
    product = query * key
    lane = lax.broadcasted_iota(jnp.int32, (rows, WIDTH), 1)
    old, own, below = [], [], []
    for h in range(HEADS):
        inside = (lane >= h * HD) & (lane < (h + 1) * HD)
        score = jnp.sum(jnp.where(inside, product, 0.0), axis=1, keepdims=True)
        best = jnp.maximum(tops[h], score)
        factor = jnp.exp2((tops[h] - best) * LOG2E_SCALE)
        self_weight = jnp.exp2((score - best) * LOG2E_SCALE)
        old.append(factor)
        own.append(self_weight.astype(BF16).astype(F32))
        below.append(factor * totals[h] + self_weight)
    numerator = by_head(old, rows) * values + by_head(own, rows) * value
    attn = (numerator / by_head(below, rows)).astype(BF16)
    terms = dot(attn, w_ref[...], ((1,), (0,)))
    for t in range(NT):
        out_ref[t] = terms[:, t * WIDTH : (t + 1) * WIDTH]


def prefill_kernel(
    len_ref, tp_ref, gain_ref, hd_ref, x0_hbm, x1_hbm, x2_hbm, x3_hbm, w_hbm, kc_hbm, vc_hbm, wo_hbm,
    o0_ref, o1_ref, o2_ref, o3_ref, kv_ref,
    x_ref, w_ref, kc_ref, vc_ref, wo_ref, wo4_s, q_s, k_s, v_s, a_s, sems,
):
    tokens, cached = x_ref.shape[1], kc_ref.shape[1]
    block = 256
    me = tp_ref[0]

    def piece(source, shift, b):
        at = pl.ds(pl.multiple_of(((me - shift + NT) & (NT - 1)) * WIDTH, WIDTH), WIDTH)
        cols = slice(b * block, (b + 1) * block)
        return source.at[:, cols], x_ref.at[at, cols]

    sources = (x0_hbm, x1_hbm, x2_hbm, x3_hbm)
    plan = [piece(source, shift, 0) for shift, source in enumerate(sources)] + [(w_hbm, w_ref)]
    plan += [piece(source, shift, 1) for shift, source in enumerate(sources)]
    plan += [(wo_hbm, wo_ref), (kc_hbm, kc_ref), (vc_hbm, vc_ref)]
    fetches = [
        pltpu.make_async_copy(source, target, sems.at[n]) for n, (source, target) in enumerate(plan)
    ]
    for fetch in fetches:
        fetch.start()
    for b in range(tokens // block):
        cols = slice(b * block, (b + 1) * block)
        for fetch in fetches[5 * b : 5 * b + 4]:
            fetch.wait()
        x = x_ref[:, cols].astype(F32)
        mean_square = jnp.sum(x * x, axis=0, keepdims=True) * (1.0 / x.shape[0])
        hidden = (x * lax.rsqrt(mean_square + EPSILON) * gain_ref[...]).astype(BF16)
        if b == 0:
            fetches[4].wait()
            for part in (1, 2):
                kv_ref[part - 1] = dot(hd_ref[...], w_ref[part], ((1,), (1,))).astype(BF16)
        for part, held in enumerate((q_s, k_s, v_s)):
            held[:, cols] = dot(w_ref[part], hidden, ((1,), (0,))).astype(BF16)
    for fetch in fetches[9:]:
        fetch.wait()
    for t in range(NT):
        wo4_s[t] = wo_ref[:, t * WIDTH : (t + 1) * WIDTH]
    length = len_ref[0]
    for b in range(tokens // block):
        cols = slice(b * block, (b + 1) * block)
        seen = (b + 1) * block
        in_cache = lax.broadcasted_iota(jnp.int32, (cached, block), 0) < length
        causal = lax.broadcasted_iota(jnp.int32, (seen, block), 0) <= (
            lax.broadcasted_iota(jnp.int32, (seen, block), 1) + b * block
        )
        for h in range(HEADS):
            feats = slice(h * HD, (h + 1) * HD)
            query = q_s[feats, cols]
            s_old = jnp.where(in_cache, dot(kc_ref[feats, :], query, ((0,), (0,))), MASKED)
            s_new = jnp.where(causal, dot(k_s[feats, 0:seen], query, ((0,), (0,))), MASKED)
            top = jnp.maximum(
                jnp.max(s_old, axis=0, keepdims=True), jnp.max(s_new, axis=0, keepdims=True)
            )
            w_old = jnp.exp2((s_old - top) * LOG2E_SCALE)
            w_new = jnp.exp2((s_new - top) * LOG2E_SCALE)
            total = jnp.sum(w_old, axis=0, keepdims=True) + jnp.sum(w_new, axis=0, keepdims=True)
            mixed = dot(vc_ref[feats, :], w_old.astype(BF16), ((1,), (0,))) + dot(
                v_s[feats, 0:seen], w_new.astype(BF16), ((1,), (0,))
            )
            a_s[feats, cols] = (mixed / total).astype(BF16)
    for shift, out_ref in enumerate((o0_ref, o1_ref, o2_ref, o3_ref)):
        terms = dot(wo4_s[(me + shift) & (NT - 1)], a_s[...], ((0,), (0,)))
        out_ref[...] = terms.astype(out_ref.dtype)


def call(
    kernel, out_shape, scalars, arrays, stored=(), scratch=(), flops=0, moved=0, limit=VMEM_LIMIT
):
    return pl.pallas_call(
        kernel,
        out_shape=out_shape,
        in_specs=[pl.BlockSpec(memory_space=pltpu.SMEM)] * len(scalars)
        + [pl.BlockSpec(memory_space=pltpu.VMEM)] * len(arrays)
        + [pl.BlockSpec(memory_space=pltpu.HBM)] * len(stored),
        out_specs=jax.tree.map(lambda _: pl.BlockSpec(memory_space=pltpu.VMEM), out_shape),
        scratch_shapes=scratch,
        compiler_params=pltpu.CompilerParams(vmem_limit_bytes=limit),
        cost_estimate=pl.CostEstimate(flops=flops, bytes_accessed=moved, transcendentals=0),
    )(*scalars, *arrays, *stored)


def shape(dims, dtype):
    return jax.ShapeDtypeStruct(dims, dtype)


def spread(block, axes, count):
    copies = jnp.broadcast_to(block[None], (count,) + block.shape)
    return lax.all_to_all(copies, axes, 0, 0, tiled=True)


def body(x_pre, x_dec, norm_gain, w_qkv, w_out, pre_keys, pre_values, pre_lens, dec_keys, dec_values, dec_lens):
    tokens, pool = x_pre.shape[0], dec_keys.shape[0]
    full = NT * WIDTH
    w_t = jnp.transpose(w_qkv, (0, 2, 1))
    index = (lax.axis_index("x") * NZ + lax.axis_index("z")) * NC + lax.axis_index("c")
    base = (index * pool).astype(jnp.int32).reshape(1)

    def turned(block, shift):
        return lax.ppermute(block, "tp", [(t, (t + shift) % NT) for t in range(NT)])

    tp = lax.axis_index("tp").astype(jnp.int32).reshape(1)
    own = (lax.axis_index("x") * NC + lax.axis_index("c")).astype(jnp.int32).reshape(1)
    x_rows = spread(x_dec, ("x", "c", "tp"), NX * NC * NT)
    x_t = x_pre.T
    x_blocks = [x_t] + [turned(x_t, shift) for shift in range(1, NT)]
    queries, own_queries, hidden = call(
        dec_project_kernel,
        (shape((NZ, 80, 128), BF16), shape((32, WIDTH), BF16), shape((32, full), BF16)),
        (),
        (x_rows, norm_gain.reshape(1, full)),
        (w_t,),
        scratch=[
            pltpu.VMEM((32, full), F32),
            pltpu.VMEM((WIDTH, full), BF16),
            pltpu.SemaphoreType.DMA,
        ],
        flops=2 * 32 * full * WIDTH,
        moved=2 * full * WIDTH,
        limit=VMEM_ALL,
    )
    term_blocks = call(
        prefill_kernel,
        (shape((WIDTH, tokens), F32),)
        + (shape((WIDTH, tokens), BF16),) * 3
        + (shape((2, 32, WIDTH), BF16),),
        (pre_lens, tp),
        (norm_gain.reshape(full, 1), hidden),
        (*x_blocks, w_t, pre_keys.T, pre_values.T, w_out),
        scratch=[
            pltpu.VMEM((full, tokens), BF16),
            pltpu.VMEM((3, WIDTH, full), BF16),
            pltpu.VMEM((WIDTH, pre_keys.shape[0]), BF16),
            pltpu.VMEM((WIDTH, pre_keys.shape[0]), BF16),
            pltpu.VMEM((WIDTH, full), BF16),
            pltpu.VMEM((NT, WIDTH, WIDTH), BF16),
        ]
        + [pltpu.VMEM((WIDTH, tokens), BF16)] * 4
        + [pltpu.SemaphoreType.DMA((12,))],
        flops=8 * tokens * full * WIDTH + 4 * tokens * 896 * WIDTH,
        moved=8 * full * WIDTH,
        limit=VMEM_ALL,
    )
    queries = lax.all_to_all(queries, "z", 0, 0, tiled=True)
    *term_blocks, own_kv = term_blocks
    own_kv, queries = lax.optimization_barrier((own_kv, queries))
    arrived = [turned(block, shift) for shift, block in enumerate(term_blocks) if shift > 0]
    pre_out = term_blocks[0] + sum(block.astype(F32) for block in arrived)
    requests = dec_lens.shape[0]
    partial = call(
        dec_attention_kernel,
        shape((requests, LANES), BF16),
        (base,),
        (queries, dec_lens.reshape(1, requests)),
        (dec_keys.T, dec_values.T),
        scratch=[
            pltpu.VMEM((requests, WIDTH), BF16),
            pltpu.VMEM((WIDTH, pool), BF16),
            pltpu.VMEM((WIDTH, pool), BF16),
            pltpu.SemaphoreType.DMA((2,)),
        ],
        flops=4 * requests * pool * WIDTH,
        moved=4 * pool * WIDTH,
    )
    partial = lax.all_to_all(partial.reshape(NX * NC, NZ * 4, LANES), ("x", "c"), 0, 0, tiled=True)
    partial = call(
        dec_merge_kernel,
        shape((NZ, 4, LANES), BF16),
        (),
        (partial,),
        flops=NX * NC * NZ * 4 * LANES,
        moved=NX * NC * NZ * 16 * LANES,
    )
    partial = lax.all_to_all(partial, "z", 0, 0, tiled=True)
    terms = call(
        dec_finish_kernel,
        shape((NT, 4, WIDTH), F32),
        (own,),
        (partial, own_queries, own_kv, w_out),
        flops=2 * 8 * full * WIDTH,
        moved=2 * full * WIDTH,
    )
    terms = lax.all_to_all(terms, "tp", 0, 0, tiled=True)
    dec_out = jnp.sum(terms, axis=0).astype(BF16)
    return pre_out.astype(BF16).T, dec_out


def solution(mesh):
    req = ("x", "z", "c")
    grid = Mesh(mesh.devices.reshape(NX, NZ, NC, NT), req + ("tp",))
    return jax.shard_map(
        body,
        mesh=grid,
        in_specs=(
            P(req, "tp"),
            P(req, "tp"),
            P(),
            P(None, None, "tp"),
            P("tp", None),
            P(req, "tp"),
            P(req, "tp"),
            P(req),
            P(req, "tp"),
            P(req, "tp"),
            P(),
        ),
        out_specs=(P(req, "tp"), P(req, "tp")),
        check_vma=False,
    )
```

```python
import math

import jax
import jax.numpy as jnp
from jax import lax
from jax.experimental import pallas as pl
from jax.experimental.pallas import tpu as pltpu
from jax.sharding import Mesh
from jax.sharding import PartitionSpec as P

HD = 80
HEADS = 4
WIDTH = HEADS * HD
LANES = 384
EPSILON = 1e-06
MASKED = -1e30
NX, NZ, NC, NT = 4, 16, 2, 4
LOG2E_SCALE = math.log2(math.e) / math.sqrt(HD)
F32, BF16 = jnp.float32, jnp.bfloat16
VMEM_LIMIT = 24 * 1024 * 1024
VMEM_ALL = 58 * 1024 * 1024


def dot(a, b, dims):
    return lax.dot_general(a, b, (dims, ((), ())), preferred_element_type=F32)


def by_head(columns, rows):
    lane = lax.broadcasted_iota(jnp.int32, (rows, WIDTH), 1)
    out = jnp.broadcast_to(columns[HEADS - 1], (rows, WIDTH))
    for h in range(HEADS - 2, -1, -1):
        out = jnp.where(lane < (h + 1) * HD, columns[h], out)
    return out


def normed_rows(x, gain):
    mean_square = jnp.sum(x * x, axis=-1, keepdims=True) * (1.0 / x.shape[-1])
    return (x * lax.rsqrt(mean_square + EPSILON) * gain).astype(BF16)


def dec_project_kernel(x_ref, gain_ref, w_ref, qb_ref, q_ref, hidden_ref, rows):
    for n in range(NX * NC):
        for t in range(NT):
            rows[4 * n : 4 * n + 4, t * WIDTH : (t + 1) * WIDTH] = x_ref[NT * n + t].astype(F32)
    hidden = normed_rows(rows[...], gain_ref[...])
    hidden_ref[...] = hidden
    value = dot(hidden, w_ref[...], ((1,), (1,)))
    q_ref[...] = value.astype(BF16)
    tail = jnp.concatenate([value[0:16, 256:WIDTH], value[16:32, 256:WIDTH]], axis=1)
    packed = jnp.concatenate([value[:, 0:128], value[:, 128:256], tail], axis=0).astype(BF16)
    for z in range(NZ):
        qb_ref[z] = packed


def dec_bounds_kernel(base_ref, lens_ref, bounds_ref, order_ref):
    requests = bounds_ref.shape[0]
    place = lax.broadcasted_iota(jnp.int32, (requests, requests), 0)
    x, c, z, i = place >> 7, (place >> 6) & 1, (place >> 2) & 15, place & 3
    request = (x << 7) | (z << 3) | (c << 2) | i
    arrived = (z << 5) | (x << 3) | (c << 2) | i
    other = lax.broadcasted_iota(jnp.int32, (requests, requests), 1)
    lens = lens_ref[...].astype(F32)
    base = base_ref[0].astype(F32)
    bounds_ref[:, 0:1] = jnp.sum(jnp.where(other < request, lens, 0.0), axis=1, keepdims=True) - base
    bounds_ref[:, 1:2] = jnp.sum(jnp.where(other <= request, lens, 0.0), axis=1, keepdims=True) - base
    order_ref[...] = jnp.where(other == arrived, 1.0, 0.0).astype(BF16)


def dec_attention_kernel(qp_ref, bounds_ref, order_ref, k_ref, v_ref, out_ref, q_s):
    for z in range(NZ):
        rows = slice(32 * z, 32 * z + 32)
        q_s[rows, 0:128] = qp_ref[z, 0:32]
        q_s[rows, 128:256] = qp_ref[z, 32:64]
        q_s[32 * z : 32 * z + 16, 256:WIDTH] = qp_ref[z, 64:80, 0:64]
        q_s[32 * z + 16 : 32 * z + 32, 256:WIDTH] = qp_ref[z, 64:80, 64:128]
    requests, pool = q_s.shape[0], k_ref.shape[1]
    queries = dot(order_ref[...], q_s[...], ((1,), (0,))).astype(BF16)
    row = lax.broadcasted_iota(jnp.int32, (requests, pool), 1).astype(F32)
    allowed = (row >= bounds_ref[:, 0:1]) & (row < bounds_ref[:, 1:2])
    tops, totals = [], []
    for h in range(HEADS):
        s = dot(queries[:, h * HD : (h + 1) * HD], k_ref[h * HD : (h + 1) * HD, :], ((1,), (0,)))
        s = jnp.where(allowed, s, MASKED)
        top = jnp.max(s, axis=1, keepdims=True)
        w = jnp.where(allowed, jnp.exp2((s - top) * LOG2E_SCALE), 0.0)
        total = jnp.sum(w, axis=1, keepdims=True)
        mixed = dot(w.astype(BF16), v_ref[h * HD : (h + 1) * HD, :], ((1,), (1,)))
        out_ref[:, h * HD : (h + 1) * HD] = mixed.astype(BF16)
        tops.append(top)
        totals.append(total)
    out_ref[:, WIDTH:LANES] = stats(tops, totals, requests)


def thirds(value):
    high = value.astype(BF16)
    rest = value - high.astype(F32)
    middle = rest.astype(BF16)
    return high, middle, (rest - middle.astype(F32)).astype(BF16)


def stats(tops, totals, rows):
    lane = lax.broadcasted_iota(jnp.int32, (rows, LANES - WIDTH), 1)
    out = jnp.zeros((rows, LANES - WIDTH), F32)
    for n, value in enumerate(tops + totals):
        for k, part in enumerate(thirds(value)):
            out = jnp.where(lane == 3 * n + k, part.astype(F32), out)
    return out.astype(BF16)


def stat(block, n):
    at = WIDTH + 3 * n
    return block[:, at : at + 1] + block[:, at + 1 : at + 2] + block[:, at + 2 : at + 3]


def merged(parts, rows, stat=stat):
    parts = [part.astype(F32) for part in parts]
    tops, totals, values = [], [], jnp.zeros((rows, WIDTH), F32)
    scales = []
    for h in range(HEADS):
        part_tops = [stat(part, h) for part in parts]
        best = part_tops[0]
        for top in part_tops[1:]:
            best = jnp.maximum(best, top)
        tops.append(best)
        scale = [jnp.exp2((top - best) * LOG2E_SCALE) for top in part_tops]
        scales.append(scale)
        total = jnp.zeros_like(best)
        for part, factor in zip(parts, scale):
            total = total + factor * stat(part, HEADS + h)
        totals.append(total)
    for n, part in enumerate(parts):
        values = values + by_head([scales[h][n] for h in range(HEADS)], rows) * part[:, :WIDTH]
    return values, tops, totals


def dec_merge_kernel(in_ref, out_ref):
    count, rows = in_ref.shape[0], in_ref.shape[1]
    values, tops, totals = merged([in_ref[n] for n in range(count)], rows)
    lane = lax.broadcasted_iota(jnp.int32, (rows, LANES - WIDTH), 1)
    extra = jnp.zeros((rows, LANES - WIDTH), F32)
    for n, value in enumerate(tops + totals):
        extra = jnp.where(lane == n, value, extra)
    for z in range(NZ):
        out_ref[z, :, 0:WIDTH] = values[4 * z : 4 * z + 4]
        out_ref[z, :, WIDTH:LANES] = extra[4 * z : 4 * z + 4]


def dec_finish_kernel(own_ref, in_ref, q_ref, kv_ref, w_ref, out_ref):
    rows = 4
    whole = lambda block, n: block[:, WIDTH + n : WIDTH + n + 1]
    values, tops, totals = merged([in_ref[n] for n in range(NZ)], rows, whole)
    row = lax.broadcasted_iota(jnp.int32, (8, 32), 0) + 4 * own_ref[0]
    mine = jnp.where(row == lax.broadcasted_iota(jnp.int32, (8, 32), 1), 1.0, 0.0).astype(BF16)
    query = dot(mine, q_ref[...], ((1,), (0,)))[0:rows]
    key = dot(mine, kv_ref[0], ((1,), (0,)))[0:rows]
    value = dot(mine, kv_ref[1], ((1,), (0,)))[0:rows]
    product = query * key
    lane = lax.broadcasted_iota(jnp.int32, (rows, WIDTH), 1)
    old, own, below = [], [], []
    for h in range(HEADS):
        inside = (lane >= h * HD) & (lane < (h + 1) * HD)
        score = jnp.sum(jnp.where(inside, product, 0.0), axis=1, keepdims=True)
        best = jnp.maximum(tops[h], score)
        factor = jnp.exp2((tops[h] - best) * LOG2E_SCALE)
        self_weight = jnp.exp2((score - best) * LOG2E_SCALE)
        old.append(factor)
        own.append(self_weight.astype(BF16).astype(F32))
        below.append(factor * totals[h] + self_weight)
    numerator = by_head(old, rows) * values + by_head(own, rows) * value
    attn = (numerator / by_head(below, rows)).astype(BF16)
    terms = dot(attn, w_ref[...], ((1,), (0,)))
    for t in range(NT):
        out_ref[t] = terms[:, t * WIDTH : (t + 1) * WIDTH]


def prefill_kernel(
    len_ref, tp_ref, gain_ref, hd_ref, x0_hbm, x1_hbm, x2_hbm, x3_hbm, w_hbm, kc_hbm, vc_hbm, wo_hbm,
    o0_ref, o1_ref, o2_ref, o3_ref, kv_ref,
    x_ref, w_ref, kc_ref, vc_ref, wo_ref, wo4_s, q_s, k_s, v_s, a_s, sems,
):
    tokens, cached = x_ref.shape[1], kc_ref.shape[1]
    block = 256
    me = tp_ref[0]

    def piece(source, shift, b):
        at = pl.ds(pl.multiple_of(((me - shift + NT) & (NT - 1)) * WIDTH, WIDTH), WIDTH)
        cols = slice(b * block, (b + 1) * block)
        return source.at[:, cols], x_ref.at[at, cols]

    sources = (x0_hbm, x1_hbm, x2_hbm, x3_hbm)
    plan = [piece(source, shift, 0) for shift, source in enumerate(sources)] + [(w_hbm, w_ref)]
    plan += [piece(source, shift, 1) for shift, source in enumerate(sources)]
    plan += [(wo_hbm, wo_ref), (kc_hbm, kc_ref), (vc_hbm, vc_ref)]
    fetches = [
        pltpu.make_async_copy(source, target, sems.at[n]) for n, (source, target) in enumerate(plan)
    ]
    for fetch in fetches:
        fetch.start()
    for b in range(tokens // block):
        cols = slice(b * block, (b + 1) * block)
        for fetch in fetches[5 * b : 5 * b + 4]:
            fetch.wait()
        x = x_ref[:, cols].astype(F32)
        mean_square = jnp.sum(x * x, axis=0, keepdims=True) * (1.0 / x.shape[0])
        hidden = (x * lax.rsqrt(mean_square + EPSILON) * gain_ref[...]).astype(BF16)
        if b == 0:
            fetches[4].wait()
            for part in (1, 2):
                kv_ref[part - 1] = dot(hd_ref[...], w_ref[part], ((1,), (1,))).astype(BF16)
        for part, held in enumerate((q_s, k_s, v_s)):
            held[:, cols] = dot(w_ref[part], hidden, ((1,), (0,))).astype(BF16)
    for fetch in fetches[9:]:
        fetch.wait()
    for t in range(NT):
        wo4_s[t] = wo_ref[:, t * WIDTH : (t + 1) * WIDTH]
    length = len_ref[0]
    for b in range(tokens // block):
        cols = slice(b * block, (b + 1) * block)
        seen = (b + 1) * block
        in_cache = lax.broadcasted_iota(jnp.int32, (cached, block), 0) < length
        causal = lax.broadcasted_iota(jnp.int32, (seen, block), 0) <= (
            lax.broadcasted_iota(jnp.int32, (seen, block), 1) + b * block
        )
        for h in range(HEADS):
            feats = slice(h * HD, (h + 1) * HD)
            query = q_s[feats, cols]
            s_old = jnp.where(in_cache, dot(kc_ref[feats, :], query, ((0,), (0,))), MASKED)
            s_new = jnp.where(causal, dot(k_s[feats, 0:seen], query, ((0,), (0,))), MASKED)
            top = jnp.maximum(
                jnp.max(s_old, axis=0, keepdims=True), jnp.max(s_new, axis=0, keepdims=True)
            )
            w_old = jnp.exp2((s_old - top) * LOG2E_SCALE)
            w_new = jnp.exp2((s_new - top) * LOG2E_SCALE)
            total = jnp.sum(w_old, axis=0, keepdims=True) + jnp.sum(w_new, axis=0, keepdims=True)
            mixed = dot(vc_ref[feats, :], w_old.astype(BF16), ((1,), (0,))) + dot(
                v_s[feats, 0:seen], w_new.astype(BF16), ((1,), (0,))
            )
            a_s[feats, cols] = (mixed / total).astype(BF16)
    for shift, out_ref in enumerate((o0_ref, o1_ref, o2_ref, o3_ref)):
        terms = dot(wo4_s[(me + shift) & (NT - 1)], a_s[...], ((0,), (0,)))
        out_ref[...] = terms.astype(out_ref.dtype)


def call(
    kernel, out_shape, scalars, arrays, stored=(), scratch=(), flops=0, moved=0, limit=VMEM_LIMIT
):
    return pl.pallas_call(
        kernel,
        out_shape=out_shape,
        in_specs=[pl.BlockSpec(memory_space=pltpu.SMEM)] * len(scalars)
        + [pl.BlockSpec(memory_space=pltpu.VMEM)] * len(arrays)
        + [pl.BlockSpec(memory_space=pltpu.HBM)] * len(stored),
        out_specs=jax.tree.map(lambda _: pl.BlockSpec(memory_space=pltpu.VMEM), out_shape),
        scratch_shapes=scratch,
        compiler_params=pltpu.CompilerParams(vmem_limit_bytes=limit),
        cost_estimate=pl.CostEstimate(flops=flops, bytes_accessed=moved, transcendentals=0),
    )(*scalars, *arrays, *stored)


def shape(dims, dtype):
    return jax.ShapeDtypeStruct(dims, dtype)


def spread(block, axes, count):
    copies = jnp.broadcast_to(block[None], (count,) + block.shape)
    return lax.all_to_all(copies, axes, 0, 0, tiled=True)


def body(x_pre, x_dec, norm_gain, w_qkv, w_out, pre_keys, pre_values, pre_lens, dec_keys, dec_values, dec_lens):
    tokens, pool = x_pre.shape[0], dec_keys.shape[0]
    full = NT * WIDTH
    w_t = jnp.transpose(w_qkv, (0, 2, 1))
    index = (lax.axis_index("x") * NZ + lax.axis_index("z")) * NC + lax.axis_index("c")
    base = (index * pool).astype(jnp.int32).reshape(1)

    requests = dec_lens.shape[0]
    bounds, order = call(
        dec_bounds_kernel,
        (shape((requests, 2), F32), shape((requests, requests), BF16)),
        (base,),
        (dec_lens.reshape(1, requests),),
        flops=8 * requests * requests,
        moved=4 * requests * requests,
    )

    def turned(block, shift):
        return lax.ppermute(block, "tp", [(t, (t + shift) % NT) for t in range(NT)])

    tp = lax.axis_index("tp").astype(jnp.int32).reshape(1)
    own = (lax.axis_index("x") * NC + lax.axis_index("c")).astype(jnp.int32).reshape(1)
    x_rows = spread(x_dec, ("x", "c", "tp"), NX * NC * NT)
    x_t = x_pre.T
    x_blocks = [x_t] + [turned(x_t, shift) for shift in range(1, NT)]
    queries, own_queries, hidden = call(
        dec_project_kernel,
        (shape((NZ, 80, 128), BF16), shape((32, WIDTH), BF16), shape((32, full), BF16)),
        (),
        (x_rows, norm_gain.reshape(1, full), w_t[0]),
        scratch=[pltpu.VMEM((32, full), F32)],
        flops=2 * 32 * full * WIDTH,
        moved=2 * full * WIDTH,
    )
    *x_blocks, queries = lax.optimization_barrier((*x_blocks, queries))
    term_blocks = call(
        prefill_kernel,
        (shape((WIDTH, tokens), F32),)
        + (shape((WIDTH, tokens), BF16),) * 3
        + (shape((2, 32, WIDTH), BF16),),
        (pre_lens, tp),
        (norm_gain.reshape(full, 1), hidden),
        (*x_blocks, w_t, pre_keys.T, pre_values.T, w_out),
        scratch=[
            pltpu.VMEM((full, tokens), BF16),
            pltpu.VMEM((3, WIDTH, full), BF16),
            pltpu.VMEM((WIDTH, pre_keys.shape[0]), BF16),
            pltpu.VMEM((WIDTH, pre_keys.shape[0]), BF16),
            pltpu.VMEM((WIDTH, full), BF16),
            pltpu.VMEM((NT, WIDTH, WIDTH), BF16),
        ]
        + [pltpu.VMEM((WIDTH, tokens), BF16)] * 4
        + [pltpu.SemaphoreType.DMA((12,))],
        flops=8 * tokens * full * WIDTH + 4 * tokens * 896 * WIDTH,
        moved=8 * full * WIDTH,
        limit=VMEM_ALL,
    )
    queries = lax.all_to_all(queries, "z", 0, 0, tiled=True)
    *term_blocks, own_kv = term_blocks
    own_kv, queries = lax.optimization_barrier((own_kv, queries))
    arrived = [turned(block, shift) for shift, block in enumerate(term_blocks) if shift > 0]
    pre_out = term_blocks[0] + sum(block.astype(F32) for block in arrived)
    partial = call(
        dec_attention_kernel,
        shape((requests, LANES), BF16),
        (),
        (queries, bounds, order, dec_keys.T, dec_values.T),
        scratch=[pltpu.VMEM((requests, WIDTH), BF16)],
        flops=4 * requests * pool * WIDTH,
        moved=4 * pool * WIDTH,
    )
    partial = lax.all_to_all(partial.reshape(NX * NC, NZ * 4, LANES), ("x", "c"), 0, 0, tiled=True)
    partial = call(
        dec_merge_kernel,
        shape((NZ, 4, LANES), F32),
        (),
        (partial,),
        flops=NX * NC * NZ * 4 * LANES,
        moved=NX * NC * NZ * 16 * LANES,
    )
    partial = lax.all_to_all(partial, "z", 0, 0, tiled=True)
    terms = call(
        dec_finish_kernel,
        shape((NT, 4, WIDTH), F32),
        (own,),
        (partial, own_queries, own_kv, w_out),
        flops=2 * 8 * full * WIDTH,
        moved=2 * full * WIDTH,
    )
    terms = lax.all_to_all(terms, "tp", 0, 0, tiled=True)
    dec_out = jnp.sum(terms, axis=0).astype(BF16)
    return pre_out.astype(BF16).T, dec_out


def solution(mesh):
    req = ("x", "z", "c")
    grid = Mesh(mesh.devices.reshape(NX, NZ, NC, NT), req + ("tp",))
    return jax.shard_map(
        body,
        mesh=grid,
        in_specs=(
            P(req, "tp"),
            P(req, "tp"),
            P(),
            P(None, None, "tp"),
            P("tp", None),
            P(req, "tp"),
            P(req, "tp"),
            P(req),
            P(req, "tp"),
            P(req, "tp"),
            P(),
        ),
        out_specs=(P(req, "tp"), P(req, "tp")),
        check_vma=False,
    )
```

```python
import math

import jax
import jax.numpy as jnp
from jax import lax
from jax.experimental import pallas as pl
from jax.experimental.pallas import tpu as pltpu
from jax.sharding import Mesh
from jax.sharding import PartitionSpec as P

HD = 80
HEADS = 4
WIDTH = HEADS * HD
LANES = 384
EPSILON = 1e-06
MASKED = -1e30
NX, NZ, NC, NT = 4, 16, 2, 4
LOG2E_SCALE = math.log2(math.e) / math.sqrt(HD)
F32, BF16 = jnp.float32, jnp.bfloat16
VMEM_LIMIT = 24 * 1024 * 1024
VMEM_ALL = 58 * 1024 * 1024


def dot(a, b, dims):
    return lax.dot_general(a, b, (dims, ((), ())), preferred_element_type=F32)


def by_head(columns, rows):
    lane = lax.broadcasted_iota(jnp.int32, (rows, WIDTH), 1)
    out = jnp.broadcast_to(columns[HEADS - 1], (rows, WIDTH))
    for h in range(HEADS - 2, -1, -1):
        out = jnp.where(lane < (h + 1) * HD, columns[h], out)
    return out


def normed_rows(x, gain):
    mean_square = jnp.sum(x * x, axis=-1, keepdims=True) * (1.0 / x.shape[-1])
    return (x * lax.rsqrt(mean_square + EPSILON) * gain).astype(BF16)


def dec_project_kernel(x_ref, gain_ref, w_ref, qb_ref, q_ref, hidden_ref, rows):
    for n in range(NX):
        for t in range(NT):
            rows[4 * n : 4 * n + 4, t * WIDTH : (t + 1) * WIDTH] = x_ref[NT * n + t].astype(F32)
    hidden = normed_rows(rows[...], gain_ref[...])
    hidden_ref[...] = hidden
    value = dot(hidden, w_ref[...], ((1,), (1,)))
    q_ref[...] = value.astype(BF16)
    tail = jnp.concatenate([value[0:8, 256:WIDTH], value[8:16, 256:WIDTH]], axis=1)
    packed = jnp.concatenate([value[:, 0:128], value[:, 128:256], tail], axis=0).astype(BF16)
    for z in range(NZ):
        qb_ref[z] = packed


def dec_bounds_kernel(base_ref, lens_ref, bounds_ref, order_ref):
    requests = bounds_ref.shape[0]
    place = lax.broadcasted_iota(jnp.int32, (requests, requests), 0)
    x, c, z, i = place >> 7, (place >> 6) & 1, (place >> 2) & 15, place & 3
    request = (x << 7) | (z << 3) | (c << 2) | i
    arrived = (c << 8) | (z << 4) | (x << 2) | i
    other = lax.broadcasted_iota(jnp.int32, (requests, requests), 1)
    lens = lens_ref[...].astype(F32)
    base = base_ref[0].astype(F32)
    bounds_ref[:, 0:1] = jnp.sum(jnp.where(other < request, lens, 0.0), axis=1, keepdims=True) - base
    bounds_ref[:, 1:2] = jnp.sum(jnp.where(other <= request, lens, 0.0), axis=1, keepdims=True) - base
    order_ref[...] = jnp.where(other == arrived, 1.0, 0.0).astype(BF16)


def dec_attention_kernel(qp_ref, bounds_ref, order_ref, k_ref, v_ref, out_ref, q_s):
    for n in range(NC * NZ):
        at = 16 * n
        q_s[at : at + 16, 0:128] = qp_ref[n, 0:16]
        q_s[at : at + 16, 128:256] = qp_ref[n, 16:32]
        q_s[at : at + 8, 256:WIDTH] = qp_ref[n, 32:40, 0:64]
        q_s[at + 8 : at + 16, 256:WIDTH] = qp_ref[n, 32:40, 64:128]
    requests, pool = q_s.shape[0], k_ref.shape[1]
    queries = dot(order_ref[...], q_s[...], ((1,), (0,))).astype(BF16)
    row = lax.broadcasted_iota(jnp.int32, (requests, pool), 1).astype(F32)
    allowed = (row >= bounds_ref[:, 0:1]) & (row < bounds_ref[:, 1:2])
    tops, totals = [], []
    for h in range(HEADS):
        s = dot(queries[:, h * HD : (h + 1) * HD], k_ref[h * HD : (h + 1) * HD, :], ((1,), (0,)))
        s = jnp.where(allowed, s, MASKED)
        top = jnp.max(s, axis=1, keepdims=True)
        w = jnp.where(allowed, jnp.exp2((s - top) * LOG2E_SCALE), 0.0)
        total = jnp.sum(w, axis=1, keepdims=True)
        mixed = dot(w.astype(BF16), v_ref[h * HD : (h + 1) * HD, :], ((1,), (1,)))
        out_ref[:, h * HD : (h + 1) * HD] = mixed.astype(BF16)
        tops.append(top)
        totals.append(total)
    out_ref[:, WIDTH:LANES] = stats(tops, totals, requests)


def thirds(value):
    high = value.astype(BF16)
    rest = value - high.astype(F32)
    middle = rest.astype(BF16)
    return high, middle, (rest - middle.astype(F32)).astype(BF16)


def stats(tops, totals, rows):
    lane = lax.broadcasted_iota(jnp.int32, (rows, LANES - WIDTH), 1)
    out = jnp.zeros((rows, LANES - WIDTH), F32)
    for n, value in enumerate(tops + totals):
        for k, part in enumerate(thirds(value)):
            out = jnp.where(lane == 3 * n + k, part.astype(F32), out)
    return out.astype(BF16)


def stat(block, n):
    at = WIDTH + 3 * n
    return block[:, at : at + 1] + block[:, at + 1 : at + 2] + block[:, at + 2 : at + 3]


def merged(parts, rows, stat=stat):
    parts = [part.astype(F32) for part in parts]
    tops, totals, values = [], [], jnp.zeros((rows, WIDTH), F32)
    scales = []
    for h in range(HEADS):
        part_tops = [stat(part, h) for part in parts]
        best = part_tops[0]
        for top in part_tops[1:]:
            best = jnp.maximum(best, top)
        tops.append(best)
        scale = [jnp.exp2((top - best) * LOG2E_SCALE) for top in part_tops]
        scales.append(scale)
        total = jnp.zeros_like(best)
        for part, factor in zip(parts, scale):
            total = total + factor * stat(part, HEADS + h)
        totals.append(total)
    for n, part in enumerate(parts):
        values = values + by_head([scales[h][n] for h in range(HEADS)], rows) * part[:, :WIDTH]
    return values, tops, totals


def dec_merge_kernel(in_ref, out_ref):
    count, rows = in_ref.shape[0], in_ref.shape[1]
    values, tops, totals = merged([in_ref[n] for n in range(count)], rows)
    lane = lax.broadcasted_iota(jnp.int32, (rows, LANES - WIDTH), 1)
    extra = jnp.zeros((rows, LANES - WIDTH), F32)
    for n, value in enumerate(tops + totals):
        extra = jnp.where(lane == n, value, extra)
    for z in range(NZ):
        out_ref[z, :, 0:WIDTH] = values[4 * z : 4 * z + 4]
        out_ref[z, :, WIDTH:LANES] = extra[4 * z : 4 * z + 4]


def dec_finish_kernel(own_ref, in_ref, q_ref, kv_ref, w_ref, out_ref):
    rows = 4
    whole = lambda block, n: block[:, WIDTH + n : WIDTH + n + 1]
    values, tops, totals = merged([in_ref[n] for n in range(NZ)], rows, whole)
    row = lax.broadcasted_iota(jnp.int32, (8, 16), 0) + 4 * own_ref[0]
    mine = jnp.where(row == lax.broadcasted_iota(jnp.int32, (8, 16), 1), 1.0, 0.0).astype(BF16)
    query = dot(mine, q_ref[...], ((1,), (0,)))[0:rows]
    key = dot(mine, kv_ref[0], ((1,), (0,)))[0:rows]
    value = dot(mine, kv_ref[1], ((1,), (0,)))[0:rows]
    product = query * key
    lane = lax.broadcasted_iota(jnp.int32, (rows, WIDTH), 1)
    old, own, below = [], [], []
    for h in range(HEADS):
        inside = (lane >= h * HD) & (lane < (h + 1) * HD)
        score = jnp.sum(jnp.where(inside, product, 0.0), axis=1, keepdims=True)
        best = jnp.maximum(tops[h], score)
        factor = jnp.exp2((tops[h] - best) * LOG2E_SCALE)
        self_weight = jnp.exp2((score - best) * LOG2E_SCALE)
        old.append(factor)
        own.append(self_weight.astype(BF16).astype(F32))
        below.append(factor * totals[h] + self_weight)
    numerator = by_head(old, rows) * values + by_head(own, rows) * value
    attn = (numerator / by_head(below, rows)).astype(BF16)
    terms = dot(attn, w_ref[...], ((1,), (0,)))
    for t in range(NT):
        out_ref[t] = terms[:, t * WIDTH : (t + 1) * WIDTH]


def prefill_kernel(
    len_ref, tp_ref, gain_ref, hd_ref, x0_hbm, x1_hbm, x2_hbm, x3_hbm, w_hbm, kc_hbm, vc_hbm, wo_hbm,
    o0_ref, o1_ref, o2_ref, o3_ref, kv_ref,
    x_ref, w_ref, kc_ref, vc_ref, wo_ref, wo4_s, q_s, k_s, v_s, a_s, sems,
):
    tokens, cached = x_ref.shape[1], kc_ref.shape[1]
    block = 256
    me = tp_ref[0]

    def piece(source, shift, b):
        at = pl.ds(pl.multiple_of(((me - shift + NT) & (NT - 1)) * WIDTH, WIDTH), WIDTH)
        cols = slice(b * block, (b + 1) * block)
        return source.at[:, cols], x_ref.at[at, cols]

    sources = (x0_hbm, x1_hbm, x2_hbm, x3_hbm)
    plan = [piece(source, shift, 0) for shift, source in enumerate(sources)] + [(w_hbm, w_ref)]
    plan += [piece(source, shift, 1) for shift, source in enumerate(sources)]
    plan += [(wo_hbm, wo_ref), (kc_hbm, kc_ref), (vc_hbm, vc_ref)]
    fetches = [
        pltpu.make_async_copy(source, target, sems.at[n]) for n, (source, target) in enumerate(plan)
    ]
    for fetch in fetches:
        fetch.start()
    for b in range(tokens // block):
        cols = slice(b * block, (b + 1) * block)
        for fetch in fetches[5 * b : 5 * b + 4]:
            fetch.wait()
        x = x_ref[:, cols].astype(F32)
        mean_square = jnp.sum(x * x, axis=0, keepdims=True) * (1.0 / x.shape[0])
        hidden = (x * lax.rsqrt(mean_square + EPSILON) * gain_ref[...]).astype(BF16)
        if b == 0:
            fetches[4].wait()
            for part in (1, 2):
                kv_ref[part - 1] = dot(hd_ref[...], w_ref[part], ((1,), (1,))).astype(BF16)
        for part, held in enumerate((q_s, k_s, v_s)):
            held[:, cols] = dot(w_ref[part], hidden, ((1,), (0,))).astype(BF16)
    for fetch in fetches[9:]:
        fetch.wait()
    for t in range(NT):
        wo4_s[t] = wo_ref[:, t * WIDTH : (t + 1) * WIDTH]
    length = len_ref[0]
    for b in range(tokens // block):
        cols = slice(b * block, (b + 1) * block)
        seen = (b + 1) * block
        in_cache = lax.broadcasted_iota(jnp.int32, (cached, block), 0) < length
        causal = lax.broadcasted_iota(jnp.int32, (seen, block), 0) <= (
            lax.broadcasted_iota(jnp.int32, (seen, block), 1) + b * block
        )
        for h in range(HEADS):
            feats = slice(h * HD, (h + 1) * HD)
            query = q_s[feats, cols]
            s_old = jnp.where(in_cache, dot(kc_ref[feats, :], query, ((0,), (0,))), MASKED)
            s_new = jnp.where(causal, dot(k_s[feats, 0:seen], query, ((0,), (0,))), MASKED)
            top = jnp.maximum(
                jnp.max(s_old, axis=0, keepdims=True), jnp.max(s_new, axis=0, keepdims=True)
            )
            w_old = jnp.exp2((s_old - top) * LOG2E_SCALE)
            w_new = jnp.exp2((s_new - top) * LOG2E_SCALE)
            total = jnp.sum(w_old, axis=0, keepdims=True) + jnp.sum(w_new, axis=0, keepdims=True)
            mixed = dot(vc_ref[feats, :], w_old.astype(BF16), ((1,), (0,))) + dot(
                v_s[feats, 0:seen], w_new.astype(BF16), ((1,), (0,))
            )
            a_s[feats, cols] = (mixed / total).astype(BF16)
    for shift, out_ref in enumerate((o0_ref, o1_ref, o2_ref, o3_ref)):
        terms = dot(wo4_s[(me + shift) & (NT - 1)], a_s[...], ((0,), (0,)))
        out_ref[...] = terms.astype(out_ref.dtype)


def call(
    kernel, out_shape, scalars, arrays, stored=(), scratch=(), flops=0, moved=0, limit=VMEM_LIMIT
):
    return pl.pallas_call(
        kernel,
        out_shape=out_shape,
        in_specs=[pl.BlockSpec(memory_space=pltpu.SMEM)] * len(scalars)
        + [pl.BlockSpec(memory_space=pltpu.VMEM)] * len(arrays)
        + [pl.BlockSpec(memory_space=pltpu.HBM)] * len(stored),
        out_specs=jax.tree.map(lambda _: pl.BlockSpec(memory_space=pltpu.VMEM), out_shape),
        scratch_shapes=scratch,
        compiler_params=pltpu.CompilerParams(vmem_limit_bytes=limit),
        cost_estimate=pl.CostEstimate(flops=flops, bytes_accessed=moved, transcendentals=0),
    )(*scalars, *arrays, *stored)


def shape(dims, dtype):
    return jax.ShapeDtypeStruct(dims, dtype)


def spread(block, axes, count):
    copies = jnp.broadcast_to(block[None], (count,) + block.shape)
    return lax.all_to_all(copies, axes, 0, 0, tiled=True)


def body(x_pre, x_dec, norm_gain, w_qkv, w_out, pre_keys, pre_values, pre_lens, dec_keys, dec_values, dec_lens):
    tokens, pool = x_pre.shape[0], dec_keys.shape[0]
    full = NT * WIDTH
    w_t = jnp.transpose(w_qkv, (0, 2, 1))
    index = (lax.axis_index("x") * NZ + lax.axis_index("z")) * NC + lax.axis_index("c")
    base = (index * pool).astype(jnp.int32).reshape(1)

    requests = dec_lens.shape[0]
    bounds, order = call(
        dec_bounds_kernel,
        (shape((requests, 2), F32), shape((requests, requests), BF16)),
        (base,),
        (dec_lens.reshape(1, requests),),
        flops=8 * requests * requests,
        moved=4 * requests * requests,
    )

    def turned(block, shift):
        return lax.ppermute(block, "tp", [(t, (t + shift) % NT) for t in range(NT)])

    tp = lax.axis_index("tp").astype(jnp.int32).reshape(1)
    own = lax.axis_index("x").astype(jnp.int32).reshape(1)
    x_rows = spread(x_dec, ("x", "tp"), NX * NT)
    x_t = x_pre.T
    x_blocks = [x_t] + [turned(x_t, shift) for shift in range(1, NT)]
    queries, own_queries, hidden = call(
        dec_project_kernel,
        (shape((NZ, 40, 128), BF16), shape((16, WIDTH), BF16), shape((16, full), BF16)),
        (),
        (x_rows, norm_gain.reshape(1, full), w_t[0]),
        scratch=[pltpu.VMEM((16, full), F32)],
        flops=2 * 16 * full * WIDTH,
        moved=2 * full * WIDTH,
    )
    gain_column = norm_gain.reshape(full, 1)
    *x_blocks, gain_column, bounds, order, queries = lax.optimization_barrier(
        (*x_blocks, gain_column, bounds, order, queries)
    )
    term_blocks = call(
        prefill_kernel,
        (shape((WIDTH, tokens), F32),)
        + (shape((WIDTH, tokens), BF16),) * 3
        + (shape((2, 16, WIDTH), BF16),),
        (pre_lens, tp),
        (gain_column, hidden),
        (*x_blocks, w_t, pre_keys.T, pre_values.T, w_out),
        scratch=[
            pltpu.VMEM((full, tokens), BF16),
            pltpu.VMEM((3, WIDTH, full), BF16),
            pltpu.VMEM((WIDTH, pre_keys.shape[0]), BF16),
            pltpu.VMEM((WIDTH, pre_keys.shape[0]), BF16),
            pltpu.VMEM((WIDTH, full), BF16),
            pltpu.VMEM((NT, WIDTH, WIDTH), BF16),
        ]
        + [pltpu.VMEM((WIDTH, tokens), BF16)] * 4
        + [pltpu.SemaphoreType.DMA((12,))],
        flops=8 * tokens * full * WIDTH + 4 * tokens * 896 * WIDTH,
        moved=8 * full * WIDTH,
        limit=VMEM_ALL,
    )
    queries = lax.all_to_all(queries, "z", 0, 0, tiled=True)
    *term_blocks, own_kv = term_blocks
    own_kv, queries = lax.optimization_barrier((own_kv, queries))
    queries = lax.all_gather(queries, "c", axis=0, tiled=True)
    arrived = [turned(block, shift) for shift, block in enumerate(term_blocks) if shift > 0]
    pre_out = term_blocks[0] + sum(block.astype(F32) for block in arrived)
    partial = call(
        dec_attention_kernel,
        shape((requests, LANES), BF16),
        (),
        (queries, bounds, order, dec_keys.T, dec_values.T),
        scratch=[pltpu.VMEM((requests, WIDTH), BF16)],
        flops=4 * requests * pool * WIDTH,
        moved=4 * pool * WIDTH,
    )
    partial = lax.all_to_all(partial.reshape(NX * NC, NZ * 4, LANES), ("x", "c"), 0, 0, tiled=True)
    partial = call(
        dec_merge_kernel,
        shape((NZ, 4, LANES), F32),
        (),
        (partial,),
        flops=NX * NC * NZ * 4 * LANES,
        moved=NX * NC * NZ * 16 * LANES,
    )
    partial = lax.all_to_all(partial, "z", 0, 0, tiled=True)
    terms = call(
        dec_finish_kernel,
        shape((NT, 4, WIDTH), F32),
        (own,),
        (partial, own_queries, own_kv, w_out),
        flops=2 * 8 * full * WIDTH,
        moved=2 * full * WIDTH,
    )
    terms = lax.all_to_all(terms, "tp", 0, 0, tiled=True)
    dec_out = jnp.sum(terms, axis=0).astype(BF16)
    return pre_out.astype(BF16).T, dec_out


def solution(mesh):
    req = ("x", "z", "c")
    grid = Mesh(mesh.devices.reshape(NX, NZ, NC, NT), req + ("tp",))
    return jax.shard_map(
        body,
        mesh=grid,
        in_specs=(
            P(req, "tp"),
            P(req, "tp"),
            P(),
            P(None, None, "tp"),
            P("tp", None),
            P(req, "tp"),
            P(req, "tp"),
            P(req),
            P(req, "tp"),
            P(req, "tp"),
            P(),
        ),
        out_specs=(P(req, "tp"), P(req, "tp")),
        check_vma=False,
    )
```

```python
import math

import jax
import jax.numpy as jnp
from jax import lax
from jax.experimental import pallas as pl
from jax.experimental.pallas import tpu as pltpu
from jax.sharding import Mesh
from jax.sharding import PartitionSpec as P

HD = 80
HEADS = 4
WIDTH = HEADS * HD
LANES = 384
EPSILON = 1e-06
MASKED = -1e30
NX, NZ, NC, NT = 4, 16, 2, 4
LOG2E_SCALE = math.log2(math.e) / math.sqrt(HD)
F32, BF16 = jnp.float32, jnp.bfloat16
VMEM_LIMIT = 24 * 1024 * 1024
VMEM_ALL = 58 * 1024 * 1024


def dot(a, b, dims):
    return lax.dot_general(a, b, (dims, ((), ())), preferred_element_type=F32)


def by_head(columns, rows):
    lane = lax.broadcasted_iota(jnp.int32, (rows, WIDTH), 1)
    out = jnp.broadcast_to(columns[HEADS - 1], (rows, WIDTH))
    for h in range(HEADS - 2, -1, -1):
        out = jnp.where(lane < (h + 1) * HD, columns[h], out)
    return out


def normed_rows(x, gain):
    mean_square = jnp.sum(x * x, axis=-1, keepdims=True) * (1.0 / x.shape[-1])
    return (x * lax.rsqrt(mean_square + EPSILON) * gain).astype(BF16)


def dec_project_kernel(x_ref, gain_ref, w_ref, qb_ref, q_ref, hidden_ref, rows):
    for n in range(NX):
        for t in range(NT):
            rows[4 * n : 4 * n + 4, t * WIDTH : (t + 1) * WIDTH] = x_ref[NT * n + t].astype(F32)
    hidden = normed_rows(rows[...], gain_ref[...])
    hidden_ref[...] = hidden
    value = dot(hidden, w_ref[...], ((1,), (1,)))
    q_ref[...] = value.astype(BF16)
    tail = jnp.concatenate([value[0:8, 256:WIDTH], value[8:16, 256:WIDTH]], axis=1)
    packed = jnp.concatenate([value[:, 0:128], value[:, 128:256], tail], axis=0).astype(BF16)
    for z in range(NZ):
        qb_ref[z] = packed


def dec_bounds_kernel(base_ref, lens_ref, bounds_ref, order_ref):
    requests = bounds_ref.shape[0]
    place = lax.broadcasted_iota(jnp.int32, (requests, requests), 0)
    x, c, z, i = place >> 7, (place >> 6) & 1, (place >> 2) & 15, place & 3
    request = (x << 7) | (z << 3) | (c << 2) | i
    arrived = (c << 8) | (z << 4) | (x << 2) | i
    other = lax.broadcasted_iota(jnp.int32, (requests, requests), 1)
    lens = lens_ref[...].astype(F32)
    base = base_ref[0].astype(F32)
    bounds_ref[:, 0:1] = jnp.sum(jnp.where(other < request, lens, 0.0), axis=1, keepdims=True) - base
    bounds_ref[:, 1:2] = jnp.sum(jnp.where(other <= request, lens, 0.0), axis=1, keepdims=True) - base
    order_ref[...] = jnp.where(other == arrived, 1.0, 0.0).astype(BF16)


def dec_attention_kernel(qp_ref, bounds_ref, order_ref, k_ref, v_ref, out_ref, q_s):
    for n in range(NC * NZ):
        at = 16 * n
        q_s[at : at + 16, 0:128] = qp_ref[n, 0:16]
        q_s[at : at + 16, 128:256] = qp_ref[n, 16:32]
        q_s[at : at + 8, 256:WIDTH] = qp_ref[n, 32:40, 0:64]
        q_s[at + 8 : at + 16, 256:WIDTH] = qp_ref[n, 32:40, 64:128]
    requests, pool = q_s.shape[0], k_ref.shape[1]
    queries = dot(order_ref[...], q_s[...], ((1,), (0,))).astype(BF16)
    row = lax.broadcasted_iota(jnp.int32, (requests, pool), 1).astype(F32)
    allowed = (row >= bounds_ref[:, 0:1]) & (row < bounds_ref[:, 1:2])
    tops, totals = [], []
    for h in range(HEADS):
        s = dot(queries[:, h * HD : (h + 1) * HD], k_ref[h * HD : (h + 1) * HD, :], ((1,), (0,)))
        s = jnp.where(allowed, s, MASKED)
        top = jnp.max(s, axis=1, keepdims=True)
        w = jnp.where(allowed, jnp.exp2((s - top) * LOG2E_SCALE), 0.0)
        total = jnp.sum(w, axis=1, keepdims=True)
        mixed = dot(w.astype(BF16), v_ref[h * HD : (h + 1) * HD, :], ((1,), (1,)))
        out_ref[:, h * HD : (h + 1) * HD] = mixed.astype(BF16)
        tops.append(top)
        totals.append(total)
    out_ref[:, WIDTH:LANES] = stats(tops, totals, requests)


def thirds(value):
    high = value.astype(BF16)
    rest = value - high.astype(F32)
    middle = rest.astype(BF16)
    return high, middle, (rest - middle.astype(F32)).astype(BF16)


def stats(tops, totals, rows):
    lane = lax.broadcasted_iota(jnp.int32, (rows, LANES - WIDTH), 1)
    out = jnp.zeros((rows, LANES - WIDTH), F32)
    for n, value in enumerate(tops + totals):
        for k, part in enumerate(thirds(value)):
            out = jnp.where(lane == 3 * n + k, part.astype(F32), out)
    return out.astype(BF16)


def stat(block, n):
    at = WIDTH + 3 * n
    return block[:, at : at + 1] + block[:, at + 1 : at + 2] + block[:, at + 2 : at + 3]


def merged(parts, rows, stat=stat):
    parts = [part.astype(F32) for part in parts]
    tops, totals, values = [], [], jnp.zeros((rows, WIDTH), F32)
    scales = []
    for h in range(HEADS):
        part_tops = [stat(part, h) for part in parts]
        best = part_tops[0]
        for top in part_tops[1:]:
            best = jnp.maximum(best, top)
        tops.append(best)
        scale = [jnp.exp2((top - best) * LOG2E_SCALE) for top in part_tops]
        scales.append(scale)
        total = jnp.zeros_like(best)
        for part, factor in zip(parts, scale):
            total = total + factor * stat(part, HEADS + h)
        totals.append(total)
    for n, part in enumerate(parts):
        values = values + by_head([scales[h][n] for h in range(HEADS)], rows) * part[:, :WIDTH]
    return values, tops, totals


def dec_merge_kernel(in_ref, out_ref):
    count, rows = in_ref.shape[0], in_ref.shape[1]
    values, tops, totals = merged([in_ref[n] for n in range(count)], rows)
    lane = lax.broadcasted_iota(jnp.int32, (rows, LANES - WIDTH), 1)
    extra = jnp.zeros((rows, LANES - WIDTH), F32)
    for n, value in enumerate(tops + totals):
        extra = jnp.where(lane == n, value, extra)
    for z in range(NZ):
        out_ref[z, :, 0:WIDTH] = values[4 * z : 4 * z + 4]
        out_ref[z, :, WIDTH:LANES] = extra[4 * z : 4 * z + 4]


def dec_finish_kernel(own_ref, in_ref, q_ref, kv_ref, w_ref, out_ref):
    rows = 4
    whole = lambda block, n: block[:, WIDTH + n : WIDTH + n + 1]
    values, tops, totals = merged([in_ref[n] for n in range(NZ)], rows, whole)
    row = lax.broadcasted_iota(jnp.int32, (8, 16), 0) + 4 * own_ref[0]
    mine = jnp.where(row == lax.broadcasted_iota(jnp.int32, (8, 16), 1), 1.0, 0.0).astype(BF16)
    query = dot(mine, q_ref[...], ((1,), (0,)))[0:rows]
    key = dot(mine, kv_ref[0], ((1,), (0,)))[0:rows]
    value = dot(mine, kv_ref[1], ((1,), (0,)))[0:rows]
    product = query * key
    lane = lax.broadcasted_iota(jnp.int32, (rows, WIDTH), 1)
    old, own, below = [], [], []
    for h in range(HEADS):
        inside = (lane >= h * HD) & (lane < (h + 1) * HD)
        score = jnp.sum(jnp.where(inside, product, 0.0), axis=1, keepdims=True)
        best = jnp.maximum(tops[h], score)
        factor = jnp.exp2((tops[h] - best) * LOG2E_SCALE)
        self_weight = jnp.exp2((score - best) * LOG2E_SCALE)
        old.append(factor)
        own.append(self_weight.astype(BF16).astype(F32))
        below.append(factor * totals[h] + self_weight)
    numerator = by_head(old, rows) * values + by_head(own, rows) * value
    attn = (numerator / by_head(below, rows)).astype(BF16)
    terms = dot(attn, w_ref[...], ((1,), (0,)))
    for t in range(NT):
        out_ref[t] = terms[:, t * WIDTH : (t + 1) * WIDTH]


def prefill_kernel(
    len_ref, tp_ref, gain_ref, hd_ref, x0_hbm, x1_hbm, x2_hbm, x3_hbm, w_hbm, kc_hbm, vc_hbm, wo_hbm,
    o0_ref, o1_ref, o2_ref, o3_ref, kv_ref,
    x_ref, w_ref, kc_ref, vc_ref, wo_ref, wo4_s, gain_s, q_s, k_s, v_s, a_s, sems,
):
    tokens, cached = x_ref.shape[1], kc_ref.shape[1]
    block = 256
    me = tp_ref[0]

    def piece(source, shift, b):
        at = pl.ds(pl.multiple_of(((me - shift + NT) & (NT - 1)) * WIDTH, WIDTH), WIDTH)
        cols = slice(b * block, (b + 1) * block)
        return source.at[:, cols], x_ref.at[at, cols]

    sources = (x0_hbm, x1_hbm, x2_hbm, x3_hbm)
    plan = [piece(source, shift, 0) for shift, source in enumerate(sources)]
    plan += [(w_hbm.at[part], w_ref.at[part]) for part in range(3)]
    plan += [piece(source, shift, 1) for shift, source in enumerate(sources)]
    plan += [(kc_hbm, kc_ref), (vc_hbm, vc_ref), (wo_hbm, wo_ref)]
    fetches = [
        pltpu.make_async_copy(source, target, sems.at[n]) for n, (source, target) in enumerate(plan)
    ]
    for fetch in fetches:
        fetch.start()
    lines = gain_ref.shape[0]
    gain_s[...] = jnp.zeros_like(gain_s)
    gain_s[0:lines] = gain_ref[...]
    gain_t = jnp.transpose(gain_s[...])
    gain = jnp.concatenate([gain_t[:, n : n + 1] for n in range(lines)], axis=0)
    for b in range(tokens // block):
        cols = slice(b * block, (b + 1) * block)
        for fetch in fetches[7 * b : 7 * b + 4]:
            fetch.wait()
        x = x_ref[:, cols].astype(F32)
        mean_square = jnp.sum(x * x, axis=0, keepdims=True) * (1.0 / x.shape[0])
        hidden = (x * lax.rsqrt(mean_square + EPSILON) * gain).astype(BF16)
        for part, held in enumerate((q_s, k_s, v_s)):
            if b == 0:
                fetches[4 + part].wait()
            held[:, cols] = dot(w_ref[part], hidden, ((1,), (0,))).astype(BF16)
    for part in (1, 2):
        kv_ref[part - 1] = dot(hd_ref[...], w_ref[part], ((1,), (1,))).astype(BF16)
    for fetch in fetches[11:]:
        fetch.wait()
    for t in range(NT):
        wo4_s[t] = wo_ref[:, t * WIDTH : (t + 1) * WIDTH]
    length = len_ref[0]
    for b in range(tokens // block):
        cols = slice(b * block, (b + 1) * block)
        seen = (b + 1) * block
        in_cache = lax.broadcasted_iota(jnp.int32, (cached, block), 0) < length
        causal = lax.broadcasted_iota(jnp.int32, (seen, block), 0) <= (
            lax.broadcasted_iota(jnp.int32, (seen, block), 1) + b * block
        )
        for h in range(HEADS):
            feats = slice(h * HD, (h + 1) * HD)
            query = q_s[feats, cols]
            s_old = jnp.where(in_cache, dot(kc_ref[feats, :], query, ((0,), (0,))), MASKED)
            s_new = jnp.where(causal, dot(k_s[feats, 0:seen], query, ((0,), (0,))), MASKED)
            top = jnp.maximum(
                jnp.max(s_old, axis=0, keepdims=True), jnp.max(s_new, axis=0, keepdims=True)
            )
            w_old = jnp.exp2((s_old - top) * LOG2E_SCALE)
            w_new = jnp.exp2((s_new - top) * LOG2E_SCALE)
            total = jnp.sum(w_old, axis=0, keepdims=True) + jnp.sum(w_new, axis=0, keepdims=True)
            mixed = dot(vc_ref[feats, :], w_old.astype(BF16), ((1,), (0,))) + dot(
                v_s[feats, 0:seen], w_new.astype(BF16), ((1,), (0,))
            )
            a_s[feats, cols] = (mixed / total).astype(BF16)
    for shift, out_ref in enumerate((o0_ref, o1_ref, o2_ref, o3_ref)):
        terms = dot(wo4_s[(me + shift) & (NT - 1)], a_s[...], ((0,), (0,)))
        out_ref[...] = terms.astype(out_ref.dtype)


def call(
    kernel, out_shape, scalars, arrays, stored=(), scratch=(), flops=0, moved=0, limit=VMEM_LIMIT
):
    return pl.pallas_call(
        kernel,
        out_shape=out_shape,
        in_specs=[pl.BlockSpec(memory_space=pltpu.SMEM)] * len(scalars)
        + [pl.BlockSpec(memory_space=pltpu.VMEM)] * len(arrays)
        + [pl.BlockSpec(memory_space=pltpu.HBM)] * len(stored),
        out_specs=jax.tree.map(lambda _: pl.BlockSpec(memory_space=pltpu.VMEM), out_shape),
        scratch_shapes=scratch,
        compiler_params=pltpu.CompilerParams(vmem_limit_bytes=limit),
        cost_estimate=pl.CostEstimate(flops=flops, bytes_accessed=moved, transcendentals=0),
    )(*scalars, *arrays, *stored)


def shape(dims, dtype):
    return jax.ShapeDtypeStruct(dims, dtype)


def spread(block, axes, count):
    copies = jnp.broadcast_to(block[None], (count,) + block.shape)
    return lax.all_to_all(copies, axes, 0, 0, tiled=True)


def body(x_pre, x_dec, norm_gain, w_qkv, w_out, pre_keys, pre_values, pre_lens, dec_keys, dec_values, dec_lens):
    tokens, pool = x_pre.shape[0], dec_keys.shape[0]
    full = NT * WIDTH
    w_t = jnp.transpose(w_qkv, (0, 2, 1))
    index = (lax.axis_index("x") * NZ + lax.axis_index("z")) * NC + lax.axis_index("c")
    base = (index * pool).astype(jnp.int32).reshape(1)

    requests = dec_lens.shape[0]
    bounds, order = call(
        dec_bounds_kernel,
        (shape((requests, 2), F32), shape((requests, requests), BF16)),
        (base,),
        (dec_lens.reshape(1, requests),),
        flops=8 * requests * requests,
        moved=4 * requests * requests,
    )

    def turned(block, shift):
        return lax.ppermute(block, "tp", [(t, (t + shift) % NT) for t in range(NT)])

    tp = lax.axis_index("tp").astype(jnp.int32).reshape(1)
    own = lax.axis_index("x").astype(jnp.int32).reshape(1)
    x_rows = spread(x_dec, ("x", "tp"), NX * NT)
    x_t = x_pre.T
    x_blocks = [x_t] + [turned(x_t, shift) for shift in range(1, NT)]
    queries, own_queries, hidden = call(
        dec_project_kernel,
        (shape((NZ, 40, 128), BF16), shape((16, WIDTH), BF16), shape((16, full), BF16)),
        (),
        (x_rows, norm_gain.reshape(1, full), w_t[0]),
        scratch=[pltpu.VMEM((16, full), F32)],
        flops=2 * 16 * full * WIDTH,
        moved=2 * full * WIDTH,
    )
    bounds, order, queries = lax.optimization_barrier((bounds, order, queries))
    queries = lax.all_to_all(queries, "z", 0, 0, tiled=True)
    queries = lax.all_gather(queries, "c", axis=0, tiled=True)
    partial = call(
        dec_attention_kernel,
        shape((requests, LANES), BF16),
        (),
        (queries, bounds, order, dec_keys.T, dec_values.T),
        scratch=[pltpu.VMEM((requests, WIDTH), BF16)],
        flops=4 * requests * pool * WIDTH,
        moved=4 * pool * WIDTH,
    )
    *x_blocks, partial = lax.optimization_barrier((*x_blocks, partial))
    term_blocks = call(
        prefill_kernel,
        (shape((WIDTH, tokens), F32),)
        + (shape((WIDTH, tokens), BF16),) * 3
        + (shape((2, 16, WIDTH), BF16),),
        (pre_lens, tp),
        (norm_gain.reshape(full // 128, 128), hidden),
        (*x_blocks, w_t, pre_keys.T, pre_values.T, w_out),
        scratch=[
            pltpu.VMEM((full, tokens), BF16),
            pltpu.VMEM((3, WIDTH, full), BF16),
            pltpu.VMEM((WIDTH, pre_keys.shape[0]), BF16),
            pltpu.VMEM((WIDTH, pre_keys.shape[0]), BF16),
            pltpu.VMEM((WIDTH, full), BF16),
            pltpu.VMEM((NT, WIDTH, WIDTH), BF16),
            pltpu.VMEM((128, 128), F32),
        ]
        + [pltpu.VMEM((WIDTH, tokens), BF16)] * 4
        + [pltpu.SemaphoreType.DMA((14,))],
        flops=8 * tokens * full * WIDTH + 4 * tokens * 896 * WIDTH,
        moved=8 * full * WIDTH,
        limit=VMEM_ALL,
    )
    partial = lax.all_to_all(partial.reshape(NX * NC, NZ * 4, LANES), ("x", "c"), 0, 0, tiled=True)
    *term_blocks, own_kv = term_blocks
    own_kv, partial = lax.optimization_barrier((own_kv, partial))
    arrived = [turned(block, shift) for shift, block in enumerate(term_blocks) if shift > 0]
    pre_out = term_blocks[0] + sum(block.astype(F32) for block in arrived)
    partial = call(
        dec_merge_kernel,
        shape((NZ, 4, LANES), F32),
        (),
        (partial,),
        flops=NX * NC * NZ * 4 * LANES,
        moved=NX * NC * NZ * 16 * LANES,
    )
    partial = lax.all_to_all(partial, "z", 0, 0, tiled=True)
    terms = call(
        dec_finish_kernel,
        shape((NT, 4, WIDTH), F32),
        (own,),
        (partial, own_queries, own_kv, w_out),
        flops=2 * 8 * full * WIDTH,
        moved=2 * full * WIDTH,
    )
    terms = lax.all_to_all(terms, "tp", 0, 0, tiled=True)
    dec_out = jnp.sum(terms, axis=0).astype(BF16)
    return pre_out.astype(BF16).T, dec_out


def solution(mesh):
    req = ("x", "z", "c")
    grid = Mesh(mesh.devices.reshape(NX, NZ, NC, NT), req + ("tp",))
    return jax.shard_map(
        body,
        mesh=grid,
        in_specs=(
            P(req, "tp"),
            P(req, "tp"),
            P(),
            P(None, None, "tp"),
            P("tp", None),
            P(req, "tp"),
            P(req, "tp"),
            P(req),
            P(req, "tp"),
            P(req, "tp"),
            P(),
        ),
        out_specs=(P(req, "tp"), P(req, "tp")),
        check_vma=False,
    )
```

```python
import math

import jax
import jax.numpy as jnp
from jax import lax
from jax.experimental import pallas as pl
from jax.experimental.pallas import tpu as pltpu
from jax.sharding import Mesh
from jax.sharding import PartitionSpec as P

HD = 80
HEADS = 4
WIDTH = HEADS * HD
LANES = 384
EPSILON = 1e-06
MASKED = -1e30
NX, NZ, NC, NT = 4, 16, 2, 4
LOG2E_SCALE = math.log2(math.e) / math.sqrt(HD)
F32, BF16 = jnp.float32, jnp.bfloat16
VMEM_LIMIT = 24 * 1024 * 1024
VMEM_ALL = 58 * 1024 * 1024


def dot(a, b, dims):
    return lax.dot_general(a, b, (dims, ((), ())), preferred_element_type=F32)


def by_head(columns, rows):
    lane = lax.broadcasted_iota(jnp.int32, (rows, WIDTH), 1)
    out = jnp.broadcast_to(columns[HEADS - 1], (rows, WIDTH))
    for h in range(HEADS - 2, -1, -1):
        out = jnp.where(lane < (h + 1) * HD, columns[h], out)
    return out


def normed_rows(x, gain):
    mean_square = jnp.sum(x * x, axis=-1, keepdims=True) * (1.0 / x.shape[-1])
    return (x * lax.rsqrt(mean_square + EPSILON) * gain).astype(BF16)


def dec_project_kernel(x_ref, gain_ref, w_ref, qb_ref, q_ref, hidden_ref, rows):
    for n in range(NX):
        for t in range(NT):
            rows[4 * n : 4 * n + 4, t * WIDTH : (t + 1) * WIDTH] = x_ref[NT * n + t].astype(F32)
    hidden = normed_rows(rows[...], gain_ref[...])
    hidden_ref[...] = hidden
    value = dot(hidden, w_ref[...], ((1,), (1,)))
    q_ref[...] = value.astype(BF16)
    tail = jnp.concatenate([value[0:8, 256:WIDTH], value[8:16, 256:WIDTH]], axis=1)
    packed = jnp.concatenate([value[:, 0:128], value[:, 128:256], tail], axis=0).astype(BF16)
    for z in range(NZ):
        qb_ref[z] = packed


def dec_bounds_kernel(base_ref, lens_ref, bounds_ref, order_ref):
    requests = bounds_ref.shape[0]
    place = lax.broadcasted_iota(jnp.int32, (requests, requests), 0)
    x, c, z, i = place >> 7, (place >> 6) & 1, (place >> 2) & 15, place & 3
    request = (x << 7) | (z << 3) | (c << 2) | i
    arrived = (c << 8) | (z << 4) | (x << 2) | i
    other = lax.broadcasted_iota(jnp.int32, (requests, requests), 1)
    lens = lens_ref[...].astype(F32)
    base = base_ref[0].astype(F32)
    bounds_ref[:, 0:1] = jnp.sum(jnp.where(other < request, lens, 0.0), axis=1, keepdims=True) - base
    bounds_ref[:, 1:2] = jnp.sum(jnp.where(other <= request, lens, 0.0), axis=1, keepdims=True) - base
    order_ref[...] = jnp.where(other == arrived, 1.0, 0.0).astype(BF16)


def dec_attention_kernel(qp_ref, bounds_ref, order_ref, k_ref, v_ref, out_ref, q_s):
    for n in range(NC * NZ):
        at = 16 * n
        q_s[at : at + 16, 0:128] = qp_ref[n, 0:16]
        q_s[at : at + 16, 128:256] = qp_ref[n, 16:32]
        q_s[at : at + 8, 256:WIDTH] = qp_ref[n, 32:40, 0:64]
        q_s[at + 8 : at + 16, 256:WIDTH] = qp_ref[n, 32:40, 64:128]
    requests, pool = q_s.shape[0], k_ref.shape[1]
    queries = dot(order_ref[...], q_s[...], ((1,), (0,))).astype(BF16)
    row = lax.broadcasted_iota(jnp.int32, (requests, pool), 1).astype(F32)
    allowed = (row >= bounds_ref[:, 0:1]) & (row < bounds_ref[:, 1:2])
    tops, totals = [], []
    for h in range(HEADS):
        s = dot(queries[:, h * HD : (h + 1) * HD], k_ref[h * HD : (h + 1) * HD, :], ((1,), (0,)))
        s = jnp.where(allowed, s, MASKED)
        top = jnp.max(s, axis=1, keepdims=True)
        w = jnp.where(allowed, jnp.exp2((s - top) * LOG2E_SCALE), 0.0)
        total = jnp.sum(w, axis=1, keepdims=True)
        mixed = dot(w.astype(BF16), v_ref[h * HD : (h + 1) * HD, :], ((1,), (1,)))
        out_ref[:, h * HD : (h + 1) * HD] = mixed.astype(BF16)
        tops.append(top)
        totals.append(total)
    out_ref[:, WIDTH:LANES] = stats(tops, totals, requests)


def thirds(value):
    high = value.astype(BF16)
    rest = value - high.astype(F32)
    middle = rest.astype(BF16)
    return high, middle, (rest - middle.astype(F32)).astype(BF16)


def stats(tops, totals, rows):
    lane = lax.broadcasted_iota(jnp.int32, (rows, LANES - WIDTH), 1)
    out = jnp.zeros((rows, LANES - WIDTH), F32)
    for n, value in enumerate(tops + totals):
        for k, part in enumerate(thirds(value)):
            out = jnp.where(lane == 3 * n + k, part.astype(F32), out)
    return out.astype(BF16)


def stat(block, n):
    at = WIDTH + 3 * n
    return block[:, at : at + 1] + block[:, at + 1 : at + 2] + block[:, at + 2 : at + 3]


def merged(parts, rows, stat=stat):
    parts = [part.astype(F32) for part in parts]
    tops, totals, values = [], [], jnp.zeros((rows, WIDTH), F32)
    scales = []
    for h in range(HEADS):
        part_tops = [stat(part, h) for part in parts]
        best = part_tops[0]
        for top in part_tops[1:]:
            best = jnp.maximum(best, top)
        tops.append(best)
        scale = [jnp.exp2((top - best) * LOG2E_SCALE) for top in part_tops]
        scales.append(scale)
        total = jnp.zeros_like(best)
        for part, factor in zip(parts, scale):
            total = total + factor * stat(part, HEADS + h)
        totals.append(total)
    for n, part in enumerate(parts):
        values = values + by_head([scales[h][n] for h in range(HEADS)], rows) * part[:, :WIDTH]
    return values, tops, totals


def dec_merge_kernel(in_ref, out_ref):
    count, rows = in_ref.shape[0], in_ref.shape[1]
    values, tops, totals = merged([in_ref[n] for n in range(count)], rows)
    lane = lax.broadcasted_iota(jnp.int32, (rows, LANES - WIDTH), 1)
    extra = jnp.zeros((rows, LANES - WIDTH), F32)
    for n, value in enumerate(tops + totals):
        extra = jnp.where(lane == n, value, extra)
    for z in range(NZ):
        out_ref[z, :, 0:WIDTH] = values[4 * z : 4 * z + 4]
        out_ref[z, :, WIDTH:LANES] = extra[4 * z : 4 * z + 4]


def dec_finish_kernel(own_ref, in_ref, q_ref, kv_ref, w_ref, out_ref):
    rows = 4
    whole = lambda block, n: block[:, WIDTH + n : WIDTH + n + 1]
    values, tops, totals = merged([in_ref[n] for n in range(NZ)], rows, whole)
    row = lax.broadcasted_iota(jnp.int32, (8, 16), 0) + 4 * own_ref[0]
    mine = jnp.where(row == lax.broadcasted_iota(jnp.int32, (8, 16), 1), 1.0, 0.0).astype(BF16)
    query = dot(mine, q_ref[...], ((1,), (0,)))[0:rows]
    key = dot(mine, kv_ref[0], ((1,), (0,)))[0:rows]
    value = dot(mine, kv_ref[1], ((1,), (0,)))[0:rows]
    product = query * key
    lane = lax.broadcasted_iota(jnp.int32, (rows, WIDTH), 1)
    old, own, below = [], [], []
    for h in range(HEADS):
        inside = (lane >= h * HD) & (lane < (h + 1) * HD)
        score = jnp.sum(jnp.where(inside, product, 0.0), axis=1, keepdims=True)
        best = jnp.maximum(tops[h], score)
        factor = jnp.exp2((tops[h] - best) * LOG2E_SCALE)
        self_weight = jnp.exp2((score - best) * LOG2E_SCALE)
        old.append(factor)
        own.append(self_weight.astype(BF16).astype(F32))
        below.append(factor * totals[h] + self_weight)
    numerator = by_head(old, rows) * values + by_head(own, rows) * value
    attn = (numerator / by_head(below, rows)).astype(BF16)
    terms = dot(attn, w_ref[...], ((1,), (0,)))
    for t in range(NT):
        out_ref[t] = terms[:, t * WIDTH : (t + 1) * WIDTH]


def prefill_kernel(
    len_ref, tp_ref, gain_ref, x0_hbm, x1_hbm, x2_hbm, x3_hbm, w_hbm, kc_hbm, vc_hbm, wo_hbm,
    o0_hbm, o1_hbm, o2_hbm, o3_hbm,
    x_ref, w_ref, kc_ref, vc_ref, wo_ref, wo4_s, gain_s, q_s, k_s, v_s, a_s, own_s, out_s, sems, out_sems,
):
    tokens, cached = x_ref.shape[1], kc_ref.shape[1]
    block = 256
    me = tp_ref[0]

    def place(shift):
        at = pl.multiple_of(((me - shift + NT) & (NT - 1)) * WIDTH, WIDTH)
        return x_ref.at[pl.ds(at, WIDTH), :]

    sources = (x0_hbm, x1_hbm, x2_hbm, x3_hbm)
    plan = [(source, place(shift)) for shift, source in enumerate(sources)]
    plan += [(w_hbm.at[part], w_ref.at[part]) for part in range(3)]
    plan += [(kc_hbm, kc_ref), (vc_hbm, vc_ref), (wo_hbm, wo_ref)]
    fetches = [
        pltpu.make_async_copy(source, target, sems.at[n]) for n, (source, target) in enumerate(plan)
    ]
    for fetch in fetches:
        fetch.start()
    lines = gain_ref.shape[0]
    gain_s[...] = jnp.zeros_like(gain_s)
    gain_s[0:lines] = gain_ref[...]
    gain_t = jnp.transpose(gain_s[...])
    gain = jnp.concatenate([gain_t[:, n : n + 1] for n in range(lines)], axis=0)
    for b in range(tokens // block):
        cols = slice(b * block, (b + 1) * block)
        if b == 0:
            for fetch in fetches[0:4]:
                fetch.wait()
        x = x_ref[:, cols].astype(F32)
        mean_square = jnp.sum(x * x, axis=0, keepdims=True) * (1.0 / x.shape[0])
        hidden = (x * lax.rsqrt(mean_square + EPSILON) * gain).astype(BF16)
        for part, held in enumerate((q_s, k_s, v_s)):
            if b == 0:
                fetches[4 + part].wait()
            held[:, cols] = dot(w_ref[part], hidden, ((1,), (0,))).astype(BF16)
    for fetch in fetches[7:]:
        fetch.wait()
    for t in range(NT):
        wo4_s[t] = wo_ref[:, t * WIDTH : (t + 1) * WIDTH]
    length = len_ref[0]
    for b in range(tokens // block):
        cols = slice(b * block, (b + 1) * block)
        seen = (b + 1) * block
        in_cache = lax.broadcasted_iota(jnp.int32, (cached, block), 0) < length
        causal = lax.broadcasted_iota(jnp.int32, (seen, block), 0) <= (
            lax.broadcasted_iota(jnp.int32, (seen, block), 1) + b * block
        )
        for h in range(HEADS):
            feats = slice(h * HD, (h + 1) * HD)
            query = q_s[feats, cols]
            s_old = jnp.where(in_cache, dot(kc_ref[feats, :], query, ((0,), (0,))), MASKED)
            s_new = jnp.where(causal, dot(k_s[feats, 0:seen], query, ((0,), (0,))), MASKED)
            top = jnp.maximum(
                jnp.max(s_old, axis=0, keepdims=True), jnp.max(s_new, axis=0, keepdims=True)
            )
            w_old = jnp.exp2((s_old - top) * LOG2E_SCALE)
            w_new = jnp.exp2((s_new - top) * LOG2E_SCALE)
            total = jnp.sum(w_old, axis=0, keepdims=True) + jnp.sum(w_new, axis=0, keepdims=True)
            mixed = dot(vc_ref[feats, :], w_old.astype(BF16), ((1,), (0,))) + dot(
                v_s[feats, 0:seen], w_new.astype(BF16), ((1,), (0,))
            )
            a_s[feats, cols] = (mixed / total).astype(BF16)
    sends = []
    for shift, target in ((1, o1_hbm), (2, o2_hbm), (3, o3_hbm), (0, o0_hbm)):
        terms = dot(wo4_s[(me + shift) & (NT - 1)], a_s[...], ((0,), (0,)))
        held = out_s.at[shift - 1] if shift else own_s
        held[...] = terms.astype(target.dtype)
        sends.append(pltpu.make_async_copy(held, target, out_sems.at[shift]))
        sends[-1].start()
    for send in sends:
        send.wait()


def dec_kv_kernel(hd_ref, w_hbm, kv_ref, w_ref, sems):
    fetches = [pltpu.make_async_copy(w_hbm.at[n + 1], w_ref.at[n], sems.at[n]) for n in range(2)]
    for fetch in fetches:
        fetch.start()
    for n, fetch in enumerate(fetches):
        fetch.wait()
        kv_ref[n] = dot(hd_ref[...], w_ref[n], ((1,), (1,))).astype(BF16)


def call(
    kernel, out_shape, scalars, arrays, stored=(), scratch=(), flops=0, moved=0, limit=VMEM_LIMIT,
    out_space=pltpu.VMEM,
):
    return pl.pallas_call(
        kernel,
        out_shape=out_shape,
        in_specs=[pl.BlockSpec(memory_space=pltpu.SMEM)] * len(scalars)
        + [pl.BlockSpec(memory_space=pltpu.VMEM)] * len(arrays)
        + [pl.BlockSpec(memory_space=pltpu.HBM)] * len(stored),
        out_specs=jax.tree.map(lambda _: pl.BlockSpec(memory_space=out_space), out_shape),
        scratch_shapes=scratch,
        compiler_params=pltpu.CompilerParams(vmem_limit_bytes=limit),
        cost_estimate=pl.CostEstimate(flops=flops, bytes_accessed=moved, transcendentals=0),
    )(*scalars, *arrays, *stored)


def shape(dims, dtype):
    return jax.ShapeDtypeStruct(dims, dtype)


def spread(block, axes, count):
    copies = jnp.broadcast_to(block[None], (count,) + block.shape)
    return lax.all_to_all(copies, axes, 0, 0, tiled=True)


def body(x_pre, x_dec, norm_gain, w_qkv, w_out, pre_keys, pre_values, pre_lens, dec_keys, dec_values, dec_lens):
    tokens, pool = x_pre.shape[0], dec_keys.shape[0]
    full = NT * WIDTH
    w_t = jnp.transpose(w_qkv, (0, 2, 1))
    index = (lax.axis_index("x") * NZ + lax.axis_index("z")) * NC + lax.axis_index("c")
    base = (index * pool).astype(jnp.int32).reshape(1)

    requests = dec_lens.shape[0]
    bounds, order = call(
        dec_bounds_kernel,
        (shape((requests, 2), F32), shape((requests, requests), BF16)),
        (base,),
        (dec_lens.reshape(1, requests),),
        flops=8 * requests * requests,
        moved=4 * requests * requests,
    )

    def turned(block, shift):
        return lax.ppermute(block, "tp", [(t, (t + shift) % NT) for t in range(NT)])

    tp = lax.axis_index("tp").astype(jnp.int32).reshape(1)
    own = lax.axis_index("x").astype(jnp.int32).reshape(1)
    x_rows = spread(x_dec, ("x", "tp"), NX * NT)
    x_t = x_pre.T
    x_blocks = [x_t] + [turned(x_t, shift) for shift in range(1, NT)]
    queries, own_queries, hidden = call(
        dec_project_kernel,
        (shape((NZ, 40, 128), BF16), shape((16, WIDTH), BF16), shape((16, full), BF16)),
        (),
        (x_rows, norm_gain.reshape(1, full), w_t[0]),
        scratch=[pltpu.VMEM((16, full), F32)],
        flops=2 * 16 * full * WIDTH,
        moved=2 * full * WIDTH,
    )
    bounds, order, queries = lax.optimization_barrier((bounds, order, queries))
    own_kv = call(
        dec_kv_kernel,
        shape((2, 16, WIDTH), BF16),
        (),
        (hidden,),
        (w_t,),
        scratch=[pltpu.VMEM((2, WIDTH, full), BF16), pltpu.SemaphoreType.DMA((2,))],
        flops=4 * 16 * full * WIDTH,
        moved=4 * full * WIDTH,
        limit=VMEM_ALL,
    )
    queries = lax.all_to_all(queries, "z", 0, 0, tiled=True)
    own_kv, queries = lax.optimization_barrier((own_kv, queries))
    queries = lax.all_gather(queries, "c", axis=0, tiled=True)
    partial = call(
        dec_attention_kernel,
        shape((requests, LANES), BF16),
        (),
        (queries, bounds, order, dec_keys.T, dec_values.T),
        scratch=[pltpu.VMEM((requests, WIDTH), BF16)],
        flops=4 * requests * pool * WIDTH,
        moved=4 * pool * WIDTH,
    )
    *x_blocks, partial = lax.optimization_barrier((*x_blocks, partial))
    term_blocks = call(
        prefill_kernel,
        (shape((WIDTH, tokens), F32),) + (shape((WIDTH, tokens), BF16),) * 3,
        (pre_lens, tp),
        (norm_gain.reshape(full // 128, 128),),
        (*x_blocks, w_t, pre_keys.T, pre_values.T, w_out),
        scratch=[
            pltpu.VMEM((full, tokens), BF16),
            pltpu.VMEM((3, WIDTH, full), BF16),
            pltpu.VMEM((WIDTH, pre_keys.shape[0]), BF16),
            pltpu.VMEM((WIDTH, pre_keys.shape[0]), BF16),
            pltpu.VMEM((WIDTH, full), BF16),
            pltpu.VMEM((NT, WIDTH, WIDTH), BF16),
            pltpu.VMEM((128, 128), F32),
        ]
        + [pltpu.VMEM((WIDTH, tokens), BF16)] * 4
        + [
            pltpu.VMEM((WIDTH, tokens), F32),
            pltpu.VMEM((3, WIDTH, tokens), BF16),
            pltpu.SemaphoreType.DMA((10,)),
            pltpu.SemaphoreType.DMA((4,)),
        ],
        out_space=pltpu.HBM,
        flops=8 * tokens * full * WIDTH + 4 * tokens * 896 * WIDTH,
        moved=8 * full * WIDTH,
        limit=VMEM_ALL,
    )
    partial = lax.all_to_all(partial.reshape(NX * NC, NZ * 4, LANES), ("x", "c"), 0, 0, tiled=True)
    term_blocks = list(term_blocks)
    term_blocks[-1], partial = lax.optimization_barrier((term_blocks[-1], partial))
    arrived = [turned(block, shift) for shift, block in enumerate(term_blocks) if shift > 0]
    pre_out = term_blocks[0] + sum(block.astype(F32) for block in arrived)
    partial = call(
        dec_merge_kernel,
        shape((NZ, 4, LANES), F32),
        (),
        (partial,),
        flops=NX * NC * NZ * 4 * LANES,
        moved=NX * NC * NZ * 16 * LANES,
    )
    partial = lax.all_to_all(partial, "z", 0, 0, tiled=True)
    terms = call(
        dec_finish_kernel,
        shape((NT, 4, WIDTH), F32),
        (own,),
        (partial, own_queries, own_kv, w_out),
        flops=2 * 8 * full * WIDTH,
        moved=2 * full * WIDTH,
    )
    terms = lax.all_to_all(terms, "tp", 0, 0, tiled=True)
    dec_out = jnp.sum(terms, axis=0).astype(BF16)
    return pre_out.astype(BF16).T, dec_out


def solution(mesh):
    req = ("x", "z", "c")
    grid = Mesh(mesh.devices.reshape(NX, NZ, NC, NT), req + ("tp",))
    return jax.shard_map(
        body,
        mesh=grid,
        in_specs=(
            P(req, "tp"),
            P(req, "tp"),
            P(),
            P(None, None, "tp"),
            P("tp", None),
            P(req, "tp"),
            P(req, "tp"),
            P(req),
            P(req, "tp"),
            P(req, "tp"),
            P(),
        ),
        out_specs=(P(req, "tp"), P(req, "tp")),
        check_vma=False,
    )
```

```python
import math

import jax
import jax.numpy as jnp
from jax import lax
from jax.experimental import pallas as pl
from jax.experimental.pallas import tpu as pltpu
from jax.sharding import Mesh
from jax.sharding import PartitionSpec as P

HD = 80
HEADS = 4
WIDTH = HEADS * HD
LANES = 384
EPSILON = 1e-06
MASKED = -1e30
NX, NZ, NC, NT = 4, 16, 2, 4
LOG2E_SCALE = math.log2(math.e) / math.sqrt(HD)
F32, BF16 = jnp.float32, jnp.bfloat16
VMEM_LIMIT = 24 * 1024 * 1024
VMEM_ALL = 58 * 1024 * 1024


def dot(a, b, dims):
    return lax.dot_general(a, b, (dims, ((), ())), preferred_element_type=F32)


def by_head(columns, rows):
    lane = lax.broadcasted_iota(jnp.int32, (rows, WIDTH), 1)
    out = jnp.broadcast_to(columns[HEADS - 1], (rows, WIDTH))
    for h in range(HEADS - 2, -1, -1):
        out = jnp.where(lane < (h + 1) * HD, columns[h], out)
    return out


def normed_rows(x, gain):
    mean_square = jnp.sum(x * x, axis=-1, keepdims=True) * (1.0 / x.shape[-1])
    return (x * lax.rsqrt(mean_square + EPSILON) * gain).astype(BF16)


def dec_project_kernel(x_ref, gain_ref, w_ref, qb_ref, q_ref, hidden_ref, rows):
    for n in range(NX):
        for t in range(NT):
            rows[4 * n : 4 * n + 4, t * WIDTH : (t + 1) * WIDTH] = x_ref[NT * n + t].astype(F32)
    hidden = normed_rows(rows[...], gain_ref[...])
    hidden_ref[...] = hidden
    value = dot(hidden, w_ref[...], ((1,), (1,)))
    q_ref[...] = value.astype(BF16)
    tail = jnp.concatenate([value[0:8, 256:WIDTH], value[8:16, 256:WIDTH]], axis=1)
    packed = jnp.concatenate([value[:, 0:128], value[:, 128:256], tail], axis=0).astype(BF16)
    for z in range(NZ):
        qb_ref[z] = packed


def dec_bounds_kernel(base_ref, lens_ref, bounds_ref, order_ref):
    requests = bounds_ref.shape[0]
    place = lax.broadcasted_iota(jnp.int32, (requests, requests), 0)
    x, c, z, i = place >> 7, (place >> 6) & 1, (place >> 2) & 15, place & 3
    request = (x << 7) | (z << 3) | (c << 2) | i
    arrived = (c << 8) | (z << 4) | (x << 2) | i
    other = lax.broadcasted_iota(jnp.int32, (requests, requests), 1)
    lens = lens_ref[...].astype(F32)
    base = base_ref[0].astype(F32)
    bounds_ref[:, 0:1] = jnp.sum(jnp.where(other < request, lens, 0.0), axis=1, keepdims=True) - base
    bounds_ref[:, 1:2] = jnp.sum(jnp.where(other <= request, lens, 0.0), axis=1, keepdims=True) - base
    order_ref[...] = jnp.where(other == arrived, 1.0, 0.0).astype(BF16)


def dec_attention_kernel(qp_ref, bounds_ref, order_ref, k_ref, v_ref, out_ref, q_s):
    for n in range(NC * NZ):
        at = 16 * n
        q_s[at : at + 16, 0:128] = qp_ref[n, 0:16]
        q_s[at : at + 16, 128:256] = qp_ref[n, 16:32]
        q_s[at : at + 8, 256:WIDTH] = qp_ref[n, 32:40, 0:64]
        q_s[at + 8 : at + 16, 256:WIDTH] = qp_ref[n, 32:40, 64:128]
    requests, pool = q_s.shape[0], k_ref.shape[1]
    queries = dot(order_ref[...], q_s[...], ((1,), (0,))).astype(BF16)
    row = lax.broadcasted_iota(jnp.int32, (requests, pool), 1).astype(F32)
    allowed = (row >= bounds_ref[:, 0:1]) & (row < bounds_ref[:, 1:2])
    tops, totals = [], []
    for h in range(HEADS):
        s = dot(queries[:, h * HD : (h + 1) * HD], k_ref[h * HD : (h + 1) * HD, :], ((1,), (0,)))
        s = jnp.where(allowed, s, MASKED)
        top = jnp.max(s, axis=1, keepdims=True)
        w = jnp.where(allowed, jnp.exp2((s - top) * LOG2E_SCALE), 0.0)
        total = jnp.sum(w, axis=1, keepdims=True)
        mixed = dot(w.astype(BF16), v_ref[h * HD : (h + 1) * HD, :], ((1,), (1,)))
        out_ref[:, h * HD : (h + 1) * HD] = mixed.astype(BF16)
        tops.append(top)
        totals.append(total)
    out_ref[:, WIDTH:LANES] = stats(tops, totals, requests)


def thirds(value):
    high = value.astype(BF16)
    rest = value - high.astype(F32)
    middle = rest.astype(BF16)
    return high, middle, (rest - middle.astype(F32)).astype(BF16)


def stats(tops, totals, rows):
    lane = lax.broadcasted_iota(jnp.int32, (rows, LANES - WIDTH), 1)
    out = jnp.zeros((rows, LANES - WIDTH), F32)
    for n, value in enumerate(tops + totals):
        for k, part in enumerate(thirds(value)):
            out = jnp.where(lane == 3 * n + k, part.astype(F32), out)
    return out.astype(BF16)


def stat(block, n):
    at = WIDTH + 3 * n
    return block[:, at : at + 1] + block[:, at + 1 : at + 2] + block[:, at + 2 : at + 3]


def merged(parts, rows, stat=stat):
    parts = [part.astype(F32) for part in parts]
    tops, totals, values = [], [], jnp.zeros((rows, WIDTH), F32)
    scales = []
    for h in range(HEADS):
        part_tops = [stat(part, h) for part in parts]
        best = part_tops[0]
        for top in part_tops[1:]:
            best = jnp.maximum(best, top)
        tops.append(best)
        scale = [jnp.exp2((top - best) * LOG2E_SCALE) for top in part_tops]
        scales.append(scale)
        total = jnp.zeros_like(best)
        for part, factor in zip(parts, scale):
            total = total + factor * stat(part, HEADS + h)
        totals.append(total)
    for n, part in enumerate(parts):
        values = values + by_head([scales[h][n] for h in range(HEADS)], rows) * part[:, :WIDTH]
    return values, tops, totals


def pick(at, rows_first):
    lanes = LANES - WIDTH
    dims = (WIDTH, lanes) if rows_first else (lanes, WIDTH)
    head = lax.broadcasted_iota(jnp.int32, dims, 0 if rows_first else 1)
    lane = lax.broadcasted_iota(jnp.int32, dims, 1 if rows_first else 0)
    out = jnp.zeros(dims, F32)
    for h in range(HEADS):
        inside = (head == h * HD) if rows_first else (head >= h * HD) & (head < (h + 1) * HD)
        out = jnp.where(inside & at(lane, h), 1.0, out)
    return out.astype(BF16)


def dec_merge_kernel(in_ref, out_ref):
    count, rows = in_ref.shape[0], in_ref.shape[1]
    of_top = pick(lambda lane, h: (lane >= 3 * h) & (lane < 3 * h + 3), False)
    of_total = pick(lambda lane, h: (lane >= 12 + 3 * h) & (lane < 15 + 3 * h), False)
    extras = [in_ref[n, :, WIDTH:LANES] for n in range(count)]
    part_tops = [dot(extra, of_top, ((1,), (0,))) for extra in extras]
    best = part_tops[0]
    for top in part_tops[1:]:
        best = jnp.maximum(best, top)
    values, totals = jnp.zeros((rows, WIDTH), F32), jnp.zeros((rows, WIDTH), F32)
    for n, top in enumerate(part_tops):
        scale = jnp.exp2((top - best) * LOG2E_SCALE)
        values = values + scale * in_ref[n, :, 0:WIDTH].astype(F32)
        totals = totals + scale * dot(extras[n], of_total, ((1,), (0,)))
    extra = jnp.zeros((rows, LANES - WIDTH), F32)
    top_lanes = pick(lambda lane, h: lane == h, True)
    total_lanes = pick(lambda lane, h: lane == HEADS + h, True)
    for top, total in zip(thirds(best), thirds(totals)):
        extra = extra + dot(top, top_lanes, ((1,), (0,))) + dot(total, total_lanes, ((1,), (0,)))
    for z in range(NZ):
        out_ref[z, :, 0:WIDTH] = values[4 * z : 4 * z + 4]
        out_ref[z, :, WIDTH:LANES] = extra[4 * z : 4 * z + 4]


def dec_finish_kernel(own_ref, in_ref, q_ref, kv_ref, w_ref, out_ref):
    rows = 4
    whole = lambda block, n: block[:, WIDTH + n : WIDTH + n + 1]
    values, tops, totals = merged([in_ref[n] for n in range(NZ)], rows, whole)
    row = lax.broadcasted_iota(jnp.int32, (8, 16), 0) + 4 * own_ref[0]
    mine = jnp.where(row == lax.broadcasted_iota(jnp.int32, (8, 16), 1), 1.0, 0.0).astype(BF16)
    query = dot(mine, q_ref[...], ((1,), (0,)))[0:rows]
    key = dot(mine, kv_ref[0], ((1,), (0,)))[0:rows]
    value = dot(mine, kv_ref[1], ((1,), (0,)))[0:rows]
    product = query * key
    lane = lax.broadcasted_iota(jnp.int32, (rows, WIDTH), 1)
    old, own, below = [], [], []
    for h in range(HEADS):
        inside = (lane >= h * HD) & (lane < (h + 1) * HD)
        score = jnp.sum(jnp.where(inside, product, 0.0), axis=1, keepdims=True)
        best = jnp.maximum(tops[h], score)
        factor = jnp.exp2((tops[h] - best) * LOG2E_SCALE)
        self_weight = jnp.exp2((score - best) * LOG2E_SCALE)
        old.append(factor)
        own.append(self_weight.astype(BF16).astype(F32))
        below.append(factor * totals[h] + self_weight)
    numerator = by_head(old, rows) * values + by_head(own, rows) * value
    attn = (numerator / by_head(below, rows)).astype(BF16)
    terms = dot(attn, w_ref[...], ((1,), (0,)))
    for t in range(NT):
        out_ref[t] = terms[:, t * WIDTH : (t + 1) * WIDTH]


def prefill_kernel(
    len_ref, tp_ref, gain_ref, x0_hbm, x1_hbm, x2_hbm, x3_hbm, w_hbm, kc_hbm, vc_hbm, wo_hbm,
    o0_hbm, o1_hbm, o2_hbm, o3_hbm,
    x_ref, w_ref, kc_ref, vc_ref, wo_ref, wo4_s, gain_s, q_s, k_s, v_s, a_s, own_s, out_s, sems, out_sems,
):
    tokens, cached = x_ref.shape[1], kc_ref.shape[1]
    block = 256
    me = tp_ref[0]

    def place(shift):
        at = pl.multiple_of(((me - shift + NT) & (NT - 1)) * WIDTH, WIDTH)
        return x_ref.at[pl.ds(at, WIDTH), :]

    sources = (x0_hbm, x1_hbm, x2_hbm, x3_hbm)
    plan = [(source, place(shift)) for shift, source in enumerate(sources)]
    plan += [(w_hbm.at[part], w_ref.at[part]) for part in range(3)]
    plan += [(kc_hbm, kc_ref), (vc_hbm, vc_ref), (wo_hbm, wo_ref)]
    fetches = [
        pltpu.make_async_copy(source, target, sems.at[n]) for n, (source, target) in enumerate(plan)
    ]
    for fetch in fetches:
        fetch.start()
    lines = gain_ref.shape[0]
    gain_s[...] = jnp.zeros_like(gain_s)
    gain_s[0:lines] = gain_ref[...]
    gain_t = jnp.transpose(gain_s[...])
    gain = jnp.concatenate([gain_t[:, n : n + 1] for n in range(lines)], axis=0)
    for b in range(tokens // block):
        cols = slice(b * block, (b + 1) * block)
        if b == 0:
            for fetch in fetches[0:4]:
                fetch.wait()
        x = x_ref[:, cols].astype(F32)
        mean_square = jnp.sum(x * x, axis=0, keepdims=True) * (1.0 / x.shape[0])
        hidden = (x * lax.rsqrt(mean_square + EPSILON) * gain).astype(BF16)
        for part, held in enumerate((q_s, k_s, v_s)):
            if b == 0:
                fetches[4 + part].wait()
            held[:, cols] = dot(w_ref[part], hidden, ((1,), (0,))).astype(BF16)
    for fetch in fetches[7:]:
        fetch.wait()
    for t in range(NT):
        wo4_s[t] = wo_ref[:, t * WIDTH : (t + 1) * WIDTH]
    length = len_ref[0]
    for b in range(tokens // block):
        cols = slice(b * block, (b + 1) * block)
        seen = (b + 1) * block
        in_cache = lax.broadcasted_iota(jnp.int32, (cached, block), 0) < length
        causal = lax.broadcasted_iota(jnp.int32, (seen, block), 0) <= (
            lax.broadcasted_iota(jnp.int32, (seen, block), 1) + b * block
        )
        for h in range(HEADS):
            feats = slice(h * HD, (h + 1) * HD)
            query = q_s[feats, cols]
            s_old = jnp.where(in_cache, dot(kc_ref[feats, :], query, ((0,), (0,))), MASKED)
            s_new = jnp.where(causal, dot(k_s[feats, 0:seen], query, ((0,), (0,))), MASKED)
            top = jnp.maximum(
                jnp.max(s_old, axis=0, keepdims=True), jnp.max(s_new, axis=0, keepdims=True)
            )
            w_old = jnp.exp2((s_old - top) * LOG2E_SCALE)
            w_new = jnp.exp2((s_new - top) * LOG2E_SCALE)
            total = jnp.sum(w_old, axis=0, keepdims=True) + jnp.sum(w_new, axis=0, keepdims=True)
            mixed = dot(vc_ref[feats, :], w_old.astype(BF16), ((1,), (0,))) + dot(
                v_s[feats, 0:seen], w_new.astype(BF16), ((1,), (0,))
            )
            a_s[feats, cols] = (mixed / total).astype(BF16)
    sends = []
    for shift, target in ((1, o1_hbm), (2, o2_hbm), (3, o3_hbm), (0, o0_hbm)):
        terms = dot(wo4_s[(me + shift) & (NT - 1)], a_s[...], ((0,), (0,)))
        held = out_s.at[shift - 1] if shift else own_s
        held[...] = terms.astype(target.dtype)
        sends.append(pltpu.make_async_copy(held, target, out_sems.at[shift]))
        sends[-1].start()
    for send in sends:
        send.wait()


def add_terms_kernel(own_ref, a_ref, b_ref, c_ref, out_ref):
    total = own_ref[...] + a_ref[...].astype(F32) + b_ref[...].astype(F32) + c_ref[...].astype(F32)
    out_ref[...] = total.astype(BF16)


def dec_kv_kernel(hd_ref, w_hbm, kv_ref, w_ref, sems):
    fetches = [pltpu.make_async_copy(w_hbm.at[n + 1], w_ref.at[n], sems.at[n]) for n in range(2)]
    for fetch in fetches:
        fetch.start()
    for n, fetch in enumerate(fetches):
        fetch.wait()
        kv_ref[n] = dot(hd_ref[...], w_ref[n], ((1,), (1,))).astype(BF16)


def call(
    kernel, out_shape, scalars, arrays, stored=(), scratch=(), flops=0, moved=0, limit=VMEM_LIMIT,
    out_space=pltpu.VMEM,
):
    return pl.pallas_call(
        kernel,
        out_shape=out_shape,
        in_specs=[pl.BlockSpec(memory_space=pltpu.SMEM)] * len(scalars)
        + [pl.BlockSpec(memory_space=pltpu.VMEM)] * len(arrays)
        + [pl.BlockSpec(memory_space=pltpu.HBM)] * len(stored),
        out_specs=jax.tree.map(lambda _: pl.BlockSpec(memory_space=out_space), out_shape),
        scratch_shapes=scratch,
        compiler_params=pltpu.CompilerParams(vmem_limit_bytes=limit),
        cost_estimate=pl.CostEstimate(flops=flops, bytes_accessed=moved, transcendentals=0),
    )(*scalars, *arrays, *stored)


def shape(dims, dtype):
    return jax.ShapeDtypeStruct(dims, dtype)


def spread(block, axes, count):
    copies = jnp.broadcast_to(block[None], (count,) + block.shape)
    return lax.all_to_all(copies, axes, 0, 0, tiled=True)


def body(x_pre, x_dec, norm_gain, w_qkv, w_out, pre_keys, pre_values, pre_lens, dec_keys, dec_values, dec_lens):
    tokens, pool = x_pre.shape[0], dec_keys.shape[0]
    full = NT * WIDTH
    w_t = jnp.transpose(w_qkv, (0, 2, 1))
    index = (lax.axis_index("x") * NZ + lax.axis_index("z")) * NC + lax.axis_index("c")
    base = (index * pool).astype(jnp.int32).reshape(1)

    requests = dec_lens.shape[0]
    bounds, order = call(
        dec_bounds_kernel,
        (shape((requests, 2), F32), shape((requests, requests), BF16)),
        (base,),
        (dec_lens.reshape(1, requests),),
        flops=8 * requests * requests,
        moved=4 * requests * requests,
    )

    def turned(block, shift):
        return lax.ppermute(block, "tp", [(t, (t + shift) % NT) for t in range(NT)])

    tp = lax.axis_index("tp").astype(jnp.int32).reshape(1)
    own = lax.axis_index("x").astype(jnp.int32).reshape(1)
    x_rows = spread(x_dec, ("x", "tp"), NX * NT)
    x_t = x_pre.T
    x_blocks = [x_t] + [turned(x_t, shift) for shift in range(1, NT)]
    queries, own_queries, hidden = call(
        dec_project_kernel,
        (shape((NZ, 40, 128), BF16), shape((16, WIDTH), BF16), shape((16, full), BF16)),
        (),
        (x_rows, norm_gain.reshape(1, full), w_t[0]),
        scratch=[pltpu.VMEM((16, full), F32)],
        flops=2 * 16 * full * WIDTH,
        moved=2 * full * WIDTH,
    )
    bounds, order, queries = lax.optimization_barrier((bounds, order, queries))
    own_kv = call(
        dec_kv_kernel,
        shape((2, 16, WIDTH), BF16),
        (),
        (hidden,),
        (w_t,),
        scratch=[pltpu.VMEM((2, WIDTH, full), BF16), pltpu.SemaphoreType.DMA((2,))],
        flops=4 * 16 * full * WIDTH,
        moved=4 * full * WIDTH,
        limit=VMEM_ALL,
    )
    queries = lax.all_to_all(queries, "z", 0, 0, tiled=True)
    own_kv, queries = lax.optimization_barrier((own_kv, queries))
    queries = lax.all_gather(queries, "c", axis=0, tiled=True)
    partial = call(
        dec_attention_kernel,
        shape((requests, LANES), BF16),
        (),
        (queries, bounds, order, dec_keys.T, dec_values.T),
        scratch=[pltpu.VMEM((requests, WIDTH), BF16)],
        flops=4 * requests * pool * WIDTH,
        moved=4 * pool * WIDTH,
    )
    *x_blocks, partial = lax.optimization_barrier((*x_blocks, partial))
    term_blocks = call(
        prefill_kernel,
        (shape((WIDTH, tokens), F32),) + (shape((WIDTH, tokens), BF16),) * 3,
        (pre_lens, tp),
        (norm_gain.reshape(full // 128, 128),),
        (*x_blocks, w_t, pre_keys.T, pre_values.T, w_out),
        scratch=[
            pltpu.VMEM((full, tokens), BF16),
            pltpu.VMEM((3, WIDTH, full), BF16),
            pltpu.VMEM((WIDTH, pre_keys.shape[0]), BF16),
            pltpu.VMEM((WIDTH, pre_keys.shape[0]), BF16),
            pltpu.VMEM((WIDTH, full), BF16),
            pltpu.VMEM((NT, WIDTH, WIDTH), BF16),
            pltpu.VMEM((128, 128), F32),
        ]
        + [pltpu.VMEM((WIDTH, tokens), BF16)] * 4
        + [
            pltpu.VMEM((WIDTH, tokens), F32),
            pltpu.VMEM((3, WIDTH, tokens), BF16),
            pltpu.SemaphoreType.DMA((10,)),
            pltpu.SemaphoreType.DMA((4,)),
        ],
        out_space=pltpu.HBM,
        flops=8 * tokens * full * WIDTH + 4 * tokens * 896 * WIDTH,
        moved=8 * full * WIDTH,
        limit=VMEM_ALL,
    )
    partial = lax.all_to_all(partial.reshape(NX * NC, NZ * 4, LANES), ("x", "c"), 0, 0, tiled=True)
    term_blocks = list(term_blocks)
    term_blocks[-1], partial = lax.optimization_barrier((term_blocks[-1], partial))
    arrived = [turned(block, shift) for shift, block in enumerate(term_blocks) if shift > 0]
    pre_out = call(
        add_terms_kernel,
        shape((WIDTH, tokens), BF16),
        (),
        (term_blocks[0], *arrived),
        flops=4 * WIDTH * tokens,
        moved=12 * WIDTH * tokens,
    )
    partial = call(
        dec_merge_kernel,
        shape((NZ, 4, LANES), F32),
        (),
        (partial,),
        flops=NX * NC * NZ * 4 * LANES,
        moved=NX * NC * NZ * 16 * LANES,
    )
    partial = lax.all_to_all(partial, "z", 0, 0, tiled=True)
    terms = call(
        dec_finish_kernel,
        shape((NT, 4, WIDTH), F32),
        (own,),
        (partial, own_queries, own_kv, w_out),
        flops=2 * 8 * full * WIDTH,
        moved=2 * full * WIDTH,
    )
    terms = lax.all_to_all(terms, "tp", 0, 0, tiled=True)
    dec_out = jnp.sum(terms, axis=0).astype(BF16)
    return pre_out.T, dec_out


def solution(mesh):
    req = ("x", "z", "c")
    grid = Mesh(mesh.devices.reshape(NX, NZ, NC, NT), req + ("tp",))
    return jax.shard_map(
        body,
        mesh=grid,
        in_specs=(
            P(req, "tp"),
            P(req, "tp"),
            P(),
            P(None, None, "tp"),
            P("tp", None),
            P(req, "tp"),
            P(req, "tp"),
            P(req),
            P(req, "tp"),
            P(req, "tp"),
            P(),
        ),
        out_specs=(P(req, "tp"), P(req, "tp")),
        check_vma=False,
    )
```

```python
import math

import jax
import jax.numpy as jnp
from jax import lax
from jax.experimental import pallas as pl
from jax.experimental.pallas import tpu as pltpu
from jax.sharding import Mesh
from jax.sharding import PartitionSpec as P

HD = 80
HEADS = 4
WIDTH = HEADS * HD
LANES = 384
EPSILON = 1e-06
MASKED = -1e30
NX, NZ, NC, NT = 4, 16, 2, 4
LOG2E_SCALE = math.log2(math.e) / math.sqrt(HD)
F32, BF16 = jnp.float32, jnp.bfloat16
VMEM_LIMIT = 24 * 1024 * 1024
VMEM_ALL = 58 * 1024 * 1024


def dot(a, b, dims):
    return lax.dot_general(a, b, (dims, ((), ())), preferred_element_type=F32)


def by_head(columns, rows):
    lane = lax.broadcasted_iota(jnp.int32, (rows, WIDTH), 1)
    out = jnp.broadcast_to(columns[HEADS - 1], (rows, WIDTH))
    for h in range(HEADS - 2, -1, -1):
        out = jnp.where(lane < (h + 1) * HD, columns[h], out)
    return out


def normed_rows(x, gain):
    mean_square = jnp.sum(x * x, axis=-1, keepdims=True) * (1.0 / x.shape[-1])
    return (x * lax.rsqrt(mean_square + EPSILON) * gain).astype(BF16)


def dec_project_kernel(x_ref, gain_ref, w_ref, qb_ref, q_ref, hidden_ref, rows):
    for n in range(NX):
        for t in range(NT):
            rows[4 * n : 4 * n + 4, t * WIDTH : (t + 1) * WIDTH] = x_ref[NT * n + t].astype(F32)
    hidden = normed_rows(rows[...], gain_ref[...])
    hidden_ref[...] = hidden
    value = dot(hidden, w_ref[...], ((1,), (1,)))
    q_ref[...] = value.astype(BF16)
    tail = jnp.concatenate([value[0:8, 256:WIDTH], value[8:16, 256:WIDTH]], axis=1)
    packed = jnp.concatenate([value[:, 0:128], value[:, 128:256], tail], axis=0).astype(BF16)
    for z in range(NZ):
        qb_ref[z] = packed


def dec_bounds_kernel(base_ref, lens_ref, bounds_ref, order_ref):
    requests = bounds_ref.shape[0]
    place = lax.broadcasted_iota(jnp.int32, (requests, requests), 0)
    x, c, z, i = place >> 7, (place >> 6) & 1, (place >> 2) & 15, place & 3
    request = (x << 7) | (z << 3) | (c << 2) | i
    arrived = (c << 8) | (z << 4) | (x << 2) | i
    other = lax.broadcasted_iota(jnp.int32, (requests, requests), 1)
    lens = lens_ref[...].astype(F32)
    base = base_ref[0].astype(F32)
    bounds_ref[:, 0:1] = jnp.sum(jnp.where(other < request, lens, 0.0), axis=1, keepdims=True) - base
    bounds_ref[:, 1:2] = jnp.sum(jnp.where(other <= request, lens, 0.0), axis=1, keepdims=True) - base
    order_ref[...] = jnp.where(other == arrived, 1.0, 0.0).astype(BF16)


def dec_attention_kernel(qp_ref, bounds_ref, order_ref, k_ref, v_ref, out_ref, q_s):
    for n in range(NC * NZ):
        at = 16 * n
        q_s[at : at + 16, 0:128] = qp_ref[n, 0:16]
        q_s[at : at + 16, 128:256] = qp_ref[n, 16:32]
        q_s[at : at + 8, 256:WIDTH] = qp_ref[n, 32:40, 0:64]
        q_s[at + 8 : at + 16, 256:WIDTH] = qp_ref[n, 32:40, 64:128]
    requests, pool = q_s.shape[0], k_ref.shape[1]
    queries = dot(order_ref[...], q_s[...], ((1,), (0,))).astype(BF16)
    row = lax.broadcasted_iota(jnp.int32, (requests, pool), 1).astype(F32)
    allowed = (row >= bounds_ref[:, 0:1]) & (row < bounds_ref[:, 1:2])
    tops, totals = [], []
    for h in range(HEADS):
        s = dot(queries[:, h * HD : (h + 1) * HD], k_ref[h * HD : (h + 1) * HD, :], ((1,), (0,)))
        s = jnp.where(allowed, s, MASKED)
        top = jnp.max(s, axis=1, keepdims=True)
        w = jnp.where(allowed, jnp.exp2((s - top) * LOG2E_SCALE), 0.0)
        total = jnp.sum(w, axis=1, keepdims=True)
        mixed = dot(w.astype(BF16), v_ref[h * HD : (h + 1) * HD, :], ((1,), (1,)))
        out_ref[:, h * HD : (h + 1) * HD] = mixed.astype(BF16)
        tops.append(top)
        totals.append(total)
    out_ref[:, WIDTH:LANES] = stats(tops, totals, requests)


def thirds(value):
    high = value.astype(BF16)
    rest = value - high.astype(F32)
    middle = rest.astype(BF16)
    return high, middle, (rest - middle.astype(F32)).astype(BF16)


def stats(tops, totals, rows):
    lane = lax.broadcasted_iota(jnp.int32, (rows, LANES - WIDTH), 1)
    out = jnp.zeros((rows, LANES - WIDTH), F32)
    for n, value in enumerate(tops + totals):
        for k, part in enumerate(thirds(value)):
            out = jnp.where(lane == 3 * n + k, part.astype(F32), out)
    return out.astype(BF16)


def stat(block, n):
    at = WIDTH + 3 * n
    return block[:, at : at + 1] + block[:, at + 1 : at + 2] + block[:, at + 2 : at + 3]


def merged(parts, rows, stat=stat):
    parts = [part.astype(F32) for part in parts]
    tops, totals, values = [], [], jnp.zeros((rows, WIDTH), F32)
    scales = []
    for h in range(HEADS):
        part_tops = [stat(part, h) for part in parts]
        best = part_tops[0]
        for top in part_tops[1:]:
            best = jnp.maximum(best, top)
        tops.append(best)
        scale = [jnp.exp2((top - best) * LOG2E_SCALE) for top in part_tops]
        scales.append(scale)
        total = jnp.zeros_like(best)
        for part, factor in zip(parts, scale):
            total = total + factor * stat(part, HEADS + h)
        totals.append(total)
    for n, part in enumerate(parts):
        values = values + by_head([scales[h][n] for h in range(HEADS)], rows) * part[:, :WIDTH]
    return values, tops, totals


def pick(at, rows_first):
    lanes = LANES - WIDTH
    dims = (WIDTH, lanes) if rows_first else (lanes, WIDTH)
    head = lax.broadcasted_iota(jnp.int32, dims, 0 if rows_first else 1)
    lane = lax.broadcasted_iota(jnp.int32, dims, 1 if rows_first else 0)
    out = jnp.zeros(dims, F32)
    for h in range(HEADS):
        inside = (head == h * HD) if rows_first else (head >= h * HD) & (head < (h + 1) * HD)
        out = jnp.where(inside & at(lane, h), 1.0, out)
    return out.astype(BF16)


def dec_merge_kernel(in_ref, out_ref):
    count, rows = in_ref.shape[0], in_ref.shape[1]
    of_top = pick(lambda lane, h: (lane >= 3 * h) & (lane < 3 * h + 3), False)
    of_total = pick(lambda lane, h: (lane >= 12 + 3 * h) & (lane < 15 + 3 * h), False)
    extras = [in_ref[n, :, WIDTH:LANES] for n in range(count)]
    part_tops = [dot(extra, of_top, ((1,), (0,))) for extra in extras]
    best = part_tops[0]
    for top in part_tops[1:]:
        best = jnp.maximum(best, top)
    values, totals = jnp.zeros((rows, WIDTH), F32), jnp.zeros((rows, WIDTH), F32)
    for n, top in enumerate(part_tops):
        scale = jnp.exp2((top - best) * LOG2E_SCALE)
        values = values + scale * in_ref[n, :, 0:WIDTH].astype(F32)
        totals = totals + scale * dot(extras[n], of_total, ((1,), (0,)))
    extra = jnp.zeros((rows, LANES - WIDTH), F32)
    top_lanes = pick(lambda lane, h: lane == h, True)
    total_lanes = pick(lambda lane, h: lane == HEADS + h, True)
    for top, total in zip(thirds(best), thirds(totals)):
        extra = extra + dot(top, top_lanes, ((1,), (0,))) + dot(total, total_lanes, ((1,), (0,)))
    for z in range(NZ):
        out_ref[z, :, 0:WIDTH] = values[4 * z : 4 * z + 4]
        out_ref[z, :, WIDTH:LANES] = extra[4 * z : 4 * z + 4]


def dec_finish_kernel(own_ref, in_ref, q_ref, kv_ref, w_ref, out_ref):
    rows = 4
    whole = lambda block, n: block[:, WIDTH + n : WIDTH + n + 1]
    values, tops, totals = merged([in_ref[n] for n in range(NZ)], rows, whole)
    row = lax.broadcasted_iota(jnp.int32, (8, 16), 0) + 4 * own_ref[0]
    mine = jnp.where(row == lax.broadcasted_iota(jnp.int32, (8, 16), 1), 1.0, 0.0).astype(BF16)
    query = dot(mine, q_ref[...], ((1,), (0,)))[0:rows]
    key = dot(mine, kv_ref[0], ((1,), (0,)))[0:rows]
    value = dot(mine, kv_ref[1], ((1,), (0,)))[0:rows]
    product = query * key
    lane = lax.broadcasted_iota(jnp.int32, (rows, WIDTH), 1)
    old, own, below = [], [], []
    for h in range(HEADS):
        inside = (lane >= h * HD) & (lane < (h + 1) * HD)
        score = jnp.sum(jnp.where(inside, product, 0.0), axis=1, keepdims=True)
        best = jnp.maximum(tops[h], score)
        factor = jnp.exp2((tops[h] - best) * LOG2E_SCALE)
        self_weight = jnp.exp2((score - best) * LOG2E_SCALE)
        old.append(factor)
        own.append(self_weight.astype(BF16).astype(F32))
        below.append(factor * totals[h] + self_weight)
    numerator = by_head(old, rows) * values + by_head(own, rows) * value
    attn = (numerator / by_head(below, rows)).astype(BF16)
    terms = dot(attn, w_ref[...], ((1,), (0,)))
    for t in range(NT):
        out_ref[t] = terms[:, t * WIDTH : (t + 1) * WIDTH]


def prefill_kernel(
    len_ref, tp_ref, gain_ref, x0_hbm, x1_hbm, x2_hbm, x3_hbm, w_hbm, kc_hbm, vc_hbm, wo_hbm,
    o0_hbm, o1_hbm, o2_hbm, o3_hbm,
    x_ref, w_ref, kc_ref, vc_ref, wo_ref, wo4_s, gain_s, q_s, k_s, v_s, a_s, own_s, out_s, sems, out_sems,
):
    tokens, cached = x_ref.shape[1], kc_ref.shape[1]
    block = 512
    me = tp_ref[0]

    def place(shift):
        at = pl.multiple_of(((me - shift + NT) & (NT - 1)) * WIDTH, WIDTH)
        return x_ref.at[pl.ds(at, WIDTH), :]

    sources = (x0_hbm, x1_hbm, x2_hbm, x3_hbm)
    plan = [(source, place(shift)) for shift, source in enumerate(sources)]
    plan += [(w_hbm.at[part], w_ref.at[part]) for part in range(3)]
    plan += [(kc_hbm, kc_ref), (vc_hbm, vc_ref), (wo_hbm, wo_ref)]
    fetches = [
        pltpu.make_async_copy(source, target, sems.at[n]) for n, (source, target) in enumerate(plan)
    ]
    for fetch in fetches:
        fetch.start()
    lines = gain_ref.shape[0]
    gain_s[...] = jnp.zeros_like(gain_s)
    gain_s[0:lines] = gain_ref[...]
    gain_t = jnp.transpose(gain_s[...])
    gain = jnp.concatenate([gain_t[:, n : n + 1] for n in range(lines)], axis=0)
    for b in range(tokens // block):
        cols = slice(b * block, (b + 1) * block)
        if b == 0:
            for fetch in fetches[0:4]:
                fetch.wait()
        x = x_ref[:, cols].astype(F32)
        mean_square = jnp.sum(x * x, axis=0, keepdims=True) * (1.0 / x.shape[0])
        hidden = (x * lax.rsqrt(mean_square + EPSILON) * gain).astype(BF16)
        for part, held in enumerate((q_s, k_s, v_s)):
            if b == 0:
                fetches[4 + part].wait()
            held[:, cols] = dot(w_ref[part], hidden, ((1,), (0,))).astype(BF16)
    for fetch in fetches[7:]:
        fetch.wait()
    for t in range(NT):
        wo4_s[t] = wo_ref[:, t * WIDTH : (t + 1) * WIDTH]
    length = len_ref[0]
    half = tokens // 2
    in_cache = lax.broadcasted_iota(jnp.int32, (cached, tokens), 0) < length
    causal = lax.broadcasted_iota(jnp.int32, (half, half), 0) <= lax.broadcasted_iota(
        jnp.int32, (half, half), 1
    )
    for h in range(HEADS):
        feats = slice(h * HD, (h + 1) * HD)
        old = jnp.where(in_cache, dot(kc_ref[feats, :], q_s[feats, :], ((0,), (0,))), MASKED)
        low = dot(k_s[feats, 0:half], q_s[feats, :], ((0,), (0,)))
        high = dot(k_s[feats, half:tokens], q_s[feats, half:tokens], ((0,), (0,)))
        first = [old[:, 0:half], jnp.where(causal, low[:, 0:half], MASKED)]
        second = [old[:, half:tokens], low[:, half:tokens], jnp.where(causal, high, MASKED)]
        for scores, cols in ((first, slice(0, half)), (second, slice(half, tokens))):
            top = jnp.max(scores[0], axis=0, keepdims=True)
            for part in scores[1:]:
                top = jnp.maximum(top, jnp.max(part, axis=0, keepdims=True))
            weights = [jnp.exp2((part - top) * LOG2E_SCALE) for part in scores]
            total = sum(jnp.sum(part, axis=0, keepdims=True) for part in weights)
            values = [vc_ref[feats, :], v_s[feats, 0:half], v_s[feats, half:tokens]]
            mixed = sum(
                dot(value, weight.astype(BF16), ((1,), (0,)))
                for value, weight in zip(values, weights)
            )
            a_s[feats, cols] = (mixed / total).astype(BF16)
    sends = []
    for shift, target in ((1, o1_hbm), (2, o2_hbm), (3, o3_hbm), (0, o0_hbm)):
        terms = dot(wo4_s[(me + shift) & (NT - 1)], a_s[...], ((0,), (0,)))
        held = out_s.at[shift - 1] if shift else own_s
        held[...] = terms.astype(target.dtype)
        sends.append(pltpu.make_async_copy(held, target, out_sems.at[shift]))
        sends[-1].start()
    for send in sends:
        send.wait()


def add_terms_kernel(own_ref, a_ref, b_ref, c_ref, out_ref):
    total = own_ref[...] + a_ref[...].astype(F32) + b_ref[...].astype(F32) + c_ref[...].astype(F32)
    out_ref[...] = total.astype(BF16)


def dec_kv_kernel(hd_ref, w_hbm, kv_ref, w_ref, sems):
    fetches = [pltpu.make_async_copy(w_hbm.at[n + 1], w_ref.at[n], sems.at[n]) for n in range(2)]
    for fetch in fetches:
        fetch.start()
    for n, fetch in enumerate(fetches):
        fetch.wait()
        kv_ref[n] = dot(hd_ref[...], w_ref[n], ((1,), (1,))).astype(BF16)


def call(
    kernel, out_shape, scalars, arrays, stored=(), scratch=(), flops=0, moved=0, limit=VMEM_LIMIT,
    out_space=pltpu.VMEM,
):
    return pl.pallas_call(
        kernel,
        out_shape=out_shape,
        in_specs=[pl.BlockSpec(memory_space=pltpu.SMEM)] * len(scalars)
        + [pl.BlockSpec(memory_space=pltpu.VMEM)] * len(arrays)
        + [pl.BlockSpec(memory_space=pltpu.HBM)] * len(stored),
        out_specs=jax.tree.map(lambda _: pl.BlockSpec(memory_space=out_space), out_shape),
        scratch_shapes=scratch,
        compiler_params=pltpu.CompilerParams(vmem_limit_bytes=limit),
        cost_estimate=pl.CostEstimate(flops=flops, bytes_accessed=moved, transcendentals=0),
    )(*scalars, *arrays, *stored)


def shape(dims, dtype):
    return jax.ShapeDtypeStruct(dims, dtype)


def spread(block, axes, count):
    copies = jnp.broadcast_to(block[None], (count,) + block.shape)
    return lax.all_to_all(copies, axes, 0, 0, tiled=True)


def body(x_pre, x_dec, norm_gain, w_qkv, w_out, pre_keys, pre_values, pre_lens, dec_keys, dec_values, dec_lens):
    tokens, pool = x_pre.shape[0], dec_keys.shape[0]
    full = NT * WIDTH
    w_t = jnp.transpose(w_qkv, (0, 2, 1))
    index = (lax.axis_index("x") * NZ + lax.axis_index("z")) * NC + lax.axis_index("c")
    base = (index * pool).astype(jnp.int32).reshape(1)

    requests = dec_lens.shape[0]
    bounds, order = call(
        dec_bounds_kernel,
        (shape((requests, 2), F32), shape((requests, requests), BF16)),
        (base,),
        (dec_lens.reshape(1, requests),),
        flops=8 * requests * requests,
        moved=4 * requests * requests,
    )

    def turned(block, shift):
        return lax.ppermute(block, "tp", [(t, (t + shift) % NT) for t in range(NT)])

    tp = lax.axis_index("tp").astype(jnp.int32).reshape(1)
    own = lax.axis_index("x").astype(jnp.int32).reshape(1)
    x_rows = spread(x_dec, ("x", "tp"), NX * NT)
    x_t = x_pre.T
    x_blocks = [x_t] + [turned(x_t, shift) for shift in range(1, NT)]
    queries, own_queries, hidden = call(
        dec_project_kernel,
        (shape((NZ, 40, 128), BF16), shape((16, WIDTH), BF16), shape((16, full), BF16)),
        (),
        (x_rows, norm_gain.reshape(1, full), w_t[0]),
        scratch=[pltpu.VMEM((16, full), F32)],
        flops=2 * 16 * full * WIDTH,
        moved=2 * full * WIDTH,
    )
    bounds, order, queries = lax.optimization_barrier((bounds, order, queries))
    own_kv = call(
        dec_kv_kernel,
        shape((2, 16, WIDTH), BF16),
        (),
        (hidden,),
        (w_t,),
        scratch=[pltpu.VMEM((2, WIDTH, full), BF16), pltpu.SemaphoreType.DMA((2,))],
        flops=4 * 16 * full * WIDTH,
        moved=4 * full * WIDTH,
        limit=VMEM_ALL,
    )
    queries = lax.all_to_all(queries, "z", 0, 0, tiled=True)
    own_kv, queries = lax.optimization_barrier((own_kv, queries))
    queries = lax.all_gather(queries, "c", axis=0, tiled=True)
    partial = call(
        dec_attention_kernel,
        shape((requests, LANES), BF16),
        (),
        (queries, bounds, order, dec_keys.T, dec_values.T),
        scratch=[pltpu.VMEM((requests, WIDTH), BF16)],
        flops=4 * requests * pool * WIDTH,
        moved=4 * pool * WIDTH,
    )
    *x_blocks, partial = lax.optimization_barrier((*x_blocks, partial))
    term_blocks = call(
        prefill_kernel,
        (shape((WIDTH, tokens), F32),) + (shape((WIDTH, tokens), BF16),) * 3,
        (pre_lens, tp),
        (norm_gain.reshape(full // 128, 128),),
        (*x_blocks, w_t, pre_keys.T, pre_values.T, w_out),
        scratch=[
            pltpu.VMEM((full, tokens), BF16),
            pltpu.VMEM((3, WIDTH, full), BF16),
            pltpu.VMEM((WIDTH, pre_keys.shape[0]), BF16),
            pltpu.VMEM((WIDTH, pre_keys.shape[0]), BF16),
            pltpu.VMEM((WIDTH, full), BF16),
            pltpu.VMEM((NT, WIDTH, WIDTH), BF16),
            pltpu.VMEM((128, 128), F32),
        ]
        + [pltpu.VMEM((WIDTH, tokens), BF16)] * 4
        + [
            pltpu.VMEM((WIDTH, tokens), F32),
            pltpu.VMEM((3, WIDTH, tokens), BF16),
            pltpu.SemaphoreType.DMA((10,)),
            pltpu.SemaphoreType.DMA((4,)),
        ],
        out_space=pltpu.HBM,
        flops=8 * tokens * full * WIDTH + 4 * tokens * 896 * WIDTH,
        moved=8 * full * WIDTH,
        limit=VMEM_ALL,
    )
    partial = lax.all_to_all(partial.reshape(NX * NC, NZ * 4, LANES), ("x", "c"), 0, 0, tiled=True)
    term_blocks = list(term_blocks)
    term_blocks[-1], partial = lax.optimization_barrier((term_blocks[-1], partial))
    arrived = [turned(term_blocks[shift], shift) for shift in (2, 1, 3)]
    pre_out = call(
        add_terms_kernel,
        shape((WIDTH, tokens), BF16),
        (),
        (term_blocks[0], *arrived),
        flops=4 * WIDTH * tokens,
        moved=12 * WIDTH * tokens,
    )
    partial = call(
        dec_merge_kernel,
        shape((NZ, 4, LANES), F32),
        (),
        (partial,),
        flops=NX * NC * NZ * 4 * LANES,
        moved=NX * NC * NZ * 16 * LANES,
    )
    partial = lax.all_to_all(partial, "z", 0, 0, tiled=True)
    terms = call(
        dec_finish_kernel,
        shape((NT, 4, WIDTH), F32),
        (own,),
        (partial, own_queries, own_kv, w_out),
        flops=2 * 8 * full * WIDTH,
        moved=2 * full * WIDTH,
    )
    terms = lax.all_to_all(terms, "tp", 0, 0, tiled=True)
    dec_out = jnp.sum(terms, axis=0).astype(BF16)
    return pre_out.T, dec_out


def solution(mesh):
    req = ("x", "z", "c")
    grid = Mesh(mesh.devices.reshape(NX, NZ, NC, NT), req + ("tp",))
    return jax.shard_map(
        body,
        mesh=grid,
        in_specs=(
            P(req, "tp"),
            P(req, "tp"),
            P(),
            P(None, None, "tp"),
            P("tp", None),
            P(req, "tp"),
            P(req, "tp"),
            P(req),
            P(req, "tp"),
            P(req, "tp"),
            P(),
        ),
        out_specs=(P(req, "tp"), P(req, "tp")),
        check_vma=False,
    )
```

```python
import math

import jax
import jax.numpy as jnp
from jax import lax
from jax.experimental import pallas as pl
from jax.experimental.pallas import tpu as pltpu
from jax.sharding import Mesh
from jax.sharding import PartitionSpec as P

HD = 80
HEADS = 4
WIDTH = HEADS * HD
LANES = 384
EPSILON = 1e-06
MASKED = -1e30
NX, NZ, NC, NT = 4, 16, 2, 4
LOG2E_SCALE = math.log2(math.e) / math.sqrt(HD)
F32, BF16 = jnp.float32, jnp.bfloat16
VMEM_LIMIT = 24 * 1024 * 1024
VMEM_ALL = 58 * 1024 * 1024


def dot(a, b, dims):
    return lax.dot_general(a, b, (dims, ((), ())), preferred_element_type=F32)


def by_head(columns, rows):
    lane = lax.broadcasted_iota(jnp.int32, (rows, WIDTH), 1)
    out = jnp.broadcast_to(columns[HEADS - 1], (rows, WIDTH))
    for h in range(HEADS - 2, -1, -1):
        out = jnp.where(lane < (h + 1) * HD, columns[h], out)
    return out


def normed_rows(x, gain):
    mean_square = jnp.sum(x * x, axis=-1, keepdims=True) * (1.0 / x.shape[-1])
    return (x * lax.rsqrt(mean_square + EPSILON) * gain).astype(BF16)


def dec_project_kernel(x_ref, gain_ref, w_ref, qb_ref, q_ref, hidden_ref, rows):
    for n in range(NX):
        for t in range(NT):
            rows[4 * n : 4 * n + 4, t * WIDTH : (t + 1) * WIDTH] = x_ref[NT * n + t].astype(F32)
    hidden = normed_rows(rows[...], gain_ref[...])
    hidden_ref[...] = hidden
    value = dot(hidden, w_ref[...], ((1,), (1,)))
    q_ref[...] = value.astype(BF16)
    tail = jnp.concatenate([value[0:8, 256:WIDTH], value[8:16, 256:WIDTH]], axis=1)
    packed = jnp.concatenate([value[:, 0:128], value[:, 128:256], tail], axis=0).astype(BF16)
    for z in range(NZ):
        qb_ref[z] = packed


def dec_bounds_kernel(base_ref, lens_ref, bounds_ref, order_ref):
    requests = bounds_ref.shape[0]
    place = lax.broadcasted_iota(jnp.int32, (requests, requests), 0)
    x, c, z, i = place >> 7, (place >> 6) & 1, (place >> 2) & 15, place & 3
    request = (x << 7) | (z << 3) | (c << 2) | i
    arrived = (c << 8) | (z << 4) | (x << 2) | i
    other = lax.broadcasted_iota(jnp.int32, (requests, requests), 1)
    lens = lens_ref[...].astype(F32)
    base = base_ref[0].astype(F32)
    bounds_ref[:, 0:1] = jnp.sum(jnp.where(other < request, lens, 0.0), axis=1, keepdims=True) - base
    bounds_ref[:, 1:2] = jnp.sum(jnp.where(other <= request, lens, 0.0), axis=1, keepdims=True) - base
    order_ref[...] = jnp.where(other == arrived, 1.0, 0.0).astype(BF16)


def dec_attention_kernel(qp_ref, bounds_ref, order_ref, k_ref, v_ref, out_ref, q_s):
    for n in range(NC * NZ):
        at = 16 * n
        q_s[at : at + 16, 0:128] = qp_ref[n, 0:16]
        q_s[at : at + 16, 128:256] = qp_ref[n, 16:32]
        q_s[at : at + 8, 256:WIDTH] = qp_ref[n, 32:40, 0:64]
        q_s[at + 8 : at + 16, 256:WIDTH] = qp_ref[n, 32:40, 64:128]
    requests, pool = q_s.shape[0], k_ref.shape[1]
    queries = dot(order_ref[...], q_s[...], ((1,), (0,))).astype(BF16)
    row = lax.broadcasted_iota(jnp.int32, (requests, pool), 1).astype(F32)
    allowed = (row >= bounds_ref[:, 0:1]) & (row < bounds_ref[:, 1:2])
    tops, totals = [], []
    for h in range(HEADS):
        s = dot(queries[:, h * HD : (h + 1) * HD], k_ref[h * HD : (h + 1) * HD, :], ((1,), (0,)))
        s = jnp.where(allowed, s, MASKED)
        top = jnp.max(s, axis=1, keepdims=True)
        w = jnp.exp2((s - top) * LOG2E_SCALE)
        total = jnp.sum(w, axis=1, keepdims=True)
        mixed = dot(w.astype(BF16), v_ref[h * HD : (h + 1) * HD, :], ((1,), (1,)))
        out_ref[:, h * HD : (h + 1) * HD] = mixed.astype(BF16)
        tops.append(top)
        totals.append(total)
    out_ref[:, WIDTH:LANES] = stats(tops, totals, requests)


def thirds(value):
    high = value.astype(BF16)
    rest = value - high.astype(F32)
    middle = rest.astype(BF16)
    return high, middle, (rest - middle.astype(F32)).astype(BF16)


def stats(tops, totals, rows):
    lanes = LANES - WIDTH
    lane = lax.broadcasted_iota(jnp.int32, (rows, lanes), 1)
    flat = jnp.zeros((rows, lanes), F32)
    for n, value in enumerate(tops + totals):
        flat = jnp.where(lane == n, value, flat)
    source = lax.broadcasted_iota(jnp.int32, (lanes, lanes), 0)
    target = lax.broadcasted_iota(jnp.int32, (lanes, lanes), 1)
    out = jnp.zeros((rows, lanes), F32)
    for k, part in enumerate(thirds(flat)):
        move = jnp.where((target == 3 * source + k) & (source < 2 * HEADS), 1.0, 0.0).astype(BF16)
        out = out + dot(part, move, ((1,), (0,)))
    return out.astype(BF16)


def stat(block, n):
    at = WIDTH + 3 * n
    return block[:, at : at + 1] + block[:, at + 1 : at + 2] + block[:, at + 2 : at + 3]


def merged(parts, rows, stat=stat):
    parts = [part.astype(F32) for part in parts]
    tops, totals, values = [], [], jnp.zeros((rows, WIDTH), F32)
    scales = []
    for h in range(HEADS):
        part_tops = [stat(part, h) for part in parts]
        best = part_tops[0]
        for top in part_tops[1:]:
            best = jnp.maximum(best, top)
        tops.append(best)
        scale = [jnp.exp2((top - best) * LOG2E_SCALE) for top in part_tops]
        scales.append(scale)
        total = jnp.zeros_like(best)
        for part, factor in zip(parts, scale):
            total = total + factor * stat(part, HEADS + h)
        totals.append(total)
    for n, part in enumerate(parts):
        values = values + by_head([scales[h][n] for h in range(HEADS)], rows) * part[:, :WIDTH]
    return values, tops, totals


def pick(at, rows_first):
    lanes = LANES - WIDTH
    dims = (WIDTH, lanes) if rows_first else (lanes, WIDTH)
    head = lax.broadcasted_iota(jnp.int32, dims, 0 if rows_first else 1)
    lane = lax.broadcasted_iota(jnp.int32, dims, 1 if rows_first else 0)
    out = jnp.zeros(dims, F32)
    for h in range(HEADS):
        inside = (head == h * HD) if rows_first else (head >= h * HD) & (head < (h + 1) * HD)
        out = jnp.where(inside & at(lane, h), 1.0, out)
    return out.astype(BF16)


def dec_merge_kernel(in_ref, out_ref):
    count, rows = in_ref.shape[0], in_ref.shape[1]
    of_top = pick(lambda lane, h: (lane >= 3 * h) & (lane < 3 * h + 3), False)
    of_total = pick(lambda lane, h: (lane >= 12 + 3 * h) & (lane < 15 + 3 * h), False)
    extras = [in_ref[n, :, WIDTH:LANES] for n in range(count)]
    part_tops = [dot(extra, of_top, ((1,), (0,))) for extra in extras]
    best = part_tops[0]
    for top in part_tops[1:]:
        best = jnp.maximum(best, top)
    values, totals = jnp.zeros((rows, WIDTH), F32), jnp.zeros((rows, WIDTH), F32)
    for n, top in enumerate(part_tops):
        scale = jnp.exp2((top - best) * LOG2E_SCALE)
        values = values + scale * in_ref[n, :, 0:WIDTH].astype(F32)
        totals = totals + scale * dot(extras[n], of_total, ((1,), (0,)))
    extra = jnp.zeros((rows, LANES - WIDTH), F32)
    top_lanes = pick(lambda lane, h: lane == h, True)
    total_lanes = pick(lambda lane, h: lane == HEADS + h, True)
    for top, total in zip(thirds(best), thirds(totals)):
        extra = extra + dot(top, top_lanes, ((1,), (0,))) + dot(total, total_lanes, ((1,), (0,)))
    for z in range(NZ):
        out_ref[z, :, 0:WIDTH] = values[4 * z : 4 * z + 4]
        out_ref[z, :, WIDTH:LANES] = extra[4 * z : 4 * z + 4]


def dec_finish_kernel(own_ref, in_ref, q_ref, kv_ref, w_ref, out_ref):
    rows = 4
    whole = lambda block, n: block[:, WIDTH + n : WIDTH + n + 1]
    values, tops, totals = merged([in_ref[n] for n in range(NZ)], rows, whole)
    row = lax.broadcasted_iota(jnp.int32, (8, 16), 0) + 4 * own_ref[0]
    mine = jnp.where(row == lax.broadcasted_iota(jnp.int32, (8, 16), 1), 1.0, 0.0).astype(BF16)
    query = dot(mine, q_ref[...], ((1,), (0,)))[0:rows]
    key = dot(mine, kv_ref[0], ((1,), (0,)))[0:rows]
    value = dot(mine, kv_ref[1], ((1,), (0,)))[0:rows]
    product = query * key
    lane = lax.broadcasted_iota(jnp.int32, (rows, WIDTH), 1)
    old, own, below = [], [], []
    for h in range(HEADS):
        inside = (lane >= h * HD) & (lane < (h + 1) * HD)
        score = jnp.sum(jnp.where(inside, product, 0.0), axis=1, keepdims=True)
        best = jnp.maximum(tops[h], score)
        factor = jnp.exp2((tops[h] - best) * LOG2E_SCALE)
        self_weight = jnp.exp2((score - best) * LOG2E_SCALE)
        old.append(factor)
        own.append(self_weight.astype(BF16).astype(F32))
        below.append(factor * totals[h] + self_weight)
    numerator = by_head(old, rows) * values + by_head(own, rows) * value
    attn = (numerator / by_head(below, rows)).astype(BF16)
    terms = dot(attn, w_ref[...], ((1,), (0,)))
    for t in range(NT):
        out_ref[t] = terms[:, t * WIDTH : (t + 1) * WIDTH]


def prefill_kernel(
    len_ref, tp_ref, gain_ref, x0_hbm, x1_hbm, x2_hbm, x3_hbm, w_hbm, kc_hbm, vc_hbm, wo_hbm,
    o0_hbm, o1_hbm, o2_hbm, o3_hbm,
    x_ref, w_ref, kc_ref, vc_ref, wo_ref, wo4_s, gain_s, q_s, k_s, v_s, a_s, own_s, out_s, sems, out_sems,
):
    tokens, cached = x_ref.shape[1], kc_ref.shape[1]
    block = 512
    me = tp_ref[0]

    def place(shift):
        at = pl.multiple_of(((me - shift + NT) & (NT - 1)) * WIDTH, WIDTH)
        return x_ref.at[pl.ds(at, WIDTH), :]

    sources = (x0_hbm, x1_hbm, x2_hbm, x3_hbm)
    plan = [(source, place(shift)) for shift, source in enumerate(sources)]
    plan += [(w_hbm.at[part], w_ref.at[part]) for part in range(3)]
    plan += [(kc_hbm, kc_ref), (vc_hbm, vc_ref), (wo_hbm, wo_ref)]
    fetches = [
        pltpu.make_async_copy(source, target, sems.at[n]) for n, (source, target) in enumerate(plan)
    ]
    for fetch in fetches:
        fetch.start()
    lines = gain_ref.shape[0]
    gain_s[...] = jnp.zeros_like(gain_s)
    gain_s[0:lines] = gain_ref[...]
    gain_t = jnp.transpose(gain_s[...])
    gain = jnp.concatenate([gain_t[:, n : n + 1] for n in range(lines)], axis=0)
    for b in range(tokens // block):
        cols = slice(b * block, (b + 1) * block)
        if b == 0:
            for fetch in fetches[0:4]:
                fetch.wait()
        x = x_ref[:, cols].astype(F32)
        mean_square = jnp.sum(x * x, axis=0, keepdims=True) * (1.0 / x.shape[0])
        hidden = (x * lax.rsqrt(mean_square + EPSILON) * gain).astype(BF16)
        for part, held in enumerate((q_s, k_s, v_s)):
            if b == 0:
                fetches[4 + part].wait()
            held[:, cols] = dot(w_ref[part], hidden, ((1,), (0,))).astype(BF16)
    for fetch in fetches[7:]:
        fetch.wait()
    for t in range(NT):
        wo4_s[t] = wo_ref[:, t * WIDTH : (t + 1) * WIDTH]
    length = len_ref[0]
    half = tokens // 2
    in_cache = lax.broadcasted_iota(jnp.int32, (cached, tokens), 0) < length
    causal = lax.broadcasted_iota(jnp.int32, (half, half), 0) <= lax.broadcasted_iota(
        jnp.int32, (half, half), 1
    )
    for h in range(HEADS):
        feats = slice(h * HD, (h + 1) * HD)
        old = jnp.where(in_cache, dot(kc_ref[feats, :], q_s[feats, :], ((0,), (0,))), MASKED)
        low = dot(k_s[feats, 0:half], q_s[feats, :], ((0,), (0,)))
        high = dot(k_s[feats, half:tokens], q_s[feats, half:tokens], ((0,), (0,)))
        first = [old[:, 0:half], jnp.where(causal, low[:, 0:half], MASKED)]
        second = [old[:, half:tokens], low[:, half:tokens], jnp.where(causal, high, MASKED)]
        for scores, cols in ((first, slice(0, half)), (second, slice(half, tokens))):
            top = jnp.max(scores[0], axis=0, keepdims=True)
            for part in scores[1:]:
                top = jnp.maximum(top, jnp.max(part, axis=0, keepdims=True))
            weights = [jnp.exp2((part - top) * LOG2E_SCALE) for part in scores]
            total = sum(jnp.sum(part, axis=0, keepdims=True) for part in weights)
            values = [vc_ref[feats, :], v_s[feats, 0:half], v_s[feats, half:tokens]]
            mixed = sum(
                dot(value, weight.astype(BF16), ((1,), (0,)))
                for value, weight in zip(values, weights)
            )
            a_s[feats, cols] = (mixed / total).astype(BF16)
    sends = []
    for shift, target in ((1, o1_hbm), (2, o2_hbm), (3, o3_hbm), (0, o0_hbm)):
        terms = dot(wo4_s[(me + shift) & (NT - 1)], a_s[...], ((0,), (0,)))
        held = out_s.at[shift - 1] if shift else own_s
        held[...] = terms.astype(target.dtype)
        sends.append(pltpu.make_async_copy(held, target, out_sems.at[shift]))
        sends[-1].start()
    for send in sends:
        send.wait()


def add_terms_kernel(own_ref, a_ref, b_ref, c_ref, out_ref):
    total = own_ref[...] + a_ref[...].astype(F32) + b_ref[...].astype(F32) + c_ref[...].astype(F32)
    out_ref[...] = total.astype(BF16)


def dec_kv_kernel(hd_ref, w_hbm, kv_ref, w_ref, sems):
    fetches = [pltpu.make_async_copy(w_hbm.at[n + 1], w_ref.at[n], sems.at[n]) for n in range(2)]
    for fetch in fetches:
        fetch.start()
    for n, fetch in enumerate(fetches):
        fetch.wait()
        kv_ref[n] = dot(hd_ref[...], w_ref[n], ((1,), (1,))).astype(BF16)


def call(
    kernel, out_shape, scalars, arrays, stored=(), scratch=(), flops=0, moved=0, limit=VMEM_LIMIT,
    out_space=pltpu.VMEM,
):
    return pl.pallas_call(
        kernel,
        out_shape=out_shape,
        in_specs=[pl.BlockSpec(memory_space=pltpu.SMEM)] * len(scalars)
        + [pl.BlockSpec(memory_space=pltpu.VMEM)] * len(arrays)
        + [pl.BlockSpec(memory_space=pltpu.HBM)] * len(stored),
        out_specs=jax.tree.map(lambda _: pl.BlockSpec(memory_space=out_space), out_shape),
        scratch_shapes=scratch,
        compiler_params=pltpu.CompilerParams(vmem_limit_bytes=limit),
        cost_estimate=pl.CostEstimate(flops=flops, bytes_accessed=moved, transcendentals=0),
    )(*scalars, *arrays, *stored)


def shape(dims, dtype):
    return jax.ShapeDtypeStruct(dims, dtype)


def spread(block, axes, count):
    copies = jnp.broadcast_to(block[None], (count,) + block.shape)
    return lax.all_to_all(copies, axes, 0, 0, tiled=True)


def body(x_pre, x_dec, norm_gain, w_qkv, w_out, pre_keys, pre_values, pre_lens, dec_keys, dec_values, dec_lens):
    tokens, pool = x_pre.shape[0], dec_keys.shape[0]
    full = NT * WIDTH
    w_t = jnp.transpose(w_qkv, (0, 2, 1))
    index = (lax.axis_index("x") * NZ + lax.axis_index("z")) * NC + lax.axis_index("c")
    base = (index * pool).astype(jnp.int32).reshape(1)

    requests = dec_lens.shape[0]
    bounds, order = call(
        dec_bounds_kernel,
        (shape((requests, 2), F32), shape((requests, requests), BF16)),
        (base,),
        (dec_lens.reshape(1, requests),),
        flops=8 * requests * requests,
        moved=4 * requests * requests,
    )

    def turned(block, shift):
        return lax.ppermute(block, "tp", [(t, (t + shift) % NT) for t in range(NT)])

    tp = lax.axis_index("tp").astype(jnp.int32).reshape(1)
    own = lax.axis_index("x").astype(jnp.int32).reshape(1)
    x_rows = spread(x_dec, ("x", "tp"), NX * NT)
    x_t = x_pre.T
    x_blocks = [x_t] + [turned(x_t, shift) for shift in range(1, NT)]
    queries, own_queries, hidden = call(
        dec_project_kernel,
        (shape((NZ, 40, 128), BF16), shape((16, WIDTH), BF16), shape((16, full), BF16)),
        (),
        (x_rows, norm_gain.reshape(1, full), w_t[0]),
        scratch=[pltpu.VMEM((16, full), F32)],
        flops=2 * 16 * full * WIDTH,
        moved=2 * full * WIDTH,
    )
    bounds, order, queries = lax.optimization_barrier((bounds, order, queries))
    own_kv = call(
        dec_kv_kernel,
        shape((2, 16, WIDTH), BF16),
        (),
        (hidden,),
        (w_t,),
        scratch=[pltpu.VMEM((2, WIDTH, full), BF16), pltpu.SemaphoreType.DMA((2,))],
        flops=4 * 16 * full * WIDTH,
        moved=4 * full * WIDTH,
        limit=VMEM_ALL,
    )
    queries = lax.all_to_all(queries, "z", 0, 0, tiled=True)
    own_kv, queries = lax.optimization_barrier((own_kv, queries))
    queries = lax.all_gather(queries, "c", axis=0, tiled=True)
    partial = call(
        dec_attention_kernel,
        shape((requests, LANES), BF16),
        (),
        (queries, bounds, order, dec_keys.T, dec_values.T),
        scratch=[pltpu.VMEM((requests, WIDTH), BF16)],
        flops=4 * requests * pool * WIDTH,
        moved=4 * pool * WIDTH,
    )
    *x_blocks, partial = lax.optimization_barrier((*x_blocks, partial))
    term_blocks = call(
        prefill_kernel,
        (shape((WIDTH, tokens), F32),) + (shape((WIDTH, tokens), BF16),) * 3,
        (pre_lens, tp),
        (norm_gain.reshape(full // 128, 128),),
        (*x_blocks, w_t, pre_keys.T, pre_values.T, w_out),
        scratch=[
            pltpu.VMEM((full, tokens), BF16),
            pltpu.VMEM((3, WIDTH, full), BF16),
            pltpu.VMEM((WIDTH, pre_keys.shape[0]), BF16),
            pltpu.VMEM((WIDTH, pre_keys.shape[0]), BF16),
            pltpu.VMEM((WIDTH, full), BF16),
            pltpu.VMEM((NT, WIDTH, WIDTH), BF16),
            pltpu.VMEM((128, 128), F32),
        ]
        + [pltpu.VMEM((WIDTH, tokens), BF16)] * 4
        + [
            pltpu.VMEM((WIDTH, tokens), F32),
            pltpu.VMEM((3, WIDTH, tokens), BF16),
            pltpu.SemaphoreType.DMA((10,)),
            pltpu.SemaphoreType.DMA((4,)),
        ],
        out_space=pltpu.HBM,
        flops=8 * tokens * full * WIDTH + 4 * tokens * 896 * WIDTH,
        moved=8 * full * WIDTH,
        limit=VMEM_ALL,
    )
    partial = lax.all_to_all(partial.reshape(NX * NC, NZ * 4, LANES), ("x", "c"), 0, 0, tiled=True)
    term_blocks = list(term_blocks)
    term_blocks[-1], partial = lax.optimization_barrier((term_blocks[-1], partial))
    arrived = [turned(term_blocks[shift], shift) for shift in (2, 1, 3)]
    pre_out = call(
        add_terms_kernel,
        shape((WIDTH, tokens), BF16),
        (),
        (term_blocks[0], *arrived),
        flops=4 * WIDTH * tokens,
        moved=12 * WIDTH * tokens,
    )
    partial = call(
        dec_merge_kernel,
        shape((NZ, 4, LANES), F32),
        (),
        (partial,),
        flops=NX * NC * NZ * 4 * LANES,
        moved=NX * NC * NZ * 16 * LANES,
    )
    partial = lax.all_to_all(partial, "z", 0, 0, tiled=True)
    terms = call(
        dec_finish_kernel,
        shape((NT, 4, WIDTH), F32),
        (own,),
        (partial, own_queries, own_kv, w_out),
        flops=2 * 8 * full * WIDTH,
        moved=2 * full * WIDTH,
    )
    terms = lax.all_to_all(terms, "tp", 0, 0, tiled=True)
    dec_out = jnp.sum(terms, axis=0).astype(BF16)
    return pre_out.T, dec_out


def solution(mesh):
    req = ("x", "z", "c")
    grid = Mesh(mesh.devices.reshape(NX, NZ, NC, NT), req + ("tp",))
    return jax.shard_map(
        body,
        mesh=grid,
        in_specs=(
            P(req, "tp"),
            P(req, "tp"),
            P(),
            P(None, None, "tp"),
            P("tp", None),
            P(req, "tp"),
            P(req, "tp"),
            P(req),
            P(req, "tp"),
            P(req, "tp"),
            P(),
        ),
        out_specs=(P(req, "tp"), P(req, "tp")),
        check_vma=False,
    )
```
